32 devices in a mesh: rep: 16 (over z, x, core), dom: 2 (over y).
Axes of the slice: x: 2, y: 2, z: 4, core: 2. Of those that a mesh axis runs over, the one named last changes fastest.
Arguments:
- field: float32 [16, 256, 2048], P('rep', 'dom'), may hold values from -2.5 to 2.5
- momentum: float32 [16, 256, 2048], P('rep', 'dom'), may hold values from -4 to 4
- labels: int32 [16], P('rep'), may hold values from 0 to 15, each once
- betas: float32 [16], replicated, may hold values from 0.4 to 1.6
- accept: int32 [16], P('rep'), may hold values 0 or 1
- swap_pairs: int32 [16], replicated, may hold values from 0 to 15, as said below
Outputs:
- field_out: float32 [16, 256, 2048], P('rep', 'dom')
- field_sorted: float32 [16, 256, 2048], P('rep', 'dom')
- labels_out: int32 [16], P('rep')
- energy_change: float32 [16], P('rep')
- ladder_action: float32 [16], P('rep')
The draws below stay inside these ranges and needn't reach their ends.
Inputs may be any that keep to these rules, and one draw needn't show every extreme that they name: Each temperature index t is paired with itself, with t - 1 or with t + 1, and the pairing is symmetric: swap_pairs[swap_pairs[t]] = t. labels is a permutation of the temperature indices.
All inputs are finite; a program needn't handle non-finite values. No bound on the sum of `accept` on one device may be relied on, other than what follows from the above.
Results may differ from the reference program's by a relative error of at most 0.0003.
Values sent between devices are 32-bit elements; how exact they have to be, the bound alone decides.
No kernel may reach another device: no remote copies, remote signals or barrier semaphores. Data moves between devices by JAX's collectives and lax.ppermute only.
A program may use at most 64 MiB of HBM per device.

```python
import math
import jax
import jax.numpy as jnp
from jax import lax

COLS = 2048
STEPS = 8
REPLICAS = 16
ROWS = 256


def draw_swap_pairs(key, part):
    key_parity = jax.random.fold_in(key, 11)
    key_accept = jax.random.fold_in(key, 12)
    parity = jax.random.randint(key_parity, (), 0, 2)
    positions = jnp.arange(REPLICAS, dtype=jnp.int32)
    offset = (positions - parity) % 2
    candidate = jnp.where(offset == 0, positions + 1, positions - 1)
    inside = (candidate >= 0) & (candidate < REPLICAS)
    flips = jax.random.randint(key_accept, (REPLICAS,), 0, 2)
    lower_end = jnp.clip(jnp.minimum(positions, candidate), 0, REPLICAS - 1)
    agreed = jnp.take(flips, lower_end) == 1
    return jnp.where(inside & agreed, candidate, positions).astype(jnp.int32)


def place_ends(values, stream_key, smallest, top_value):
    shape = values.shape
    spot = [jax.random.randint(jax.random.fold_in(stream_key, axis), (), 0, shape[axis]) for axis in range(len(shape))]
    values = values.at[tuple(spot)].set(smallest)
    longest = shape.index(max(shape))
    spot[longest] = (spot[longest] + 1) % shape[longest]
    return values.at[tuple(spot)].set(top_value)


def levels(rng, extent, cuts, smallest, top_value):
    def one(position, blocks):
        draws = jax.random.uniform(jax.random.fold_in(jax.random.fold_in(rng, 6), position), (blocks,), jnp.float32, smallest / len(cuts), top_value / len(cuts))
        return jnp.repeat(jnp.exp(draws), extent[position] // blocks).reshape((-1,) + (1,) * (len(extent) - position - 1))

    level = one(*cuts[0])
    for cut in cuts[1:]:
        level = level * one(*cut)
    return level


def noise(key, extent, deviation, most, pieces=(), held_as=jnp.bfloat16):
    entries = jax.random.normal(key, extent, jnp.float32) * deviation
    if len(pieces) > 0:
        entries = levels(key, extent, pieces, -0.22, 0.18) * entries
    return jnp.clip(entries, min=-most, max=most).astype(held_as)


def setup_inputs(seed: int = 0) -> dict:
    keys = jax.random.split(jax.random.key(seed), 7)
    return {
        "field": noise(keys[0], (REPLICAS, ROWS, COLS), 0.7, 2.5, ((0, 16), (1, 2)), jnp.float32),
        "momentum": noise(keys[1], (REPLICAS, ROWS, COLS), 1.0, 4.0, ((0, 16), (1, 2)), jnp.float32),
        "labels": jax.random.permutation(keys[2], REPLICAS).astype(jnp.int32),
        "betas": jnp.clip(jnp.exp(jax.random.uniform(keys[3], (REPLICAS,), jnp.float32, math.log(0.4), math.log(1.6))), 0.4, 1.6),
        "accept": place_ends((jax.random.randint(keys[4], (REPLICAS,), 0, 4) < 3).astype(jnp.int32), jax.random.fold_in(keys[4], 1), 0, 1),
        "swap_pairs": draw_swap_pairs(jax.random.fold_in(keys[6], 71), 0),
    }


hopping = 0.18
quartic = 0.3
step_size = 0.05


def force_field(values, coldness):
    beside_all = (jnp.roll(values, 1, 0) + jnp.roll(values, -1, 0)) + (jnp.roll(values, 1, 1) + jnp.roll(values, -1, 1))
    return coldness * (-2.0 * hopping * beside_all + 2.0 * values + 4.0 * quartic * values * (values * values - 1.0))


def site_action(values):
    neighbours = jnp.roll(values, -1, 0) + jnp.roll(values, -1, 1)
    squared = values * values
    return -2.0 * hopping * values * neighbours + squared + quartic * (squared - 1.0) * (squared - 1.0)


def trajectory(inputs):
    start_field, start_moment, coldness = inputs
    moment = start_moment - 0.5 * step_size * force_field(start_field, coldness)
    current = start_field
    for leap_step in range(STEPS):
        current = current + step_size * moment
        factor = 0.5 * step_size if leap_step == STEPS - 1 else step_size
        moment = moment - factor * force_field(current, coldness)
    old_action = site_action(start_field)
    new_action = site_action(current)
    change = jnp.sum((0.5 * moment * moment + coldness * new_action) - (0.5 * start_moment * start_moment + coldness * old_action))
    return current, change, jnp.sum(old_action), jnp.sum(new_action)


def reference(field, momentum, labels, betas, accept, swap_pairs):
    coldness = betas[labels]
    labels_out = swap_pairs[labels]
    proposal, change, old_total, new_total = lax.map(trajectory, (field, momentum, coldness))
    accepted = accept == 1
    field_out = jnp.where(accepted[:, None, None], proposal, field)
    action = jnp.where(accepted, new_total, old_total)
    holder = jnp.zeros((REPLICAS,), jnp.int32).at[labels_out].set(jnp.arange(REPLICAS, dtype=jnp.int32))
    field_sorted = field_out[holder]
    ladder_action = action[holder] / (ROWS * COLS)
    return field_out, field_sorted, labels_out, change, ladder_action
```

```python
import functools

import jax
import jax.numpy as jnp
from jax import lax
from jax.experimental import pallas as pl
from jax.experimental.pallas import tpu as pltpu
from jax.sharding import PartitionSpec as P

STEPS = 8
hopping = 0.18
quartic = 0.3
step_size = 0.05

SUB = 8
LANES = 128
LINEAR = (1.0 - 2.0 * quartic) / hopping
CUBIC = 2.0 * quartic / hopping


def tile(ref, row, col):
    return ref[pl.ds(row, SUB), pl.ds(col * LANES, LANES)]


def lane_index():
    return lax.broadcasted_iota(jnp.int32, (SUB, LANES), 1)


def beside(values, lane):
    count = len(values)
    ahead = [pltpu.roll(v, 1, 1) for v in values]
    back = [pltpu.roll(v, LANES - 1, 1) for v in values]
    left = [jnp.where(lane == 0, ahead[i - 1], ahead[i]) for i in range(count)]
    right = [jnp.where(lane == LANES - 1, back[(i + 1) % count], back[i]) for i in range(count)]
    return [a + b for a, b in zip(left, right)], right


def pull(total, value):
    return total - value * (LINEAR + CUBIC * (value * value))


def pack_kernel(scale_ref, head_ref, tail_ref, head_m_ref, tail_m_ref, out_ref):
    inverse = scale_ref[1]
    lane = lane_index()
    row = lax.broadcasted_iota(jnp.int32, (SUB, LANES), 0)
    tiles = head_ref.shape[1] // LANES
    for side, ref, m_ref in ((0, head_ref, head_m_ref), (1, tail_ref, tail_m_ref)):
        base = 0 if side == 0 else SUB
        inner = SUB - base
        values = [tile(ref, base, i) for i in range(tiles)]
        others = [tile(ref, inner, i) for i in range(tiles)]
        sums, _ = beside(values, lane)
        for i in range(tiles):
            up = pltpu.roll(values[i], 1, 0)
            down = pltpu.roll(values[i], SUB - 1, 0)
            if side == 0:
                up = jnp.where(row == 0, 0.0, up)
                down = jnp.where(row == SUB - 1, pltpu.roll(others[i], SUB - 1, 0), down)
            else:
                up = jnp.where(row == 0, pltpu.roll(others[i], 1, 0), up)
                down = jnp.where(row == SUB - 1, 0.0, down)
            kick = m_ref[:, pl.ds(i * LANES, LANES)] * inverse + 0.5 * pull(
                (up + down) + sums[i], values[i]
            )
            out_ref[side, 0, :, pl.ds(i * LANES, LANES)] = values[i]
            out_ref[side, 1, :, pl.ds(i * LANES, LANES)] = kick


def path_kernel(
    per_member,
    scale_ref,
    field_ref,
    momentum_ref,
    above_ref,
    below_ref,
    out_ref,
    send_ref,
    first,
    second,
    push,
    energy,
):
    cold = scale_ref[0]
    inverse = scale_ref[1]
    unit = scale_ref[2]
    drift = scale_ref[3]
    label = scale_ref[4]
    accepted = scale_ref[5] > 0.5
    rows, width = field_ref.shape
    tiles = width // LANES
    blocks = rows // SUB
    lane = lane_index()
    sub = lax.broadcasted_iota(jnp.int32, (SUB, LANES), 0)
    own = 2 * SUB
    end = own + rows

    def load(i, carry):
        row = pl.multiple_of(i * SUB, SUB)
        for t in range(tiles):
            first[t, pl.ds(own + row, SUB), :] = tile(field_ref, row, t)
        return carry

    lax.fori_loop(0, blocks, load, 0)
    zero = jnp.zeros((SUB, LANES), jnp.float32)
    for t in range(tiles):
        cols = pl.ds(t * LANES, LANES)
        for ref, row in ((above_ref, SUB), (below_ref, end)):
            first[t, row : row + SUB, :] = ref[0, :, cols]
        for row in (0, end + SUB):
            first[t, row : row + SUB, :] = zero
            second[t, row : row + SUB, :] = zero
        top = first[t, own : own + SUB, :]
        low = first[t, end - SUB : end, :]
        for ref, row, mine in (
            (above_ref, SUB, jnp.where(sub == SUB - 1, pltpu.roll(top, SUB - 1, 0), 0.0)),
            (below_ref, end, jnp.where(sub == 0, pltpu.roll(low, 1, 0), 0.0)),
        ):
            kick = ref[1, :, cols] + 0.5 * mine
            push[t, row : row + SUB, :] = kick
            second[t, row : row + SUB, :] = ref[0, :, cols] + drift * kick

    def site(value, down, right):
        squared = value * value
        return (-2.0 * hopping) * value * (down + right) + (
            squared + quartic * (squared - 1.0) * (squared - 1.0)
        )

    def begin(i, total):
        row = pl.multiple_of(own + i * SUB, SUB)
        source = pl.multiple_of(i * SUB, SUB)
        values = [first[t, pl.ds(row, SUB), :] for t in range(tiles)]
        sums, right = beside(values, lane)
        for t in range(tiles):
            up = first[t, pl.ds(row - 1, SUB), :]
            down = first[t, pl.ds(row + 1, SUB), :]
            moment = tile(momentum_ref, source, t)
            action = site(values[t], down, right[t])
            energy[t, pl.ds(source, SUB), :] = 0.5 * moment * moment + cold * action
            total = total + action
            kick = moment * inverse + 0.5 * pull((up + down) + sums[t], values[t])
            push[t, pl.ds(row, SUB), :] = kick
            second[t, pl.ds(row, SUB), :] = values[t] + drift * kick
        return total

    old_action = lax.fori_loop(0, blocks, begin, zero)

    def sweep(before, after):
        def one(i, carry):
            row = pl.multiple_of(SUB + i * SUB, SUB)
            values = [before[t, pl.ds(row, SUB), :] for t in range(tiles)]
            sums, _ = beside(values, lane)
            for t in range(tiles):
                up = before[t, pl.ds(row - 1, SUB), :]
                down = before[t, pl.ds(row + 1, SUB), :]
                kick = push[t, pl.ds(row, SUB), :] + pull((up + down) + sums[t], values[t])
                push[t, pl.ds(row, SUB), :] = kick
                after[t, pl.ds(row, SUB), :] = values[t] + drift * kick
            return carry

        lax.fori_loop(0, blocks + 2, one, 0)

    for leap in range(STEPS - 1):
        before, after = (second, first) if leap % 2 == 0 else (first, second)
        sweep(before, after)
    last = second if (STEPS - 1) % 2 == 0 else first

    def finish(i, carry):
        change, total = carry
        row = pl.multiple_of(own + i * SUB, SUB)
        source = pl.multiple_of(i * SUB, SUB)
        values = [last[t, pl.ds(row, SUB), :] for t in range(tiles)]
        sums, right = beside(values, lane)
        for t in range(tiles):
            up = last[t, pl.ds(row - 1, SUB), :]
            down = last[t, pl.ds(row + 1, SUB), :]
            kick = push[t, pl.ds(row, SUB), :] + 0.5 * pull((up + down) + sums[t], values[t])
            moment = unit * kick
            action = site(values[t], down, right[t])
            total = total + action
            change = change + (
                (0.5 * moment * moment + cold * action) - energy[t, pl.ds(source, SUB), :]
            )
            chosen = jnp.where(accepted, values[t], tile(field_ref, source, t))
            out_ref[pl.ds(source, SUB), pl.ds(t * LANES, LANES)] = chosen
            member = i * (tiles // per_member) + t // per_member
            send_ref[member, :, pl.ds((t % per_member) * LANES, LANES)] = chosen
        return change, total

    change, new_action = lax.fori_loop(0, blocks, finish, (zero, zero))
    action = jnp.sum(jnp.where(accepted, new_action, old_action))
    change = jnp.sum(change)
    note = jnp.where(lane == 0, label, jnp.where(lane == 1, action, jnp.where(lane == 2, change, 0.0)))

    def annotate(m, carry):
        send_ref[m, :, pl.ds(per_member * LANES, LANES)] = note
        return carry

    lax.fori_loop(0, send_ref.shape[0], annotate, 0)


def place_kernel(got_ref, out_ref, note_ref, labels_ref, sem, note_sem):
    members, _, width = out_ref.shape
    for r in range(members):
        note_ref[r : r + 1, :] = got_ref[r, 0:1, width:]
    fetch = pltpu.make_async_copy(note_ref, labels_ref, note_sem)
    fetch.start()
    fetch.wait()
    copies = []
    for r in range(members):
        slot = labels_ref[r, 0].astype(jnp.int32)
        copy = pltpu.make_async_copy(got_ref.at[r, :, pl.ds(0, width)], out_ref.at[slot], sem.at[r])
        copy.start()
        copies.append(copy)
    for copy in copies:
        copy.wait()


def body(field, momentum, labels, betas, accept, swap_pairs):
    rows = field.shape[1]
    width = field.shape[2]
    members = lax.axis_size("rep")
    strips = lax.axis_size("dom")
    tiles = width // LANES
    per_member = (rows // SUB) * tiles // members
    ladder_index = jnp.arange(betas.shape[0], dtype=jnp.int32)
    chosen = ladder_index == labels[0]
    cold = jnp.sum(jnp.where(chosen, betas, 0.0))
    new_label = jnp.sum(jnp.where(chosen, swap_pairs, 0))
    unit = 2.0 * hopping * step_size * cold
    scale = jnp.stack(
        (
            cold,
            1.0 / unit,
            unit,
            step_size * unit,
            new_label.astype(jnp.float32),
            accept[0].astype(jnp.float32),
        )
    )
    start = field[0]
    moment = momentum[0]
    smem = pl.BlockSpec(memory_space=pltpu.SMEM)
    vmem = pl.BlockSpec(memory_space=pltpu.VMEM)
    last16 = rows // (2 * SUB) - 1
    last8 = rows // SUB - 1
    edges = pl.pallas_call(
        pack_kernel,
        grid=(1,),
        out_shape=jax.ShapeDtypeStruct((2, 2, SUB, width), jnp.float32),
        in_specs=[
            smem,
            pl.BlockSpec((2 * SUB, width), lambda i: (0, 0)),
            pl.BlockSpec((2 * SUB, width), lambda i: (last16, 0)),
            pl.BlockSpec((SUB, width), lambda i: (0, 0)),
            pl.BlockSpec((SUB, width), lambda i: (last8, 0)),
        ],
        out_specs=pl.BlockSpec((2, 2, SUB, width), lambda i: (0, 0, 0, 0)),
    )(scale, start, start, moment, moment)
    forward = [(i, (i + 1) % strips) for i in range(strips)]
    backward = [((i + 1) % strips, i) for i in range(strips)]
    if strips == 2:
        edges = lax.ppermute(edges, "dom", forward)
        above, below = edges[1], edges[0]
    else:
        above = lax.ppermute(edges[1], "dom", forward)
        below = lax.ppermute(edges[0], "dom", backward)
    state = pltpu.VMEM((tiles, rows + 4 * SUB, LANES), jnp.float32)
    field_out, outgoing = pl.pallas_call(
        functools.partial(path_kernel, per_member),
        out_shape=(
            jax.ShapeDtypeStruct((rows, width), jnp.float32),
            jax.ShapeDtypeStruct((members, SUB, (per_member + 1) * LANES), jnp.float32),
        ),
        in_specs=[smem, vmem, vmem, vmem, vmem],
        out_specs=(vmem, vmem),
        scratch_shapes=[state, state, state, pltpu.VMEM((tiles, rows, LANES), jnp.float32)],
    )(scale, start, moment, above, below)
    received = lax.all_to_all(outgoing, "rep", split_axis=0, concat_axis=0, tiled=True)
    piece = per_member * LANES
    ordered, notes = pl.pallas_call(
        place_kernel,
        out_shape=(
            jax.ShapeDtypeStruct((members, SUB, piece), jnp.float32),
            jax.ShapeDtypeStruct((members, LANES), jnp.float32),
        ),
        in_specs=[vmem],
        out_specs=(pl.BlockSpec(memory_space=pl.ANY), vmem),
        scratch_shapes=[
            pltpu.SMEM((members, LANES), jnp.float32),
            pltpu.SemaphoreType.DMA((members,)),
            pltpu.SemaphoreType.DMA,
        ],
    )(received)
    returned = lax.all_to_all(ordered, "rep", split_axis=0, concat_axis=0, tiled=True)
    whole = width // piece
    returned = returned.reshape(rows // SUB, whole, SUB, piece).transpose(0, 2, 1, 3)
    returned = returned.reshape(1, rows, width)
    sums = notes
    passing = notes
    for _ in range(strips - 1):
        passing = lax.ppermute(passing, "dom", forward)
        sums = sums + passing
    me = lax.axis_index("rep")
    held_labels = notes[:, 0].astype(jnp.int32)
    sites = strips * rows * width
    ladder = jnp.sum(jnp.where(held_labels == me, sums[:, 1], 0.0)) / sites
    change = jnp.sum(jnp.where(ladder_index == me, sums[:, 2], 0.0))
    return (field_out[None], returned, new_label[None], change[None], ladder[None])


def solution(mesh):
    placed = (P("rep", "dom", None), P("rep", "dom", None), P("rep"), P(), P("rep"), P())
    return jax.shard_map(
        body,
        mesh=mesh,
        in_specs=placed,
        out_specs=(P("rep", "dom", None), P("rep", "dom", None), P("rep"), P("rep"), P("rep")),
        check_vma=False,
    )
```

```python
import functools

import jax
import jax.numpy as jnp
from jax import lax
from jax.experimental import pallas as pl
from jax.experimental.pallas import tpu as pltpu
from jax.sharding import PartitionSpec as P

STEPS = 8
hopping = 0.18
quartic = 0.3
step_size = 0.05

SUB = 8
LANES = 128
EDGE = 3
GROUP = 7


def lane_index():
    return lax.broadcasted_iota(jnp.int32, (SUB, LANES), 1)


def row_index():
    return lax.broadcasted_iota(jnp.int32, (SUB, LANES), 0)


class Scales:
    def __init__(self, cold):
        self.cold = cold
        squared = jnp.full((SUB, LANES), (4.0 * quartic * step_size * step_size) * cold)
        self.root = jnp.sqrt(squared)
        self.back = 1.0 / self.root
        self.back2 = self.back * self.back
        self.pull = (2.0 * hopping * step_size * step_size) * cold
        self.slope = -((2.0 - 4.0 * quartic) * step_size * step_size) * cold
        self.speed = step_size * self.root
        self.unspeed = 1.0 / self.speed

    def half(self, near, value):
        return 0.5 * (self.pull * near + value * (self.slope - value * value))

    def step(self, near, value, before):
        return value + ((value - before) + (self.pull * near + value * (self.slope - value * value)))

    def site(self, value, ahead):
        squared = value * value * self.back2
        return (-2.0 * hopping) * (self.back2 * (value * ahead)) + (
            squared + quartic * (squared - 1.0) * (squared - 1.0)
        )


def chosen_scalars(labels_ref, betas_ref):
    return betas_ref[labels_ref[0]]


def beside(values, lane):
    count = len(values)
    ahead = [pltpu.roll(v, 1, 1) for v in values]
    back = [pltpu.roll(v, LANES - 1, 1) for v in values]
    left = [jnp.where(lane == 0, ahead[i - 1], ahead[i]) for i in range(count)]
    right = [jnp.where(lane == LANES - 1, back[(i + 1) % count], back[i]) for i in range(count)]
    return [a + b for a, b in zip(left, right)], right


def around(ref, row, tiles, lane):
    values = [ref[t, pl.ds(row, SUB), :] for t in range(tiles)]
    sums, right = beside(values, lane)
    below = [ref[t, pl.ds(row + 1, SUB), :] for t in range(tiles)]
    near = [(ref[t, pl.ds(row - 1, SUB), :] + below[t]) + sums[t] for t in range(tiles)]
    return values, near, below, right


def advance(before, after, row, tiles, lane, scales, keep=None):
    values, near, _, _ = around(before, row, tiles, lane)
    for t in range(tiles):
        old = after[t, pl.ds(row, SUB), :]
        new = scales.step(near[t], values[t], old)
        if keep is not None:
            new = jnp.where(keep, old, new)
        after[t, pl.ds(row, SUB), :] = new


def pack_kernel(labels_ref, betas_ref, head_ref, tail_ref, head_m_ref, tail_m_ref, out_ref):
    scales = Scales(chosen_scalars(labels_ref, betas_ref))
    lane = lane_index()
    row = row_index()
    tiles = head_ref.shape[1] // LANES
    for side, ref, m_ref in ((0, head_ref, head_m_ref), (1, tail_ref, tail_m_ref)):
        base = 0 if side == 0 else SUB
        inner = SUB - base
        values = [scales.root * ref[base : base + SUB, pl.ds(i * LANES, LANES)] for i in range(tiles)]
        sums, _ = beside(values, lane)
        for i in range(tiles):
            cols = pl.ds(i * LANES, LANES)
            other = scales.root * ref[inner : inner + SUB, cols]
            up = pltpu.roll(values[i], 1, 0)
            down = pltpu.roll(values[i], SUB - 1, 0)
            if side == 0:
                up = jnp.where(row == 0, 0.0, up)
                down = jnp.where(row == SUB - 1, pltpu.roll(other, SUB - 1, 0), down)
            else:
                up = jnp.where(row == 0, pltpu.roll(other, 1, 0), up)
                down = jnp.where(row == SUB - 1, 0.0, down)
            push = scales.speed * m_ref[:, cols] + scales.half((up + down) + sums[i], values[i])
            out_ref[side, 0, :, cols] = values[i]
            out_ref[side, 1, :, cols] = values[i] + push


def slots(row_block, tiles, per_member):
    shares = tiles // per_member
    return [(row_block * shares + s, s * per_member * LANES) for s in range(shares)]


def inner_kernel(
    per_member,
    labels_ref,
    betas_ref,
    accept_ref,
    field_hbm,
    momentum_hbm,
    out_hbm,
    send_hbm,
    state_hbm,
    energy_hbm,
    sums_ref,
    field_ref,
    momentum_ref,
    chosen_ref,
    first,
    second,
    energy,
    in_sem,
    out_sem,
    send_sem,
    state_sem,
):
    rows, width = field_ref.shape
    tiles = width // LANES
    blocks = rows // SUB
    chunk = rows // 8
    loads = []
    for a, (source, target) in enumerate(((field_hbm, field_ref), (momentum_hbm, momentum_ref))):
        for k in range(8):
            part = pl.ds(k * chunk, chunk)
            copy = pltpu.make_async_copy(source.at[part, :], target.at[part, :], in_sem.at[a, k])
            copy.start()
            loads.append(copy)
    scales = Scales(chosen_scalars(labels_ref, betas_ref))
    accepted = accept_ref[0] == 1
    lane = lane_index()
    sub = row_index()
    zero = jnp.zeros((SUB, LANES), jnp.float32)
    for ref in (first, second):
        for t in range(tiles):
            ref[t, 0:SUB, :] = zero
            ref[t, SUB + rows : 2 * SUB + rows, :] = zero
    for k in range(8):
        loads[k].wait()
        for b in range(chunk // SUB):
            row = k * chunk + b * SUB
            for t in range(tiles):
                first[t, SUB + row : 2 * SUB + row, :] = (
                    scales.root * field_ref[row : row + SUB, pl.ds(t * LANES, LANES)]
                )

    def begin(block, total):
        source = pl.multiple_of(block * SUB, SUB)
        row = pl.multiple_of(SUB + block * SUB, SUB)
        values, near, below, right = around(first, row, tiles, lane)
        for t in range(tiles):
            push = scales.speed * momentum_ref[pl.ds(source, SUB), pl.ds(t * LANES, LANES)]
            moment = scales.unspeed * push
            action = scales.site(values[t], below[t] + right[t])
            energy[t, pl.ds(source, SUB), :] = 0.5 * moment * moment + scales.cold * action
            total = total + action
            second[t, pl.ds(row, SUB), :] = values[t] + (push + scales.half(near[t], values[t]))
        return total

    for k in range(8):
        loads[8 + k].wait()

    per_turn = 2

    def begin_turn(i, total):
        for b in range(per_turn):
            total = begin(i * per_turn + b, total)
        return total

    old_action = lax.fori_loop(0, blocks // per_turn, begin_turn, zero)

    group = GROUP if (blocks - 2) % GROUP == 0 else 1
    for time in range(1, STEPS):
        before, after = (second, first) if time % 2 == 1 else (first, second)
        advance(before, after, SUB, tiles, lane, scales, keep=sub <= time)
        advance(before, after, rows, tiles, lane, scales, keep=sub >= SUB - 1 - time)

        def turn(i, carry, before=before, after=after):
            for b in range(group):
                row = pl.multiple_of(2 * SUB + (i * group + b) * SUB, SUB)
                advance(before, after, row, tiles, lane, scales)
            return carry

        lax.fori_loop(0, (blocks - 2) // group, turn, 0)
    last, previous = (first, second) if STEPS % 2 == 0 else (second, first)
    stores = []
    for n, buffer in enumerate((last, previous)):
        for side, row in ((0, SUB), (1, SUB + rows - EDGE * SUB)):
            copy = pltpu.make_async_copy(
                buffer.at[:, pl.ds(row, EDGE * SUB), :], state_hbm.at[side, n], state_sem.at[side, n]
            )
            copy.start()
            stores.append(copy)
    for side, row in ((0, 0), (1, rows - 2 * SUB)):
        copy = pltpu.make_async_copy(
            energy.at[:, pl.ds(row, 2 * SUB), :], energy_hbm.at[side], state_sem.at[side, 2]
        )
        copy.start()
        stores.append(copy)

    def emit(block):
        row = block * SUB
        copies = [
            pltpu.make_async_copy(
                chosen_ref.at[pl.ds(row, SUB), :], out_hbm.at[pl.ds(row, SUB), :], out_sem.at[block]
            )
        ]
        for member, column in slots(block, tiles, per_member):
            width_here = per_member * LANES
            copies.append(
                pltpu.make_async_copy(
                    chosen_ref.at[pl.ds(row, SUB), pl.ds(column, width_here)],
                    send_hbm.at[member, :, pl.ds(0, width_here)],
                    send_sem.at[member],
                )
            )
        return copies

    def choose(block, value, t):
        row = pl.multiple_of(block * SUB, SUB)
        cols = pl.ds(t * LANES, LANES)
        kept = field_ref[pl.ds(row, SUB), cols]
        chosen_ref[pl.ds(row, SUB), cols] = jnp.where(accepted, scales.back * value, kept)

    for block in (1, blocks - 2):
        for t in range(tiles):
            choose(block, last[t, SUB + block * SUB : 2 * SUB + block * SUB, :], t)
        for copy in emit(block):
            copy.start()
            stores.append(copy)

    def finish(block, carry):
        change, total = carry
        row = pl.multiple_of(SUB + block * SUB, SUB)
        source = pl.multiple_of(block * SUB, SUB)
        values, near, below, right = around(last, row, tiles, lane)
        for t in range(tiles):
            gone = values[t] - previous[t, pl.ds(row, SUB), :]
            moment = scales.unspeed * (gone + scales.half(near[t], values[t]))
            action = scales.site(values[t], below[t] + right[t])
            total = total + action
            change = change + (
                (0.5 * moment * moment + scales.cold * action) - energy[t, pl.ds(source, SUB), :]
            )
            choose(block, values[t], t)
        return change, total

    sums = (zero, zero)
    if (blocks - 4) % per_turn == 0:
        for i in range((blocks - 4) // per_turn):
            sums = lax.fori_loop(
                0,
                1,
                lambda _, carry, i=i: functools.reduce(
                    lambda c, b: finish(2 + i * per_turn + b, c), range(per_turn), carry
                ),
                sums,
            )
            for b in range(per_turn):
                for copy in emit(2 + i * per_turn + b):
                    copy.start()
                    stores.append(copy)
    else:
        for block in range(2, blocks - 2):
            sums = finish(block, sums)
            for copy in emit(block):
                copy.start()
                stores.append(copy)
    sums_ref[0] = sums[0]
    sums_ref[1] = sums[1]
    sums_ref[2] = old_action
    for copy in stores:
        copy.wait()


def outer_kernel(
    per_member,
    halos,
    labels_ref,
    betas_ref,
    accept_ref,
    swap_ref,
    *refs,
):
    halo_refs = refs[:halos]
    (
        state_ref,
        energy_ref,
        sums_ref,
        head_ref,
        tail_ref,
        _,
        _,
        out_hbm,
        send_hbm,
        first,
        second,
        chosen_ref,
        note_ref,
        out_sem,
        send_sem,
        note_sem,
    ) = refs[halos:]
    scales = Scales(chosen_scalars(labels_ref, betas_ref))
    label = swap_ref[labels_ref[0]].astype(jnp.float32)
    accepted = accept_ref[0] == 1
    lane = lane_index()
    sub = row_index()
    tiles = first.shape[1]
    members = send_hbm.shape[0]
    blocks = out_hbm.shape[0] // SUB
    zero = jnp.zeros((SUB, LANES), jnp.float32)
    last, previous = (first, second) if STEPS % 2 == 0 else (second, first)
    old_extra = zero
    energy_extra = []
    for side in range(2):
        ref = halo_refs[side % halos]
        own = 2 * SUB if side == 0 else 0
        edge = SUB if side == 0 else EDGE * SUB
        pad = 0 if side == 0 else (EDGE + 1) * SUB
        mine = own if side == 0 else (EDGE - 1) * SUB
        for t in range(tiles):
            cols = pl.ds(t * LANES, LANES)
            for n, buffer in enumerate((last, previous)):
                buffer[side, t, own : own + EDGE * SUB, :] = state_ref[side, n, t]
                buffer[side, t, pad : pad + SUB, :] = zero
            start_halo = ref[1 - side, 0, :, cols]
            start_mine = first[side, t, mine : mine + SUB, :]
            if side == 0:
                own_part = jnp.where(sub == SUB - 1, pltpu.roll(start_mine, SUB - 1, 0), 0.0)
                halo_part = jnp.where(sub == 0, pltpu.roll(start_halo, 1, 0), 0.0)
            else:
                own_part = jnp.where(sub == 0, pltpu.roll(start_mine, 1, 0), 0.0)
                halo_part = jnp.where(sub == SUB - 1, pltpu.roll(start_halo, SUB - 1, 0), 0.0)
                missing = (-2.0 * hopping) * (scales.back2 * (start_mine * halo_part))
                old_extra = old_extra + missing
                energy_extra.append(scales.cold * missing)
            first[side, t, edge : edge + SUB, :] = start_halo
            second[side, t, edge : edge + SUB, :] = ref[1 - side, 1, :, cols] + (
                0.5 * scales.pull
            ) * own_part
            second[side, t, mine : mine + SUB, :] = (
                second[side, t, mine : mine + SUB, :] + (0.5 * scales.pull) * halo_part
            )
    for time in range(1, STEPS):
        before, after = (second, first) if time % 2 == 1 else (first, second)
        for side in range(2):
            mine = 2 * SUB if side == 0 else (EDGE - 1) * SUB
            edge = SUB if side == 0 else EDGE * SUB
            keep = sub > time if side == 0 else sub < SUB - 1 - time
            advance(before.at[side], after.at[side], edge, tiles, lane, scales)
            advance(before.at[side], after.at[side], mine, tiles, lane, scales, keep=keep)
    change = sums_ref[0]
    total = sums_ref[1]
    copies = []
    for side in range(2):
        own = 2 * SUB if side == 0 else 0
        for b in range(2):
            place = b if side == 0 else EDGE - 2 + b
            row = own + place * SUB
            values, near, below, right = around(last.at[side], row, tiles, lane)
            outermost = (side == 0 and b == 0) or (side == 1 and b == 1)
            for t in range(tiles):
                gone = values[t] - previous[side, t, pl.ds(row, SUB), :]
                moment = scales.unspeed * (gone + scales.half(near[t], values[t]))
                action = scales.site(values[t], below[t] + right[t])
                total = total + action
                old = energy_ref[side, t, b * SUB : (b + 1) * SUB, :]
                if side == 1 and outermost:
                    old = old + energy_extra[t]
                change = change + ((0.5 * moment * moment + scales.cold * action) - old)
                if outermost:
                    cols = pl.ds(t * LANES, LANES)
                    kept = head_ref[:, cols] if side == 0 else tail_ref[:, cols]
                    chosen_ref[side, :, cols] = jnp.where(accepted, scales.back * values[t], kept)
        block = 0 if side == 0 else blocks - 1
        copies.append(
            pltpu.make_async_copy(
                chosen_ref.at[side], out_hbm.at[pl.ds(block * SUB, SUB), :], out_sem.at[side]
            )
        )
        for n, (member, column) in enumerate(slots(block, tiles, per_member)):
            size = per_member * LANES
            copies.append(
                pltpu.make_async_copy(
                    chosen_ref.at[side, :, pl.ds(column, size)],
                    send_hbm.at[member, :, pl.ds(0, size)],
                    send_sem.at[side, n],
                )
            )
    for copy in copies:
        copy.start()
    old_action = sums_ref[2] + old_extra
    action = jnp.sum(jnp.where(accepted, total, old_action))
    change = jnp.sum(change)
    note_ref[...] = jnp.where(
        lane == 0, label, jnp.where(lane == 1, action, jnp.where(lane == 2, change, 0.0))
    )
    for member in range(members):
        copy = pltpu.make_async_copy(
            note_ref,
            send_hbm.at[member, :, pl.ds(per_member * LANES, LANES)],
            note_sem.at[member],
        )
        copy.start()
        copies.append(copy)
    for copy in copies:
        copy.wait()


def place_kernel(got_hbm, out_hbm, notes_hbm, pieces_ref, labels_ref, load_sem, sem, note_sem):
    members, _, width = out_hbm.shape
    notes = got_hbm.at[:, 0, pl.ds(width, LANES)]
    fetch = pltpu.make_async_copy(notes, labels_ref, note_sem.at[0])
    fetch.start()
    keep = pltpu.make_async_copy(notes, notes_hbm, note_sem.at[1])
    keep.start()
    loads = []
    for r in range(members):
        load = pltpu.make_async_copy(got_hbm.at[r, :, pl.ds(0, width)], pieces_ref.at[r], load_sem.at[r])
        load.start()
        loads.append(load)
    fetch.wait()
    copies = []
    for r in range(members):
        loads[r].wait()
        slot = labels_ref[r, 0].astype(jnp.int32)
        copy = pltpu.make_async_copy(pieces_ref.at[r], out_hbm.at[slot], sem.at[r])
        copy.start()
        copies.append(copy)
    keep.wait()
    for copy in copies:
        copy.wait()


def body(field, momentum, labels, betas, accept, swap_pairs):
    rows = field.shape[1]
    width = field.shape[2]
    members = lax.axis_size("rep")
    strips = lax.axis_size("dom")
    tiles = width // LANES
    per_member = (rows // SUB) * tiles // members
    shares = tiles // per_member
    piece = per_member * LANES
    f32 = jnp.float32
    start = field[0]
    moment = momentum[0]
    smem = pl.BlockSpec(memory_space=pltpu.SMEM)
    vmem = pl.BlockSpec(memory_space=pltpu.VMEM)
    anywhere = pl.BlockSpec(memory_space=pl.ANY)
    dma = pltpu.SemaphoreType.DMA
    last16 = rows // (2 * SUB) - 1
    last8 = rows // SUB - 1
    edges = pl.pallas_call(
        pack_kernel,
        grid=(1,),
        out_shape=jax.ShapeDtypeStruct((2, 2, SUB, width), f32),
        in_specs=[
            smem,
            smem,
            pl.BlockSpec((2 * SUB, width), lambda i: (0, 0)),
            pl.BlockSpec((2 * SUB, width), lambda i: (last16, 0)),
            pl.BlockSpec((SUB, width), lambda i: (0, 0)),
            pl.BlockSpec((SUB, width), lambda i: (last8, 0)),
        ],
        out_specs=pl.BlockSpec((2, 2, SUB, width), lambda i: (0, 0, 0, 0)),
        name="pack",
    )(labels, betas, start, start, moment, moment)
    forward = [(i, (i + 1) % strips) for i in range(strips)]
    backward = [((i + 1) % strips, i) for i in range(strips)]
    halos = (lax.ppermute(edges, "dom", forward),)
    if strips > 2:
        halos = halos + (lax.ppermute(edges, "dom", backward),)
    column = pltpu.VMEM((tiles, rows + 2 * SUB, LANES), f32)
    strip = pltpu.VMEM((rows, width), f32)
    out, outgoing, state, energy, sums = pl.pallas_call(
        functools.partial(inner_kernel, per_member),
        out_shape=(
            jax.ShapeDtypeStruct((rows, width), f32),
            jax.ShapeDtypeStruct((members, SUB, piece + LANES), f32),
            jax.ShapeDtypeStruct((2, 2, tiles, EDGE * SUB, LANES), f32),
            jax.ShapeDtypeStruct((2, tiles, 2 * SUB, LANES), f32),
            jax.ShapeDtypeStruct((3, SUB, LANES), f32),
        ),
        in_specs=[smem, smem, smem, anywhere, anywhere],
        out_specs=(anywhere, anywhere, anywhere, anywhere, vmem),
        scratch_shapes=[
            strip,
            strip,
            strip,
            column,
            column,
            pltpu.VMEM((tiles, rows, LANES), f32),
            dma((2, 8)),
            dma((rows // SUB,)),
            dma((members,)),
            dma((2, 3)),
        ],
        cost_estimate=pl.CostEstimate(
            flops=100 * rows * width, bytes_accessed=16 * rows * width, transcendentals=0
        ),
        name="inner",
    )(labels, betas, accept, start, moment)
    window = pltpu.VMEM((2, tiles, (EDGE + 2) * SUB, LANES), f32)
    count = 4 + len(halos)
    out, outgoing = pl.pallas_call(
        functools.partial(outer_kernel, per_member, len(halos)),
        grid=(1,),
        out_shape=(
            jax.ShapeDtypeStruct((rows, width), f32),
            jax.ShapeDtypeStruct((members, SUB, piece + LANES), f32),
        ),
        in_specs=[smem] * 4
        + [vmem] * (len(halos) + 3)
        + [
            pl.BlockSpec((SUB, width), lambda i: (0, 0)),
            pl.BlockSpec((SUB, width), lambda i: (last8, 0)),
            anywhere,
            anywhere,
        ],
        out_specs=(anywhere, anywhere),
        scratch_shapes=[
            window,
            window,
            pltpu.VMEM((2, SUB, width), f32),
            pltpu.VMEM((SUB, LANES), f32),
            dma((2,)),
            dma((2, shares)),
            dma((members,)),
        ],
        input_output_aliases={count + 5: 0, count + 6: 1},
        name="outer",
    )(labels, betas, accept, swap_pairs, *halos, state, energy, sums, start, start, out, outgoing)
    received = lax.all_to_all(outgoing, "rep", split_axis=0, concat_axis=0, tiled=True)
    ordered, notes = pl.pallas_call(
        place_kernel,
        out_shape=(
            jax.ShapeDtypeStruct((members, SUB, piece), f32),
            jax.ShapeDtypeStruct((members, LANES), f32),
        ),
        in_specs=[anywhere],
        out_specs=(anywhere, anywhere),
        scratch_shapes=[
            pltpu.VMEM((members, SUB, piece), f32),
            pltpu.SMEM((members, LANES), f32),
            dma((members,)),
            dma((members,)),
            dma((2,)),
        ],
        name="place",
    )(received)
    returned = lax.all_to_all(ordered, "rep", split_axis=0, concat_axis=0, tiled=True)
    returned = returned.reshape(rows // SUB, shares, SUB, piece).transpose(0, 2, 1, 3)
    returned = returned.reshape(1, rows, width)
    sums = notes
    passing = notes
    for _ in range(strips - 1):
        passing = lax.ppermute(passing, "dom", forward)
        sums = sums + passing
    me = lax.axis_index("rep")
    ladder_index = jnp.arange(betas.shape[0], dtype=jnp.int32)
    held_labels = notes[:, 0].astype(jnp.int32)
    sites = strips * rows * width
    ladder = jnp.sum(jnp.where(held_labels == me, sums[:, 1], 0.0)) / sites
    change = jnp.sum(jnp.where(ladder_index == me, sums[:, 2], 0.0))
    new_label = jnp.sum(jnp.where(ladder_index == me, held_labels, 0))
    return (out[None], returned, new_label[None], change[None], ladder[None])


def solution(mesh):
    placed = (P("rep", "dom", None), P("rep", "dom", None), P("rep"), P(), P("rep"), P())
    return jax.shard_map(
        body,
        mesh=mesh,
        in_specs=placed,
        out_specs=(P("rep", "dom", None), P("rep", "dom", None), P("rep"), P("rep"), P("rep")),
        check_vma=False,
    )
```

```python
import functools

import jax
import jax.numpy as jnp
from jax import lax
from jax.experimental import pallas as pl
from jax.experimental.pallas import tpu as pltpu
from jax.sharding import PartitionSpec as P

STEPS = 8
hopping = 0.18
quartic = 0.3
step_size = 0.05

SUB = 8
LANES = 128
EDGE = 3
GROUP = 7
WHOLE_VMEM = 67043328


def lane_index():
    return lax.broadcasted_iota(jnp.int32, (SUB, LANES), 1)


def row_index():
    return lax.broadcasted_iota(jnp.int32, (SUB, LANES), 0)


class Scales:
    def __init__(self, cold):
        self.cold = cold
        squared = jnp.full((SUB, LANES), (4.0 * quartic * step_size * step_size) * cold)
        self.root = jnp.sqrt(squared)
        self.back = 1.0 / self.root
        self.back2 = self.back * self.back
        self.pull = (2.0 * hopping * step_size * step_size) * cold
        self.slope = -((2.0 - 4.0 * quartic) * step_size * step_size) * cold
        self.speed = step_size * self.root
        self.unspeed = 1.0 / self.speed

    def half(self, near, value):
        return 0.5 * (self.pull * near + value * (self.slope - value * value))

    def step(self, near, value, before):
        return value + ((value - before) + (self.pull * near + value * (self.slope - value * value)))

    def site(self, value, ahead):
        squared = value * value * self.back2
        return (-2.0 * hopping) * (self.back2 * (value * ahead)) + (
            squared + quartic * (squared - 1.0) * (squared - 1.0)
        )


def chosen_scalars(labels_ref, betas_ref):
    return betas_ref[labels_ref[0]]


def beside(values, lane):
    count = len(values)
    ahead = [pltpu.roll(v, 1, 1) for v in values]
    back = [pltpu.roll(v, LANES - 1, 1) for v in values]
    left = [jnp.where(lane == 0, ahead[i - 1], ahead[i]) for i in range(count)]
    right = [jnp.where(lane == LANES - 1, back[(i + 1) % count], back[i]) for i in range(count)]
    return [a + b for a, b in zip(left, right)], right


def around(ref, row, tiles, lane):
    values = [ref[t, pl.ds(row, SUB), :] for t in range(tiles)]
    sums, right = beside(values, lane)
    below = [ref[t, pl.ds(row + 1, SUB), :] for t in range(tiles)]
    near = [(ref[t, pl.ds(row - 1, SUB), :] + below[t]) + sums[t] for t in range(tiles)]
    return values, near, below, right


def advance(before, after, row, tiles, lane, scales, keep=None):
    values, near, _, _ = around(before, row, tiles, lane)
    for t in range(tiles):
        old = after[t, pl.ds(row, SUB), :]
        new = scales.step(near[t], values[t], old)
        if keep is not None:
            new = jnp.where(keep, old, new)
        after[t, pl.ds(row, SUB), :] = new


def pack_kernel(labels_ref, betas_ref, head_ref, tail_ref, head_m_ref, tail_m_ref, out_ref):
    scales = Scales(chosen_scalars(labels_ref, betas_ref))
    lane = lane_index()
    row = row_index()
    tiles = head_ref.shape[1] // LANES
    for side, ref, m_ref in ((0, head_ref, head_m_ref), (1, tail_ref, tail_m_ref)):
        base = 0 if side == 0 else SUB
        inner = SUB - base
        values = [scales.root * ref[base : base + SUB, pl.ds(i * LANES, LANES)] for i in range(tiles)]
        sums, _ = beside(values, lane)
        for i in range(tiles):
            cols = pl.ds(i * LANES, LANES)
            other = scales.root * ref[inner : inner + SUB, cols]
            up = pltpu.roll(values[i], 1, 0)
            down = pltpu.roll(values[i], SUB - 1, 0)
            if side == 0:
                up = jnp.where(row == 0, 0.0, up)
                down = jnp.where(row == SUB - 1, pltpu.roll(other, SUB - 1, 0), down)
            else:
                up = jnp.where(row == 0, pltpu.roll(other, 1, 0), up)
                down = jnp.where(row == SUB - 1, 0.0, down)
            push = scales.speed * m_ref[:, cols] + scales.half((up + down) + sums[i], values[i])
            out_ref[side, 0, i] = values[i]
            out_ref[side, 1, i] = values[i] + push


def slots(row_block, tiles, per_member):
    shares = tiles // per_member
    return [(row_block * shares + s, s * per_member * LANES) for s in range(shares)]


def inner_kernel(
    per_member,
    labels_ref,
    betas_ref,
    accept_ref,
    field_hbm,
    momentum_hbm,
    out_hbm,
    send_hbm,
    state_hbm,
    energy_hbm,
    sums_ref,
    field_ref,
    momentum_ref,
    chosen_ref,
    first,
    second,
    energy,
    in_sem,
    out_sem,
    send_sem,
    state_sem,
):
    rows, width = field_ref.shape
    tiles = width // LANES
    blocks = rows // SUB
    chunk = rows // 8
    loads = []
    for a, (source, target) in enumerate(((field_hbm, field_ref), (momentum_hbm, momentum_ref))):
        for k in range(8):
            part = pl.ds(k * chunk, chunk)
            copy = pltpu.make_async_copy(source.at[part, :], target.at[part, :], in_sem.at[a, k])
            copy.start()
            loads.append(copy)
    scales = Scales(chosen_scalars(labels_ref, betas_ref))
    accepted = accept_ref[0] == 1
    lane = lane_index()
    sub = row_index()
    zero = jnp.zeros((SUB, LANES), jnp.float32)
    for ref in (first, second):
        for t in range(tiles):
            ref[t, 0:SUB, :] = zero
            ref[t, SUB + rows : 2 * SUB + rows, :] = zero
    for k in range(8):
        loads[k].wait()
        for b in range(chunk // SUB):
            row = k * chunk + b * SUB
            for t in range(tiles):
                first[t, SUB + row : 2 * SUB + row, :] = (
                    scales.root * field_ref[row : row + SUB, pl.ds(t * LANES, LANES)]
                )

    def begin(block, total):
        source = pl.multiple_of(block * SUB, SUB)
        row = pl.multiple_of(SUB + block * SUB, SUB)
        values, near, below, right = around(first, row, tiles, lane)
        for t in range(tiles):
            push = scales.speed * momentum_ref[pl.ds(source, SUB), pl.ds(t * LANES, LANES)]
            moment = scales.unspeed * push
            action = scales.site(values[t], below[t] + right[t])
            energy[t, pl.ds(source, SUB), :] = 0.5 * moment * moment + scales.cold * action
            total = total + action
            second[t, pl.ds(row, SUB), :] = values[t] + (push + scales.half(near[t], values[t]))
        return total

    for k in range(8):
        loads[8 + k].wait()

    per_turn = 2

    def begin_turn(i, total):
        for b in range(per_turn):
            total = begin(i * per_turn + b, total)
        return total

    old_action = lax.fori_loop(0, blocks // per_turn, begin_turn, zero)

    group = GROUP if (blocks - 2) % GROUP == 0 else 1
    for time in range(1, STEPS):
        before, after = (second, first) if time % 2 == 1 else (first, second)
        advance(before, after, SUB, tiles, lane, scales, keep=sub <= time)
        advance(before, after, rows, tiles, lane, scales, keep=sub >= SUB - 1 - time)

        def turn(i, carry, before=before, after=after):
            for b in range(group):
                row = pl.multiple_of(2 * SUB + (i * group + b) * SUB, SUB)
                advance(before, after, row, tiles, lane, scales)
            return carry

        lax.fori_loop(0, (blocks - 2) // group, turn, 0)
    last, previous = (first, second) if STEPS % 2 == 0 else (second, first)
    stores = []
    for n, buffer in enumerate((last, previous)):
        for side, row in ((0, SUB), (1, SUB + rows - EDGE * SUB)):
            copy = pltpu.make_async_copy(
                buffer.at[:, pl.ds(row, EDGE * SUB), :], state_hbm.at[side, n], state_sem.at[side, n]
            )
            copy.start()
            stores.append(copy)
    for side, row in ((0, 0), (1, rows - 2 * SUB)):
        copy = pltpu.make_async_copy(
            energy.at[:, pl.ds(row, 2 * SUB), :], energy_hbm.at[side], state_sem.at[side, 2]
        )
        copy.start()
        stores.append(copy)

    def emit(block):
        row = block * SUB
        copies = [
            pltpu.make_async_copy(
                chosen_ref.at[pl.ds(row, SUB), :], out_hbm.at[pl.ds(row, SUB), :], out_sem.at[block]
            )
        ]
        for member, column in slots(block, tiles, per_member):
            width_here = per_member * LANES
            copies.append(
                pltpu.make_async_copy(
                    chosen_ref.at[pl.ds(row, SUB), pl.ds(column, width_here)],
                    send_hbm.at[member],
                    send_sem.at[member],
                )
            )
        return copies

    def choose(block, value, t):
        row = pl.multiple_of(block * SUB, SUB)
        cols = pl.ds(t * LANES, LANES)
        kept = field_ref[pl.ds(row, SUB), cols]
        chosen_ref[pl.ds(row, SUB), cols] = jnp.where(accepted, scales.back * value, kept)

    for block in (1, blocks - 2):
        for t in range(tiles):
            choose(block, last[t, SUB + block * SUB : 2 * SUB + block * SUB, :], t)
        for copy in emit(block):
            copy.start()
            stores.append(copy)

    def finish(block, carry):
        change, total = carry
        row = pl.multiple_of(SUB + block * SUB, SUB)
        source = pl.multiple_of(block * SUB, SUB)
        values, near, below, right = around(last, row, tiles, lane)
        for t in range(tiles):
            gone = values[t] - previous[t, pl.ds(row, SUB), :]
            moment = scales.unspeed * (gone + scales.half(near[t], values[t]))
            action = scales.site(values[t], below[t] + right[t])
            total = total + action
            change = change + (
                (0.5 * moment * moment + scales.cold * action) - energy[t, pl.ds(source, SUB), :]
            )
            choose(block, values[t], t)
        return change, total

    sums = (zero, zero)
    if (blocks - 4) % per_turn == 0:
        for i in range((blocks - 4) // per_turn):
            sums = lax.fori_loop(
                0,
                1,
                lambda _, carry, i=i: functools.reduce(
                    lambda c, b: finish(2 + i * per_turn + b, c), range(per_turn), carry
                ),
                sums,
            )
            for b in range(per_turn):
                for copy in emit(2 + i * per_turn + b):
                    copy.start()
                    stores.append(copy)
    else:
        for block in range(2, blocks - 2):
            sums = finish(block, sums)
            for copy in emit(block):
                copy.start()
                stores.append(copy)
    sums_ref[0] = sums[0]
    sums_ref[1] = sums[1]
    sums_ref[2] = old_action
    for copy in stores:
        copy.wait()


def outer_kernel(
    per_member,
    halos,
    labels_ref,
    betas_ref,
    accept_ref,
    swap_ref,
    *refs,
):
    halo_refs = refs[:halos]
    (
        state_hbm,
        energy_hbm,
        sums_ref,
        head_ref,
        tail_ref,
        _,
        _,
        out_hbm,
        send_hbm,
        note_ref,
        first,
        second,
        energy_ref,
        halo_ref,
        chosen_ref,
        in_sem,
        out_sem,
        send_sem,
    ) = refs[halos:]
    last, previous = (first, second) if STEPS % 2 == 0 else (second, first)
    loads = []
    for side in range(2):
        own = 2 * SUB if side == 0 else 0
        parts = [
            (state_hbm.at[side, n], buffer.at[side, :, pl.ds(own, EDGE * SUB), :])
            for n, buffer in enumerate((last, previous))
        ]
        parts.append((halo_refs[side % halos].at[1 - side], halo_ref.at[side]))
        parts.append((energy_hbm.at[side], energy_ref.at[side]))
        for n, (source, target) in enumerate(parts):
            copy = pltpu.make_async_copy(source, target, in_sem.at[side, n])
            copy.start()
            loads.append(copy)
    scales = Scales(chosen_scalars(labels_ref, betas_ref))
    label = swap_ref[labels_ref[0]].astype(jnp.float32)
    accepted = accept_ref[0] == 1
    lane = lane_index()
    sub = row_index()
    tiles = first.shape[1]
    blocks = out_hbm.shape[0] // SUB
    zero = jnp.zeros((SUB, LANES), jnp.float32)
    old_extra = zero
    energy_extra = []
    for copy in loads:
        copy.wait()
    for side in range(2):
        edge = SUB if side == 0 else EDGE * SUB
        pad = 0 if side == 0 else (EDGE + 1) * SUB
        mine = 2 * SUB if side == 0 else (EDGE - 1) * SUB
        for t in range(tiles):
            for buffer in (last, previous):
                buffer[side, t, pad : pad + SUB, :] = zero
            start_halo = halo_ref[side, 0, t]
            start_mine = first[side, t, mine : mine + SUB, :]
            if side == 0:
                own_part = jnp.where(sub == SUB - 1, pltpu.roll(start_mine, SUB - 1, 0), 0.0)
                halo_part = jnp.where(sub == 0, pltpu.roll(start_halo, 1, 0), 0.0)
            else:
                own_part = jnp.where(sub == 0, pltpu.roll(start_mine, 1, 0), 0.0)
                halo_part = jnp.where(sub == SUB - 1, pltpu.roll(start_halo, SUB - 1, 0), 0.0)
                missing = (-2.0 * hopping) * (scales.back2 * (start_mine * halo_part))
                old_extra = old_extra + missing
                energy_extra.append(scales.cold * missing)
            first[side, t, edge : edge + SUB, :] = start_halo
            second[side, t, edge : edge + SUB, :] = halo_ref[side, 1, t] + (
                0.5 * scales.pull
            ) * own_part
            second[side, t, mine : mine + SUB, :] = (
                second[side, t, mine : mine + SUB, :] + (0.5 * scales.pull) * halo_part
            )
    for time in range(1, STEPS):
        before, after = (second, first) if time % 2 == 1 else (first, second)
        for side in range(2):
            mine = 2 * SUB if side == 0 else (EDGE - 1) * SUB
            edge = SUB if side == 0 else EDGE * SUB
            keep = sub > time if side == 0 else sub < SUB - 1 - time
            advance(before.at[side], after.at[side], edge, tiles, lane, scales)
            advance(before.at[side], after.at[side], mine, tiles, lane, scales, keep=keep)
    change = sums_ref[0]
    total = sums_ref[1]
    copies = []
    for side in range(2):
        own = 2 * SUB if side == 0 else 0
        for b in range(2):
            place = b if side == 0 else EDGE - 2 + b
            row = own + place * SUB
            values, near, below, right = around(last.at[side], row, tiles, lane)
            outermost = (side == 0 and b == 0) or (side == 1 and b == 1)
            for t in range(tiles):
                gone = values[t] - previous[side, t, pl.ds(row, SUB), :]
                moment = scales.unspeed * (gone + scales.half(near[t], values[t]))
                action = scales.site(values[t], below[t] + right[t])
                total = total + action
                old = energy_ref[side, t, b * SUB : (b + 1) * SUB, :]
                if side == 1 and outermost:
                    old = old + energy_extra[t]
                change = change + ((0.5 * moment * moment + scales.cold * action) - old)
                if outermost:
                    cols = pl.ds(t * LANES, LANES)
                    kept = head_ref[:, cols] if side == 0 else tail_ref[:, cols]
                    chosen_ref[side, :, cols] = jnp.where(accepted, scales.back * values[t], kept)
        block = 0 if side == 0 else blocks - 1
        copies.append(
            pltpu.make_async_copy(
                chosen_ref.at[side], out_hbm.at[pl.ds(block * SUB, SUB), :], out_sem.at[side]
            )
        )
        for n, (member, column) in enumerate(slots(block, tiles, per_member)):
            size = per_member * LANES
            copies.append(
                pltpu.make_async_copy(
                    chosen_ref.at[side, :, pl.ds(column, size)],
                    send_hbm.at[member],
                    send_sem.at[side, n],
                )
            )
    for copy in copies:
        copy.start()
    old_action = sums_ref[2] + old_extra
    action = jnp.sum(jnp.where(accepted, total, old_action))
    change = jnp.sum(change)
    note_ref[...] = jnp.where(
        lane == 0, label, jnp.where(lane == 1, action, jnp.where(lane == 2, change, 0.0))
    )[0:1]
    for copy in copies:
        copy.wait()


def place_kernel(got_ref, notes_hbm, out_hbm, labels_ref, sem, note_sem):
    members = out_hbm.shape[0]
    me = lax.axis_index("rep")
    fetch = pltpu.make_async_copy(notes_hbm, labels_ref, note_sem)
    fetch.start()
    fetch.wait()
    copies = []
    for r in range(members):
        slot = labels_ref[lax.rem(members + r - me, members), 0].astype(jnp.int32)
        copy = pltpu.make_async_copy(got_ref.at[r], out_hbm.at[slot], sem.at[r])
        copy.start()
        copies.append(copy)
    for copy in copies:
        copy.wait()


def ladder_kernel(sites, notes_ref, both_ref, label_ref, change_ref, ladder_ref):
    notes = notes_ref[...]
    lane = lax.broadcasted_iota(jnp.int32, notes.shape, 1)
    me = lax.axis_index("rep")
    mine = (lane == 0) & (notes.astype(jnp.int32) == me)
    actions = pltpu.roll(notes, LANES - 1, 1)
    ladder_ref[0] = jnp.sum(jnp.where(mine, actions, 0.0)) / sites
    both = both_ref[...]
    place = lax.broadcasted_iota(jnp.int32, both.shape, 1)
    label_ref[0] = jnp.sum(jnp.where(place == 0, both, 0.0)).astype(jnp.int32)
    change_ref[0] = jnp.sum(jnp.where(place == 2, both, 0.0))


def gather_notes(note, axis, radix=4):
    count = lax.axis_size(axis)
    held = note
    stride = 1
    while stride < count:
        parts = [held]
        for k in range(1, radix):
            if k * stride < count:
                pairs = [((i + k * stride) % count, i) for i in range(count)]
                parts.append(lax.ppermute(held, axis, pairs))
        held = jnp.concatenate(parts, 0)[:count]
        stride *= radix
    return held


def body(field, momentum, labels, betas, accept, swap_pairs):
    rows = field.shape[1]
    width = field.shape[2]
    members = lax.axis_size("rep")
    strips = lax.axis_size("dom")
    tiles = width // LANES
    per_member = (rows // SUB) * tiles // members
    shares = tiles // per_member
    piece = per_member * LANES
    f32 = jnp.float32
    start = field[0]
    moment = momentum[0]
    smem = pl.BlockSpec(memory_space=pltpu.SMEM)
    vmem = pl.BlockSpec(memory_space=pltpu.VMEM)
    anywhere = pl.BlockSpec(memory_space=pl.ANY)
    inhbm = pl.BlockSpec(memory_space=pltpu.HBM)
    dma = pltpu.SemaphoreType.DMA
    last16 = rows // (2 * SUB) - 1
    last8 = rows // SUB - 1
    edges = pl.pallas_call(
        pack_kernel,
        grid=(1,),
        out_shape=jax.ShapeDtypeStruct((2, 2, tiles, SUB, LANES), f32),
        in_specs=[
            smem,
            smem,
            pl.BlockSpec((2 * SUB, width), lambda i: (0, 0)),
            pl.BlockSpec((2 * SUB, width), lambda i: (last16, 0)),
            pl.BlockSpec((SUB, width), lambda i: (0, 0)),
            pl.BlockSpec((SUB, width), lambda i: (last8, 0)),
        ],
        out_specs=pl.BlockSpec((2, 2, tiles, SUB, LANES), lambda i: (0, 0, 0, 0, 0)),
        name="pack",
    )(labels, betas, start, start, moment, moment)
    forward = [(i, (i + 1) % strips) for i in range(strips)]
    backward = [((i + 1) % strips, i) for i in range(strips)]
    halos = (lax.ppermute(edges, "dom", forward),)
    if strips > 2:
        halos = halos + (lax.ppermute(edges, "dom", backward),)
    column = pltpu.VMEM((tiles, rows + 2 * SUB, LANES), f32)
    strip = pltpu.VMEM((rows, width), f32)
    out, outgoing, state, energy, sums = pl.pallas_call(
        functools.partial(inner_kernel, per_member),
        out_shape=(
            jax.ShapeDtypeStruct((rows, width), f32),
            jax.ShapeDtypeStruct((members, SUB, piece), f32),
            jax.ShapeDtypeStruct((2, 2, tiles, EDGE * SUB, LANES), f32),
            jax.ShapeDtypeStruct((2, tiles, 2 * SUB, LANES), f32),
            jax.ShapeDtypeStruct((3, SUB, LANES), f32),
        ),
        in_specs=[smem, smem, smem, inhbm, inhbm],
        out_specs=(inhbm, inhbm, inhbm, inhbm, vmem),
        scratch_shapes=[
            strip,
            strip,
            strip,
            column,
            column,
            pltpu.VMEM((tiles, rows, LANES), f32),
            dma((2, 8)),
            dma((rows // SUB,)),
            dma((members,)),
            dma((2, 3)),
        ],
        cost_estimate=pl.CostEstimate(
            flops=100 * rows * width, bytes_accessed=16 * rows * width, transcendentals=0
        ),
        compiler_params=pltpu.CompilerParams(vmem_limit_bytes=WHOLE_VMEM),
        name="inner",
    )(labels, betas, accept, start, moment)
    window = pltpu.VMEM((2, tiles, (EDGE + 2) * SUB, LANES), f32)
    count = 4 + len(halos)
    out, outgoing, note = pl.pallas_call(
        functools.partial(outer_kernel, per_member, len(halos)),
        grid=(1,),
        out_shape=(
            jax.ShapeDtypeStruct((rows, width), f32),
            jax.ShapeDtypeStruct((members, SUB, piece), f32),
            jax.ShapeDtypeStruct((1, LANES), f32),
        ),
        in_specs=[smem] * 4
        + [anywhere] * len(halos)
        + [inhbm, inhbm, vmem]
        + [
            pl.BlockSpec((SUB, width), lambda i: (0, 0)),
            pl.BlockSpec((SUB, width), lambda i: (last8, 0)),
            inhbm,
            inhbm,
        ],
        out_specs=(inhbm, inhbm, vmem),
        scratch_shapes=[
            window,
            window,
            pltpu.VMEM((2, tiles, 2 * SUB, LANES), f32),
            pltpu.VMEM((2, 2, tiles, SUB, LANES), f32),
            pltpu.VMEM((2, SUB, width), f32),
            dma((2, 4)),
            dma((2,)),
            dma((2, shares)),
        ],
        input_output_aliases={count + 5: 0, count + 6: 1},
        name="outer",
    )(labels, betas, accept, swap_pairs, *halos, state, energy, sums, start, start, out, outgoing)
    received = lax.all_to_all(outgoing, "rep", split_axis=0, concat_axis=0, tiled=True)
    passing = note
    both = note
    for _ in range(strips - 1):
        passing = lax.ppermute(passing, "dom", forward)
        both = both + passing
    both = jnp.where(jnp.arange(LANES)[None, :] == 0, note, both)
    notes = gather_notes(both, "rep")
    ordered = pl.pallas_call(
        place_kernel,
        out_shape=jax.ShapeDtypeStruct((members, SUB, piece), f32),
        in_specs=[anywhere, anywhere],
        out_specs=inhbm,
        scratch_shapes=[
            pltpu.SMEM((members, LANES), f32),
            dma((members,)),
            dma,
        ],
        compiler_params=pltpu.CompilerParams(vmem_limit_bytes=4 << 20),
        name="place",
    )(received, notes)
    returned = lax.all_to_all(ordered, "rep", split_axis=0, concat_axis=0, tiled=True)
    returned = returned.reshape(rows // SUB, shares, SUB, piece).transpose(0, 2, 1, 3)
    returned = returned.reshape(1, rows, width)
    new_label, change, ladder = pl.pallas_call(
        functools.partial(ladder_kernel, strips * rows * width),
        out_shape=(
            jax.ShapeDtypeStruct((1,), jnp.int32),
            jax.ShapeDtypeStruct((1,), f32),
            jax.ShapeDtypeStruct((1,), f32),
        ),
        in_specs=[vmem, vmem],
        out_specs=(smem, smem, smem),
        compiler_params=pltpu.CompilerParams(vmem_limit_bytes=4 << 20),
        name="ladder",
    )(notes, both)
    return (out[None], returned, new_label, change, ladder)


def solution(mesh):
    placed = (P("rep", "dom", None), P("rep", "dom", None), P("rep"), P(), P("rep"), P())
    return jax.shard_map(
        body,
        mesh=mesh,
        in_specs=placed,
        out_specs=(P("rep", "dom", None), P("rep", "dom", None), P("rep"), P("rep"), P("rep")),
        check_vma=False,
    )
```

```python
import functools

import jax
import jax.numpy as jnp
from jax import lax
from jax.experimental import pallas as pl
from jax.experimental.pallas import tpu as pltpu
from jax.sharding import PartitionSpec as P

STEPS = 8
hopping = 0.18
quartic = 0.3
step_size = 0.05

SUB = 8
LANES = 128
EDGE = 3
GROUP = 7
WHOLE_VMEM = 67043328


def lane_index():
    return lax.broadcasted_iota(jnp.int32, (SUB, LANES), 1)


def row_index():
    return lax.broadcasted_iota(jnp.int32, (SUB, LANES), 0)


class Scales:
    def __init__(self, cold):
        self.cold = cold
        squared = jnp.full((SUB, LANES), (4.0 * quartic * step_size * step_size) * cold)
        self.root = jnp.sqrt(squared)
        self.back = 1.0 / self.root
        self.back2 = self.back * self.back
        self.pull = (2.0 * hopping * step_size * step_size) * cold
        self.slope = -((2.0 - 4.0 * quartic) * step_size * step_size) * cold
        self.speed = step_size * self.root
        self.unspeed = 1.0 / self.speed

    def half(self, near, value):
        return 0.5 * (self.pull * near + value * (self.slope - value * value))

    def step(self, near, value, before):
        return value + ((value - before) + (self.pull * near + value * (self.slope - value * value)))

    def site(self, value, ahead):
        squared = value * value * self.back2
        return (-2.0 * hopping) * (self.back2 * (value * ahead)) + (
            squared + quartic * (squared - 1.0) * (squared - 1.0)
        )


def chosen_scalars(labels_ref, betas_ref):
    return betas_ref[labels_ref[0]]


def beside(values, lane):
    count = len(values)
    ahead = [pltpu.roll(v, 1, 1) for v in values]
    back = [pltpu.roll(v, LANES - 1, 1) for v in values]
    left = [jnp.where(lane == 0, ahead[i - 1], ahead[i]) for i in range(count)]
    right = [jnp.where(lane == LANES - 1, back[(i + 1) % count], back[i]) for i in range(count)]
    return [a + b for a, b in zip(left, right)], right


def around(ref, row, tiles, lane):
    values = [ref[t, pl.ds(row, SUB), :] for t in range(tiles)]
    sums, right = beside(values, lane)
    below = [ref[t, pl.ds(row + 1, SUB), :] for t in range(tiles)]
    near = [(ref[t, pl.ds(row - 1, SUB), :] + below[t]) + sums[t] for t in range(tiles)]
    return values, near, below, right


def advance(before, after, row, tiles, lane, scales, keep=None):
    values, near, _, _ = around(before, row, tiles, lane)
    for t in range(tiles):
        old = after[t, pl.ds(row, SUB), :]
        new = scales.step(near[t], values[t], old)
        if keep is not None:
            new = jnp.where(keep, old, new)
        after[t, pl.ds(row, SUB), :] = new


def pack_kernel(labels_ref, betas_ref, head_ref, tail_ref, head_m_ref, tail_m_ref, out_ref):
    scales = Scales(chosen_scalars(labels_ref, betas_ref))
    lane = lane_index()
    row = row_index()
    tiles = head_ref.shape[1] // LANES
    for side, ref, m_ref in ((0, head_ref, head_m_ref), (1, tail_ref, tail_m_ref)):
        base = 0 if side == 0 else SUB
        inner = SUB - base
        values = [scales.root * ref[base : base + SUB, pl.ds(i * LANES, LANES)] for i in range(tiles)]
        sums, _ = beside(values, lane)
        for i in range(tiles):
            cols = pl.ds(i * LANES, LANES)
            other = scales.root * ref[inner : inner + SUB, cols]
            up = pltpu.roll(values[i], 1, 0)
            down = pltpu.roll(values[i], SUB - 1, 0)
            if side == 0:
                up = jnp.where(row == 0, 0.0, up)
                down = jnp.where(row == SUB - 1, pltpu.roll(other, SUB - 1, 0), down)
            else:
                up = jnp.where(row == 0, pltpu.roll(other, 1, 0), up)
                down = jnp.where(row == SUB - 1, 0.0, down)
            push = scales.speed * m_ref[:, cols] + scales.half((up + down) + sums[i], values[i])
            out_ref[side, 0, i] = values[i]
            out_ref[side, 1, i] = values[i] + push


def slots(row_block, tiles, per_member):
    shares = tiles // per_member
    return [(row_block * shares + s, s * per_member * LANES) for s in range(shares)]


def inner_kernel(
    per_member,
    labels_ref,
    betas_ref,
    accept_ref,
    field_hbm,
    momentum_hbm,
    send_hbm,
    state_hbm,
    energy_hbm,
    sums_ref,
    field_ref,
    momentum_ref,
    chosen_ref,
    first,
    second,
    energy,
    in_sem,
    send_sem,
    state_sem,
):
    rows, width = field_ref.shape
    tiles = width // LANES
    blocks = rows // SUB
    chunk = rows // 8
    loads = []
    for a, (source, target) in enumerate(((field_hbm, field_ref), (momentum_hbm, momentum_ref))):
        for k in range(8):
            part = pl.ds(k * chunk, chunk)
            copy = pltpu.make_async_copy(source.at[part, :], target.at[part, :], in_sem.at[a, k])
            copy.start()
            loads.append(copy)
    scales = Scales(chosen_scalars(labels_ref, betas_ref))
    accepted = accept_ref[0] == 1
    lane = lane_index()
    sub = row_index()
    zero = jnp.zeros((SUB, LANES), jnp.float32)
    for ref in (first, second):
        for t in range(tiles):
            ref[t, 0:SUB, :] = zero
            ref[t, SUB + rows : 2 * SUB + rows, :] = zero
    for k in range(8):
        loads[k].wait()
        for b in range(chunk // SUB):
            row = k * chunk + b * SUB
            for t in range(tiles):
                first[t, SUB + row : 2 * SUB + row, :] = (
                    scales.root * field_ref[row : row + SUB, pl.ds(t * LANES, LANES)]
                )

    def begin(block, total):
        source = pl.multiple_of(block * SUB, SUB)
        row = pl.multiple_of(SUB + block * SUB, SUB)
        values, near, below, right = around(first, row, tiles, lane)
        for t in range(tiles):
            push = scales.speed * momentum_ref[pl.ds(source, SUB), pl.ds(t * LANES, LANES)]
            moment = scales.unspeed * push
            action = scales.site(values[t], below[t] + right[t])
            energy[t, pl.ds(source, SUB), :] = 0.5 * moment * moment + scales.cold * action
            total = total + action
            second[t, pl.ds(row, SUB), :] = values[t] + (push + scales.half(near[t], values[t]))
        return total

    for k in range(8):
        loads[8 + k].wait()

    per_turn = 2

    def begin_turn(i, total):
        for b in range(per_turn):
            total = begin(i * per_turn + b, total)
        return total

    old_action = lax.fori_loop(0, blocks // per_turn, begin_turn, zero)

    group = GROUP if (blocks - 2) % GROUP == 0 else 1
    for time in range(1, STEPS):
        before, after = (second, first) if time % 2 == 1 else (first, second)
        advance(before, after, SUB, tiles, lane, scales, keep=sub <= time)
        advance(before, after, rows, tiles, lane, scales, keep=sub >= SUB - 1 - time)

        def turn(i, carry, before=before, after=after):
            for b in range(group):
                row = pl.multiple_of(2 * SUB + (i * group + b) * SUB, SUB)
                advance(before, after, row, tiles, lane, scales)
            return carry

        lax.fori_loop(0, (blocks - 2) // group, turn, 0)
    last, previous = (first, second) if STEPS % 2 == 0 else (second, first)
    stores = []
    for n, buffer in enumerate((last, previous)):
        for side, row in ((0, SUB), (1, SUB + rows - EDGE * SUB)):
            copy = pltpu.make_async_copy(
                buffer.at[:, pl.ds(row, EDGE * SUB), :], state_hbm.at[side, n], state_sem.at[side, n]
            )
            copy.start()
            stores.append(copy)
    for side, row in ((0, 0), (1, rows - 2 * SUB)):
        copy = pltpu.make_async_copy(
            energy.at[:, pl.ds(row, 2 * SUB), :], energy_hbm.at[side], state_sem.at[side, 2]
        )
        copy.start()
        stores.append(copy)

    def emit(block):
        row = block * SUB
        copies = []
        for member, column in slots(block, tiles, per_member):
            width_here = per_member * LANES
            copies.append(
                pltpu.make_async_copy(
                    chosen_ref.at[pl.ds(row, SUB), pl.ds(column, width_here)],
                    send_hbm.at[member, :, pl.ds(0, width_here)],
                    send_sem.at[member],
                )
            )
        return copies

    def choose(block, value, t):
        row = pl.multiple_of(block * SUB, SUB)
        cols = pl.ds(t * LANES, LANES)
        kept = field_ref[pl.ds(row, SUB), cols]
        chosen_ref[pl.ds(row, SUB), cols] = jnp.where(accepted, scales.back * value, kept)

    for block in (1, blocks - 2):
        for t in range(tiles):
            choose(block, last[t, SUB + block * SUB : 2 * SUB + block * SUB, :], t)
        for copy in emit(block):
            copy.start()
            stores.append(copy)

    def finish(block, carry):
        change, total = carry
        row = pl.multiple_of(SUB + block * SUB, SUB)
        source = pl.multiple_of(block * SUB, SUB)
        values, near, below, right = around(last, row, tiles, lane)
        for t in range(tiles):
            gone = values[t] - previous[t, pl.ds(row, SUB), :]
            moment = scales.unspeed * (gone + scales.half(near[t], values[t]))
            action = scales.site(values[t], below[t] + right[t])
            total = total + action
            change = change + (
                (0.5 * moment * moment + scales.cold * action) - energy[t, pl.ds(source, SUB), :]
            )
            choose(block, values[t], t)
        return change, total

    sums = (zero, zero)
    if (blocks - 4) % per_turn == 0:
        for i in range((blocks - 4) // per_turn):
            sums = lax.fori_loop(
                0,
                1,
                lambda _, carry, i=i: functools.reduce(
                    lambda c, b: finish(2 + i * per_turn + b, c), range(per_turn), carry
                ),
                sums,
            )
            for b in range(per_turn):
                for copy in emit(2 + i * per_turn + b):
                    copy.start()
                    stores.append(copy)
    else:
        for block in range(2, blocks - 2):
            sums = finish(block, sums)
            for copy in emit(block):
                copy.start()
                stores.append(copy)
    sums_ref[0] = sums[0]
    sums_ref[1] = sums[1]
    sums_ref[2] = old_action
    for copy in stores:
        copy.wait()


def outer_kernel(
    per_member,
    halos,
    labels_ref,
    betas_ref,
    accept_ref,
    swap_ref,
    *refs,
):
    halo_refs = refs[:halos]
    (
        state_hbm,
        energy_hbm,
        sums_ref,
        head_ref,
        tail_ref,
        _,
        send_hbm,
        first,
        second,
        energy_ref,
        halo_ref,
        chosen_ref,
        note_ref,
        in_sem,
        send_sem,
        note_sem,
    ) = refs[halos:]
    last, previous = (first, second) if STEPS % 2 == 0 else (second, first)
    loads = []
    for side in range(2):
        own = 2 * SUB if side == 0 else 0
        parts = [
            (state_hbm.at[side, n], buffer.at[side, :, pl.ds(own, EDGE * SUB), :])
            for n, buffer in enumerate((last, previous))
        ]
        parts.append((halo_refs[side % halos].at[1 - side], halo_ref.at[side]))
        parts.append((energy_hbm.at[side], energy_ref.at[side]))
        for n, (source, target) in enumerate(parts):
            copy = pltpu.make_async_copy(source, target, in_sem.at[side, n])
            copy.start()
            loads.append(copy)
    scales = Scales(chosen_scalars(labels_ref, betas_ref))
    label = swap_ref[labels_ref[0]].astype(jnp.float32)
    accepted = accept_ref[0] == 1
    lane = lane_index()
    sub = row_index()
    tiles = first.shape[1]
    members = send_hbm.shape[0]
    blocks = members * per_member // tiles
    zero = jnp.zeros((SUB, LANES), jnp.float32)
    old_extra = zero
    energy_extra = []
    for copy in loads:
        copy.wait()
    for side in range(2):
        edge = SUB if side == 0 else EDGE * SUB
        pad = 0 if side == 0 else (EDGE + 1) * SUB
        mine = 2 * SUB if side == 0 else (EDGE - 1) * SUB
        for t in range(tiles):
            for buffer in (last, previous):
                buffer[side, t, pad : pad + SUB, :] = zero
            start_halo = halo_ref[side, 0, t]
            start_mine = first[side, t, mine : mine + SUB, :]
            if side == 0:
                own_part = jnp.where(sub == SUB - 1, pltpu.roll(start_mine, SUB - 1, 0), 0.0)
                halo_part = jnp.where(sub == 0, pltpu.roll(start_halo, 1, 0), 0.0)
            else:
                own_part = jnp.where(sub == 0, pltpu.roll(start_mine, 1, 0), 0.0)
                halo_part = jnp.where(sub == SUB - 1, pltpu.roll(start_halo, SUB - 1, 0), 0.0)
                missing = (-2.0 * hopping) * (scales.back2 * (start_mine * halo_part))
                old_extra = old_extra + missing
                energy_extra.append(scales.cold * missing)
            first[side, t, edge : edge + SUB, :] = start_halo
            second[side, t, edge : edge + SUB, :] = halo_ref[side, 1, t] + (
                0.5 * scales.pull
            ) * own_part
            second[side, t, mine : mine + SUB, :] = (
                second[side, t, mine : mine + SUB, :] + (0.5 * scales.pull) * halo_part
            )
    for time in range(1, STEPS):
        before, after = (second, first) if time % 2 == 1 else (first, second)
        for side in range(2):
            mine = 2 * SUB if side == 0 else (EDGE - 1) * SUB
            edge = SUB if side == 0 else EDGE * SUB
            keep = sub > time if side == 0 else sub < SUB - 1 - time
            advance(before.at[side], after.at[side], edge, tiles, lane, scales)
            advance(before.at[side], after.at[side], mine, tiles, lane, scales, keep=keep)
    change = sums_ref[0]
    total = sums_ref[1]
    copies = []
    for side in range(2):
        own = 2 * SUB if side == 0 else 0
        for b in range(2):
            place = b if side == 0 else EDGE - 2 + b
            row = own + place * SUB
            values, near, below, right = around(last.at[side], row, tiles, lane)
            outermost = (side == 0 and b == 0) or (side == 1 and b == 1)
            for t in range(tiles):
                gone = values[t] - previous[side, t, pl.ds(row, SUB), :]
                moment = scales.unspeed * (gone + scales.half(near[t], values[t]))
                action = scales.site(values[t], below[t] + right[t])
                total = total + action
                old = energy_ref[side, t, b * SUB : (b + 1) * SUB, :]
                if side == 1 and outermost:
                    old = old + energy_extra[t]
                change = change + ((0.5 * moment * moment + scales.cold * action) - old)
                if outermost:
                    cols = pl.ds(t * LANES, LANES)
                    kept = head_ref[:, cols] if side == 0 else tail_ref[:, cols]
                    chosen_ref[side, :, cols] = jnp.where(accepted, scales.back * values[t], kept)
        block = 0 if side == 0 else blocks - 1
        for n, (member, column) in enumerate(slots(block, tiles, per_member)):
            size = per_member * LANES
            copies.append(
                pltpu.make_async_copy(
                    chosen_ref.at[side, :, pl.ds(column, size)],
                    send_hbm.at[member, :, pl.ds(0, size)],
                    send_sem.at[side, n],
                )
            )
    for copy in copies:
        copy.start()
    old_action = sums_ref[2] + old_extra
    action = jnp.sum(jnp.where(accepted, total, old_action))
    change = jnp.sum(change)
    note_ref[...] = jnp.where(
        lane == 0, label, jnp.where(lane == 1, action, jnp.where(lane == 2, change, 0.0))
    )
    for member in range(members):
        copy = pltpu.make_async_copy(
            note_ref,
            send_hbm.at[member, :, pl.ds(per_member * LANES, LANES)],
            note_sem.at[member],
        )
        copy.start()
        copies.append(copy)
    for copy in copies:
        copy.wait()


def place_kernel(got_ref, _, out_hbm, notes_hbm, labels_ref, sem, note_sem):
    members, _, width = out_hbm.shape
    notes = got_ref.at[:, 0, pl.ds(width, LANES)]
    fetch = pltpu.make_async_copy(notes, labels_ref, note_sem.at[0])
    fetch.start()
    keep = pltpu.make_async_copy(notes, notes_hbm, note_sem.at[1])
    keep.start()
    fetch.wait()
    copies = []
    for r in range(members):
        slot = labels_ref[r, 0].astype(jnp.int32)
        copy = pltpu.make_async_copy(got_ref.at[r, :, pl.ds(0, width)], out_hbm.at[slot], sem.at[r])
        copy.start()
        copies.append(copy)
    keep.wait()
    for copy in copies:
        copy.wait()


def ladder_kernel(sites, notes_ref, sums_ref, label_ref, change_ref, ladder_ref):
    me = lax.axis_index("rep")
    notes = notes_ref[...]
    sums = sums_ref[...]
    lane = lax.broadcasted_iota(jnp.int32, notes.shape, 1)
    replica = lax.broadcasted_iota(jnp.int32, notes.shape, 0)
    held = (lane == 0) & (notes.astype(jnp.int32) == me)
    actions = pltpu.roll(sums, LANES - 1, 1)
    ladder_ref[0] = jnp.sum(jnp.where(held, actions, 0.0)) / sites
    own = replica == me
    label_ref[0] = jnp.sum(jnp.where(own & (lane == 0), notes, 0.0)).astype(jnp.int32)
    change_ref[0] = jnp.sum(jnp.where(own & (lane == 2), sums, 0.0))


def body(field, momentum, labels, betas, accept, swap_pairs):
    rows = field.shape[1]
    width = field.shape[2]
    members = lax.axis_size("rep")
    strips = lax.axis_size("dom")
    tiles = width // LANES
    per_member = (rows // SUB) * tiles // members
    shares = tiles // per_member
    piece = per_member * LANES
    f32 = jnp.float32
    start = field[0]
    moment = momentum[0]
    smem = pl.BlockSpec(memory_space=pltpu.SMEM)
    vmem = pl.BlockSpec(memory_space=pltpu.VMEM)
    anywhere = pl.BlockSpec(memory_space=pl.ANY)
    inhbm = pl.BlockSpec(memory_space=pltpu.HBM)
    dma = pltpu.SemaphoreType.DMA
    last16 = rows // (2 * SUB) - 1
    last8 = rows // SUB - 1
    edges = pl.pallas_call(
        pack_kernel,
        grid=(1,),
        out_shape=jax.ShapeDtypeStruct((2, 2, tiles, SUB, LANES), f32),
        in_specs=[
            smem,
            smem,
            pl.BlockSpec((2 * SUB, width), lambda i: (0, 0)),
            pl.BlockSpec((2 * SUB, width), lambda i: (last16, 0)),
            pl.BlockSpec((SUB, width), lambda i: (0, 0)),
            pl.BlockSpec((SUB, width), lambda i: (last8, 0)),
        ],
        out_specs=pl.BlockSpec((2, 2, tiles, SUB, LANES), lambda i: (0, 0, 0, 0, 0)),
        name="pack",
    )(labels, betas, start, start, moment, moment)
    forward = [(i, (i + 1) % strips) for i in range(strips)]
    backward = [((i + 1) % strips, i) for i in range(strips)]
    halos = (lax.ppermute(edges, "dom", forward),)
    if strips > 2:
        halos = halos + (lax.ppermute(edges, "dom", backward),)

    def strip_of(pieces):
        grouped = pieces.reshape(rows // SUB, shares, SUB, piece).transpose(0, 2, 1, 3)
        return grouped.reshape(1, rows, width)

    column = pltpu.VMEM((tiles, rows + 2 * SUB, LANES), f32)
    strip = pltpu.VMEM((rows, width), f32)
    outgoing, state, energy, sums = pl.pallas_call(
        functools.partial(inner_kernel, per_member),
        out_shape=(
            jax.ShapeDtypeStruct((members, SUB, piece + LANES), f32),
            jax.ShapeDtypeStruct((2, 2, tiles, EDGE * SUB, LANES), f32),
            jax.ShapeDtypeStruct((2, tiles, 2 * SUB, LANES), f32),
            jax.ShapeDtypeStruct((3, SUB, LANES), f32),
        ),
        in_specs=[smem, smem, smem, inhbm, inhbm],
        out_specs=(inhbm, inhbm, inhbm, vmem),
        scratch_shapes=[
            strip,
            strip,
            strip,
            column,
            column,
            pltpu.VMEM((tiles, rows, LANES), f32),
            dma((2, 8)),
            dma((members,)),
            dma((2, 3)),
        ],
        cost_estimate=pl.CostEstimate(
            flops=100 * rows * width, bytes_accessed=16 * rows * width, transcendentals=0
        ),
        compiler_params=pltpu.CompilerParams(vmem_limit_bytes=WHOLE_VMEM),
        name="inner",
    )(labels, betas, accept, start, moment)
    window = pltpu.VMEM((2, tiles, (EDGE + 2) * SUB, LANES), f32)
    count = 4 + len(halos)
    outgoing = pl.pallas_call(
        functools.partial(outer_kernel, per_member, len(halos)),
        grid=(1,),
        out_shape=jax.ShapeDtypeStruct((members, SUB, piece + LANES), f32),
        in_specs=[smem] * 4
        + [anywhere] * len(halos)
        + [inhbm, inhbm, vmem]
        + [
            pl.BlockSpec((SUB, width), lambda i: (0, 0)),
            pl.BlockSpec((SUB, width), lambda i: (last8, 0)),
            inhbm,
        ],
        out_specs=inhbm,
        scratch_shapes=[
            window,
            window,
            pltpu.VMEM((2, tiles, 2 * SUB, LANES), f32),
            pltpu.VMEM((2, 2, tiles, SUB, LANES), f32),
            pltpu.VMEM((2, SUB, width), f32),
            pltpu.VMEM((SUB, LANES), f32),
            dma((2, 4)),
            dma((2, shares)),
            dma((members,)),
        ],
        input_output_aliases={count + 5: 0},
        name="outer",
    )(labels, betas, accept, swap_pairs, *halos, state, energy, sums, start, start, outgoing)
    received = lax.all_to_all(outgoing, "rep", split_axis=0, concat_axis=0, tiled=True)
    out = strip_of(outgoing[:, :, :piece])
    ordered, notes = pl.pallas_call(
        place_kernel,
        out_shape=(
            jax.ShapeDtypeStruct((members, SUB, piece), f32),
            jax.ShapeDtypeStruct((members, LANES), f32),
        ),
        in_specs=[anywhere, anywhere],
        out_specs=(inhbm, inhbm),
        scratch_shapes=[
            pltpu.SMEM((members, LANES), f32),
            dma((members,)),
            dma((2,)),
        ],
        compiler_params=pltpu.CompilerParams(vmem_limit_bytes=4 << 20),
        name="place",
    )(received, out)
    returned = lax.all_to_all(ordered, "rep", split_axis=0, concat_axis=0, tiled=True)
    passing = notes
    both = notes
    for _ in range(strips - 1):
        passing = lax.ppermute(passing, "dom", forward)
        both = both + passing
    new_label, change, ladder = pl.pallas_call(
        functools.partial(ladder_kernel, strips * rows * width),
        out_shape=(
            jax.ShapeDtypeStruct((1,), jnp.int32),
            jax.ShapeDtypeStruct((1,), f32),
            jax.ShapeDtypeStruct((1,), f32),
        ),
        in_specs=[vmem, vmem],
        out_specs=(smem, smem, smem),
        compiler_params=pltpu.CompilerParams(vmem_limit_bytes=4 << 20),
        name="ladder",
    )(notes, both)
    return (out, strip_of(returned), new_label, change, ladder)


def solution(mesh):
    placed = (P("rep", "dom", None), P("rep", "dom", None), P("rep"), P(), P("rep"), P())
    return jax.shard_map(
        body,
        mesh=mesh,
        in_specs=placed,
        out_specs=(P("rep", "dom", None), P("rep", "dom", None), P("rep"), P("rep"), P("rep")),
        check_vma=False,
    )
```

```python
import functools

import jax
import jax.numpy as jnp
from jax import lax
from jax.experimental import pallas as pl
from jax.experimental.pallas import tpu as pltpu
from jax.sharding import PartitionSpec as P

STEPS = 8
hopping = 0.18
quartic = 0.3
step_size = 0.05

SUB = 8
LANES = 128
EDGE = 3
GROUP = 14
WHOLE_VMEM = 67043328


def lane_index():
    return lax.broadcasted_iota(jnp.int32, (SUB, LANES), 1)


def row_index():
    return lax.broadcasted_iota(jnp.int32, (SUB, LANES), 0)


class Scales:
    def __init__(self, cold):
        self.cold = cold
        squared = jnp.full((SUB, LANES), (4.0 * quartic * step_size * step_size) * cold)
        self.root = jnp.sqrt(squared)
        self.back = 1.0 / self.root
        self.back2 = self.back * self.back
        self.pull = (2.0 * hopping * step_size * step_size) * cold
        self.slope = -((2.0 - 4.0 * quartic) * step_size * step_size) * cold
        self.speed = step_size * self.root
        self.linear = ((1.0 - 2.0 * quartic) * cold) * self.back2
        self.square = (quartic * cold) * (self.back2 * self.back2)
        self.bond = ((2.0 * hopping) * cold) * self.back2
        unspeed = 1.0 / self.speed
        self.kinetic = 0.5 * (unspeed * unspeed)

    def half(self, near, value):
        return 0.5 * (self.pull * near + value * (self.slope - value * value))

    def step(self, near, value, before):
        return value + ((value - before) + (self.pull * near + value * (self.slope - value * value)))

    def site(self, value, ahead):
        squared = value * value
        return squared * (self.linear + self.square * squared) - self.bond * (value * ahead)

    def action(self, total, sites):
        return jnp.sum(total) / self.cold + quartic * sites


def chosen_scalars(labels_ref, betas_ref):
    return betas_ref[labels_ref[0]]


def beside(values, lane):
    count = len(values)
    ahead = [pltpu.roll(v, 1, 1) for v in values]
    back = [pltpu.roll(v, LANES - 1, 1) for v in values]
    left = [jnp.where(lane == 0, ahead[i - 1], ahead[i]) for i in range(count)]
    right = [jnp.where(lane == LANES - 1, back[(i + 1) % count], back[i]) for i in range(count)]
    return [a + b for a, b in zip(left, right)], right


def around(ref, row, tiles, lane):
    load = lambda t: ref[t % tiles, pl.ds(row, SUB), :]
    ahead = pltpu.roll(load(tiles - 1), 1, 1)
    value = load(0)
    first_back = pltpu.roll(value, LANES - 1, 1)
    back = first_back
    for t in range(tiles):
        following = load(t + 1)
        behind, ahead = ahead, pltpu.roll(value, 1, 1)
        back_next = first_back if t == tiles - 1 else pltpu.roll(following, LANES - 1, 1)
        left = jnp.where(lane == 0, behind, ahead)
        right = jnp.where(lane == LANES - 1, back_next, back)
        below = ref[t, pl.ds(row + 1, SUB), :]
        near = (ref[t, pl.ds(row - 1, SUB), :] + below) + (left + right)
        yield t, value, near, below, right
        value, back = following, back_next


def advance(before, after, row, tiles, lane, scales, keep=None):
    for t, value, near, _, _ in around(before, row, tiles, lane):
        old = after[t, pl.ds(row, SUB), :]
        new = scales.step(near, value, old)
        if keep is not None:
            new = jnp.where(keep, old, new)
        after[t, pl.ds(row, SUB), :] = new


def pack_kernel(labels_ref, betas_ref, head_ref, tail_ref, head_m_ref, tail_m_ref, out_ref):
    scales = Scales(chosen_scalars(labels_ref, betas_ref))
    lane = lane_index()
    row = row_index()
    tiles = head_ref.shape[1] // LANES
    for side, ref, m_ref in ((0, head_ref, head_m_ref), (1, tail_ref, tail_m_ref)):
        base = 0 if side == 0 else SUB
        inner = SUB - base
        values = [scales.root * ref[base : base + SUB, pl.ds(i * LANES, LANES)] for i in range(tiles)]
        sums, _ = beside(values, lane)
        for i in range(tiles):
            cols = pl.ds(i * LANES, LANES)
            other = scales.root * ref[inner : inner + SUB, cols]
            up = pltpu.roll(values[i], 1, 0)
            down = pltpu.roll(values[i], SUB - 1, 0)
            if side == 0:
                up = jnp.where(row == 0, 0.0, up)
                down = jnp.where(row == SUB - 1, pltpu.roll(other, SUB - 1, 0), down)
            else:
                up = jnp.where(row == 0, pltpu.roll(other, 1, 0), up)
                down = jnp.where(row == SUB - 1, 0.0, down)
            push = scales.speed * m_ref[:, cols] + scales.half((up + down) + sums[i], values[i])
            out_ref[side, 0, i] = values[i]
            out_ref[side, 1, i] = values[i] + push


def slots(row_block, tiles, per_member):
    shares = tiles // per_member
    return [(row_block * shares + s, s * per_member * LANES) for s in range(shares)]


def inner_kernel(
    per_member,
    labels_ref,
    betas_ref,
    accept_ref,
    field_hbm,
    momentum_hbm,
    send_hbm,
    state_hbm,
    energy_hbm,
    sums_ref,
    field_ref,
    momentum_ref,
    chosen_ref,
    first,
    second,
    energy,
    in_sem,
    send_sem,
    state_sem,
):
    rows, width = field_ref.shape
    tiles = width // LANES
    blocks = rows // SUB
    chunk = rows // 8
    loads = []
    for a, (source, target) in enumerate(((field_hbm, field_ref), (momentum_hbm, momentum_ref))):
        for k in range(8):
            part = pl.ds(k * chunk, chunk)
            copy = pltpu.make_async_copy(source.at[part, :], target.at[part, :], in_sem.at[a, k])
            copy.start()
            loads.append(copy)
    scales = Scales(chosen_scalars(labels_ref, betas_ref))
    accepted = accept_ref[0] == 1
    lane = lane_index()
    sub = row_index()
    zero = jnp.zeros((SUB, LANES), jnp.float32)
    for ref in (first, second):
        for t in range(tiles):
            ref[t, 0:SUB, :] = zero
            ref[t, SUB + rows : 2 * SUB + rows, :] = zero
    for k in range(8):
        loads[k].wait()
        for b in range(chunk // SUB):
            row = k * chunk + b * SUB
            for t in range(tiles):
                first[t, SUB + row : 2 * SUB + row, :] = (
                    scales.root * field_ref[row : row + SUB, pl.ds(t * LANES, LANES)]
                )

    def begin(block, total):
        source = pl.multiple_of(block * SUB, SUB)
        row = pl.multiple_of(SUB + block * SUB, SUB)
        for t, value, near, below, right in around(first, row, tiles, lane):
            push = scales.speed * momentum_ref[pl.ds(source, SUB), pl.ds(t * LANES, LANES)]
            action = scales.site(value, below + right)
            energy[t, pl.ds(source, SUB), :] = scales.kinetic * (push * push) + action
            total = total + action
            second[t, pl.ds(row, SUB), :] = value + (push + scales.half(near, value))
        return total

    for k in range(8):
        loads[8 + k].wait()

    per_turn = 2

    def begin_turn(i, total):
        for b in range(per_turn):
            total = begin(i * per_turn + b, total)
        return total

    old_action = lax.fori_loop(0, blocks // per_turn, begin_turn, zero)

    group = GROUP if (blocks - 2) % GROUP == 0 else 1
    for time in range(1, STEPS):
        before, after = (second, first) if time % 2 == 1 else (first, second)
        advance(before, after, SUB, tiles, lane, scales, keep=sub <= time)
        advance(before, after, rows, tiles, lane, scales, keep=sub >= SUB - 1 - time)

        def turn(i, carry, before=before, after=after):
            for b in range(group):
                row = pl.multiple_of(2 * SUB + (i * group + b) * SUB, SUB)
                advance(before, after, row, tiles, lane, scales)
            return carry

        if group == blocks - 2:
            turn(0, 0)
        else:
            lax.fori_loop(0, (blocks - 2) // group, turn, 0)
    last, previous = (first, second) if STEPS % 2 == 0 else (second, first)
    stores = []
    for n, buffer in enumerate((last, previous)):
        for side, row in ((0, SUB), (1, SUB + rows - EDGE * SUB)):
            copy = pltpu.make_async_copy(
                buffer.at[:, pl.ds(row, EDGE * SUB), :], state_hbm.at[side, n], state_sem.at[side, n]
            )
            copy.start()
            stores.append(copy)
    for side, row in ((0, 0), (1, rows - 2 * SUB)):
        copy = pltpu.make_async_copy(
            energy.at[:, pl.ds(row, 2 * SUB), :], energy_hbm.at[side], state_sem.at[side, 2]
        )
        copy.start()
        stores.append(copy)

    def emit(block):
        row = block * SUB
        copies = []
        for member, column in slots(block, tiles, per_member):
            width_here = per_member * LANES
            copies.append(
                pltpu.make_async_copy(
                    chosen_ref.at[pl.ds(row, SUB), pl.ds(column, width_here)],
                    send_hbm.at[member, :, pl.ds(0, width_here)],
                    send_sem.at[member],
                )
            )
        return copies

    def choose(block, value, t):
        row = pl.multiple_of(block * SUB, SUB)
        cols = pl.ds(t * LANES, LANES)
        kept = field_ref[pl.ds(row, SUB), cols]
        chosen_ref[pl.ds(row, SUB), cols] = jnp.where(accepted, scales.back * value, kept)

    for block in (1, blocks - 2):
        for t in range(tiles):
            choose(block, last[t, SUB + block * SUB : 2 * SUB + block * SUB, :], t)
        for copy in emit(block):
            copy.start()
            stores.append(copy)

    def finish(block, carry):
        change, total = carry
        row = pl.multiple_of(SUB + block * SUB, SUB)
        source = pl.multiple_of(block * SUB, SUB)
        for t, value, near, below, right in around(last, row, tiles, lane):
            gone = value - previous[t, pl.ds(row, SUB), :]
            moment = gone + scales.half(near, value)
            action = scales.site(value, below + right)
            total = total + action
            change = change + (
                (scales.kinetic * (moment * moment) + action) - energy[t, pl.ds(source, SUB), :]
            )
            choose(block, value, t)
        return change, total

    sums = (zero, zero)
    if (blocks - 4) % per_turn == 0:
        for i in range((blocks - 4) // per_turn):
            sums = lax.fori_loop(
                0,
                1,
                lambda _, carry, i=i: functools.reduce(
                    lambda c, b: finish(2 + i * per_turn + b, c), range(per_turn), carry
                ),
                sums,
            )
            for b in range(per_turn):
                for copy in emit(2 + i * per_turn + b):
                    copy.start()
                    stores.append(copy)
    else:
        for block in range(2, blocks - 2):
            sums = finish(block, sums)
            for copy in emit(block):
                copy.start()
                stores.append(copy)
    sums_ref[0] = sums[0]
    sums_ref[1] = sums[1]
    sums_ref[2] = old_action
    for copy in stores:
        copy.wait()


def outer_kernel(
    per_member,
    halos,
    labels_ref,
    betas_ref,
    accept_ref,
    swap_ref,
    *refs,
):
    halo_refs = refs[:halos]
    (
        state_hbm,
        energy_hbm,
        sums_ref,
        head_ref,
        tail_ref,
        _,
        send_hbm,
        first,
        second,
        energy_ref,
        halo_ref,
        chosen_ref,
        note_ref,
        in_sem,
        send_sem,
        note_sem,
    ) = refs[halos:]
    last, previous = (first, second) if STEPS % 2 == 0 else (second, first)
    loads = []
    for side in range(2):
        own = 2 * SUB if side == 0 else 0
        parts = [
            (state_hbm.at[side, n], buffer.at[side, :, pl.ds(own, EDGE * SUB), :])
            for n, buffer in enumerate((last, previous))
        ]
        parts.append((halo_refs[side % halos].at[1 - side], halo_ref.at[side]))
        parts.append((energy_hbm.at[side], energy_ref.at[side]))
        for n, (source, target) in enumerate(parts):
            copy = pltpu.make_async_copy(source, target, in_sem.at[side, n])
            copy.start()
            loads.append(copy)
    scales = Scales(chosen_scalars(labels_ref, betas_ref))
    label = swap_ref[labels_ref[0]].astype(jnp.float32)
    accepted = accept_ref[0] == 1
    lane = lane_index()
    sub = row_index()
    tiles = first.shape[1]
    members = send_hbm.shape[0]
    blocks = members * per_member // tiles
    zero = jnp.zeros((SUB, LANES), jnp.float32)
    old_extra = zero
    energy_extra = []
    for copy in loads:
        copy.wait()
    for side in range(2):
        edge = SUB if side == 0 else EDGE * SUB
        pad = 0 if side == 0 else (EDGE + 1) * SUB
        mine = 2 * SUB if side == 0 else (EDGE - 1) * SUB
        for t in range(tiles):
            for buffer in (last, previous):
                buffer[side, t, pad : pad + SUB, :] = zero
            start_halo = halo_ref[side, 0, t]
            start_mine = first[side, t, mine : mine + SUB, :]
            if side == 0:
                own_part = jnp.where(sub == SUB - 1, pltpu.roll(start_mine, SUB - 1, 0), 0.0)
                halo_part = jnp.where(sub == 0, pltpu.roll(start_halo, 1, 0), 0.0)
            else:
                own_part = jnp.where(sub == 0, pltpu.roll(start_mine, 1, 0), 0.0)
                halo_part = jnp.where(sub == SUB - 1, pltpu.roll(start_halo, SUB - 1, 0), 0.0)
                missing = -scales.bond * (start_mine * halo_part)
                old_extra = old_extra + missing
                energy_extra.append(missing)
            first[side, t, edge : edge + SUB, :] = start_halo
            second[side, t, edge : edge + SUB, :] = halo_ref[side, 1, t] + (
                0.5 * scales.pull
            ) * own_part
            second[side, t, mine : mine + SUB, :] = (
                second[side, t, mine : mine + SUB, :] + (0.5 * scales.pull) * halo_part
            )
    for time in range(1, STEPS):
        before, after = (second, first) if time % 2 == 1 else (first, second)
        for side in range(2):
            mine = 2 * SUB if side == 0 else (EDGE - 1) * SUB
            edge = SUB if side == 0 else EDGE * SUB
            keep = sub > time if side == 0 else sub < SUB - 1 - time
            advance(before.at[side], after.at[side], edge, tiles, lane, scales)
            advance(before.at[side], after.at[side], mine, tiles, lane, scales, keep=keep)
    change = sums_ref[0]
    total = sums_ref[1]
    copies = []
    for side in range(2):
        own = 2 * SUB if side == 0 else 0
        for b in range(2):
            place = b if side == 0 else EDGE - 2 + b
            row = own + place * SUB
            outermost = (side == 0 and b == 0) or (side == 1 and b == 1)
            for t, value, near, below, right in around(last.at[side], row, tiles, lane):
                gone = value - previous[side, t, pl.ds(row, SUB), :]
                moment = gone + scales.half(near, value)
                action = scales.site(value, below + right)
                total = total + action
                old = energy_ref[side, t, b * SUB : (b + 1) * SUB, :]
                if side == 1 and outermost:
                    old = old + energy_extra[t]
                change = change + ((scales.kinetic * (moment * moment) + action) - old)
                if outermost:
                    cols = pl.ds(t * LANES, LANES)
                    kept = head_ref[:, cols] if side == 0 else tail_ref[:, cols]
                    chosen_ref[side, :, cols] = jnp.where(accepted, scales.back * value, kept)
        block = 0 if side == 0 else blocks - 1
        for n, (member, column) in enumerate(slots(block, tiles, per_member)):
            size = per_member * LANES
            copies.append(
                pltpu.make_async_copy(
                    chosen_ref.at[side, :, pl.ds(column, size)],
                    send_hbm.at[member, :, pl.ds(0, size)],
                    send_sem.at[side, n],
                )
            )
    for copy in copies:
        copy.start()
    old_action = sums_ref[2] + old_extra
    sites = blocks * SUB * tiles * LANES
    action = scales.action(jnp.where(accepted, total, old_action), sites)
    change = jnp.sum(change)
    note_ref[...] = jnp.where(
        lane == 0, label, jnp.where(lane == 1, action, jnp.where(lane == 2, change, 0.0))
    )
    for member in range(members):
        copy = pltpu.make_async_copy(
            note_ref,
            send_hbm.at[member, :, pl.ds(per_member * LANES, LANES)],
            note_sem.at[member],
        )
        copy.start()
        copies.append(copy)
    for copy in copies:
        copy.wait()


def place_kernel(got_ref, _, out_hbm, notes_hbm, labels_ref, sem, note_sem):
    members, _, width = out_hbm.shape
    notes = got_ref.at[:, 0, pl.ds(width, LANES)]
    fetch = pltpu.make_async_copy(notes, labels_ref, note_sem.at[0])
    fetch.start()
    keep = pltpu.make_async_copy(notes, notes_hbm, note_sem.at[1])
    keep.start()
    fetch.wait()
    copies = []
    for r in range(members):
        slot = labels_ref[r, 0].astype(jnp.int32)
        copy = pltpu.make_async_copy(got_ref.at[r, :, pl.ds(0, width)], out_hbm.at[slot], sem.at[r])
        copy.start()
        copies.append(copy)
    keep.wait()
    for copy in copies:
        copy.wait()


def ladder_kernel(sites, notes_ref, sums_ref, label_ref, change_ref, ladder_ref):
    me = lax.axis_index("rep")
    notes = notes_ref[...]
    sums = sums_ref[...]
    lane = lax.broadcasted_iota(jnp.int32, notes.shape, 1)
    replica = lax.broadcasted_iota(jnp.int32, notes.shape, 0)
    held = (lane == 0) & (notes.astype(jnp.int32) == me)
    actions = pltpu.roll(sums, LANES - 1, 1)
    ladder_ref[0] = jnp.sum(jnp.where(held, actions, 0.0)) / sites
    own = replica == me
    label_ref[0] = jnp.sum(jnp.where(own & (lane == 0), notes, 0.0)).astype(jnp.int32)
    change_ref[0] = jnp.sum(jnp.where(own & (lane == 2), sums, 0.0))


def body(field, momentum, labels, betas, accept, swap_pairs):
    rows = field.shape[1]
    width = field.shape[2]
    members = lax.axis_size("rep")
    strips = lax.axis_size("dom")
    tiles = width // LANES
    per_member = (rows // SUB) * tiles // members
    shares = tiles // per_member
    piece = per_member * LANES
    f32 = jnp.float32
    start = field[0]
    moment = momentum[0]
    smem = pl.BlockSpec(memory_space=pltpu.SMEM)
    vmem = pl.BlockSpec(memory_space=pltpu.VMEM)
    anywhere = pl.BlockSpec(memory_space=pl.ANY)
    inhbm = pl.BlockSpec(memory_space=pltpu.HBM)
    dma = pltpu.SemaphoreType.DMA
    last16 = rows // (2 * SUB) - 1
    last8 = rows // SUB - 1
    edges = pl.pallas_call(
        pack_kernel,
        grid=(1,),
        out_shape=jax.ShapeDtypeStruct((2, 2, tiles, SUB, LANES), f32),
        in_specs=[
            smem,
            smem,
            pl.BlockSpec((2 * SUB, width), lambda i: (0, 0)),
            pl.BlockSpec((2 * SUB, width), lambda i: (last16, 0)),
            pl.BlockSpec((SUB, width), lambda i: (0, 0)),
            pl.BlockSpec((SUB, width), lambda i: (last8, 0)),
        ],
        out_specs=pl.BlockSpec((2, 2, tiles, SUB, LANES), lambda i: (0, 0, 0, 0, 0)),
        name="pack",
    )(labels, betas, start, start, moment, moment)
    forward = [(i, (i + 1) % strips) for i in range(strips)]
    backward = [((i + 1) % strips, i) for i in range(strips)]
    halos = (lax.ppermute(edges, "dom", forward),)
    if strips > 2:
        halos = halos + (lax.ppermute(edges, "dom", backward),)

    def strip_of(pieces):
        grouped = pieces.reshape(rows // SUB, shares, SUB, piece).transpose(0, 2, 1, 3)
        return grouped.reshape(1, rows, width)

    column = pltpu.VMEM((tiles, rows + 2 * SUB, LANES), f32)
    strip = pltpu.VMEM((rows, width), f32)
    outgoing, state, energy, sums = pl.pallas_call(
        functools.partial(inner_kernel, per_member),
        out_shape=(
            jax.ShapeDtypeStruct((members, SUB, piece + LANES), f32),
            jax.ShapeDtypeStruct((2, 2, tiles, EDGE * SUB, LANES), f32),
            jax.ShapeDtypeStruct((2, tiles, 2 * SUB, LANES), f32),
            jax.ShapeDtypeStruct((3, SUB, LANES), f32),
        ),
        in_specs=[smem, smem, smem, inhbm, inhbm],
        out_specs=(inhbm, inhbm, inhbm, vmem),
        scratch_shapes=[
            strip,
            strip,
            strip,
            column,
            column,
            pltpu.VMEM((tiles, rows, LANES), f32),
            dma((2, 8)),
            dma((members,)),
            dma((2, 3)),
        ],
        cost_estimate=pl.CostEstimate(
            flops=100 * rows * width, bytes_accessed=16 * rows * width, transcendentals=0
        ),
        compiler_params=pltpu.CompilerParams(vmem_limit_bytes=WHOLE_VMEM),
        name="inner",
    )(labels, betas, accept, start, moment)
    window = pltpu.VMEM((2, tiles, (EDGE + 2) * SUB, LANES), f32)
    count = 4 + len(halos)
    outgoing = pl.pallas_call(
        functools.partial(outer_kernel, per_member, len(halos)),
        grid=(1,),
        out_shape=jax.ShapeDtypeStruct((members, SUB, piece + LANES), f32),
        in_specs=[smem] * 4
        + [anywhere] * len(halos)
        + [inhbm, inhbm, vmem]
        + [
            pl.BlockSpec((SUB, width), lambda i: (0, 0)),
            pl.BlockSpec((SUB, width), lambda i: (last8, 0)),
            inhbm,
        ],
        out_specs=inhbm,
        scratch_shapes=[
            window,
            window,
            pltpu.VMEM((2, tiles, 2 * SUB, LANES), f32),
            pltpu.VMEM((2, 2, tiles, SUB, LANES), f32),
            pltpu.VMEM((2, SUB, width), f32),
            pltpu.VMEM((SUB, LANES), f32),
            dma((2, 4)),
            dma((2, shares)),
            dma((members,)),
        ],
        input_output_aliases={count + 5: 0},
        name="outer",
    )(labels, betas, accept, swap_pairs, *halos, state, energy, sums, start, start, outgoing)
    received = lax.all_to_all(outgoing, "rep", split_axis=0, concat_axis=0, tiled=True)
    out = strip_of(outgoing[:, :, :piece])
    ordered, notes = pl.pallas_call(
        place_kernel,
        out_shape=(
            jax.ShapeDtypeStruct((members, SUB, piece), f32),
            jax.ShapeDtypeStruct((members, LANES), f32),
        ),
        in_specs=[anywhere, anywhere],
        out_specs=(inhbm, inhbm),
        scratch_shapes=[
            pltpu.SMEM((members, LANES), f32),
            dma((members,)),
            dma((2,)),
        ],
        compiler_params=pltpu.CompilerParams(vmem_limit_bytes=4 << 20),
        name="place",
    )(received, out)
    returned = lax.all_to_all(ordered, "rep", split_axis=0, concat_axis=0, tiled=True)
    passing = notes
    both = notes
    for _ in range(strips - 1):
        passing = lax.ppermute(passing, "dom", forward)
        both = both + passing
    new_label, change, ladder = pl.pallas_call(
        functools.partial(ladder_kernel, strips * rows * width),
        out_shape=(
            jax.ShapeDtypeStruct((1,), jnp.int32),
            jax.ShapeDtypeStruct((1,), f32),
            jax.ShapeDtypeStruct((1,), f32),
        ),
        in_specs=[vmem, vmem],
        out_specs=(smem, smem, smem),
        compiler_params=pltpu.CompilerParams(vmem_limit_bytes=4 << 20),
        name="ladder",
    )(notes, both)
    return (out, strip_of(returned), new_label, change, ladder)


def solution(mesh):
    placed = (P("rep", "dom", None), P("rep", "dom", None), P("rep"), P(), P("rep"), P())
    return jax.shard_map(
        body,
        mesh=mesh,
        in_specs=placed,
        out_specs=(P("rep", "dom", None), P("rep", "dom", None), P("rep"), P("rep"), P("rep")),
        check_vma=False,
    )
```

```python
import functools

import jax
import jax.numpy as jnp
from jax import lax
from jax.experimental import pallas as pl
from jax.experimental.pallas import tpu as pltpu
from jax.sharding import PartitionSpec as P

STEPS = 8
hopping = 0.18
quartic = 0.3
step_size = 0.05

SUB = 8
LANES = 128
EDGE = 3
GROUP = 14
WHOLE_VMEM = 67043328


def lane_index():
    return lax.broadcasted_iota(jnp.int32, (SUB, LANES), 1)


def row_index():
    return lax.broadcasted_iota(jnp.int32, (SUB, LANES), 0)


class Scales:
    def __init__(self, cold):
        self.cold = cold
        squared = jnp.full((SUB, LANES), (4.0 * quartic * step_size * step_size) * cold)
        self.root = jnp.sqrt(squared)
        self.back = 1.0 / self.root
        self.back2 = self.back * self.back
        self.pull = (2.0 * hopping * step_size * step_size) * cold
        self.slope = -((2.0 - 4.0 * quartic) * step_size * step_size) * cold
        self.speed = step_size * self.root
        self.linear = ((1.0 - 2.0 * quartic) * cold) * self.back2
        self.square = (quartic * cold) * (self.back2 * self.back2)
        self.bond = ((2.0 * hopping) * cold) * self.back2
        unspeed = 1.0 / self.speed
        self.kinetic = 0.5 * (unspeed * unspeed)

    def half(self, near, value):
        return 0.5 * (self.pull * near + value * (self.slope - value * value))

    def step(self, near, value, before):
        return value + ((value - before) + (self.pull * near + value * (self.slope - value * value)))

    def site(self, value, ahead):
        squared = value * value
        return squared * (self.linear + self.square * squared) - self.bond * (value * ahead)

    def action(self, total, sites):
        return jnp.sum(total) / self.cold + quartic * sites


def fetch(copies):
    started = [pltpu.make_async_copy(*copy) for copy in copies]
    for copy in started:
        copy.start()
    return started


def beside(values, lane):
    count = len(values)
    ahead = [pltpu.roll(v, 1, 1) for v in values]
    back = [pltpu.roll(v, LANES - 1, 1) for v in values]
    left = [jnp.where(lane == 0, ahead[i - 1], ahead[i]) for i in range(count)]
    right = [jnp.where(lane == LANES - 1, back[(i + 1) % count], back[i]) for i in range(count)]
    return [a + b for a, b in zip(left, right)], right


def around(ref, row, tiles, lane):
    load = lambda t: ref[t % tiles, pl.ds(row, SUB), :]
    ahead = pltpu.roll(load(tiles - 1), 1, 1)
    value = load(0)
    first_back = pltpu.roll(value, LANES - 1, 1)
    back = first_back
    for t in range(tiles):
        following = load(t + 1)
        behind, ahead = ahead, pltpu.roll(value, 1, 1)
        back_next = first_back if t == tiles - 1 else pltpu.roll(following, LANES - 1, 1)
        left = jnp.where(lane == 0, behind, ahead)
        right = jnp.where(lane == LANES - 1, back_next, back)
        below = ref[t, pl.ds(row + 1, SUB), :]
        near = (ref[t, pl.ds(row - 1, SUB), :] + below) + (left + right)
        yield t, value, near, below, right
        value, back = following, back_next


def advance(before, after, row, tiles, lane, scales, keep=None):
    for t, value, near, _, _ in around(before, row, tiles, lane):
        old = after[t, pl.ds(row, SUB), :]
        new = scales.step(near, value, old)
        if keep is not None:
            new = jnp.where(keep, old, new)
        after[t, pl.ds(row, SUB), :] = new


def pack_kernel(
    betas_ref, labels_hbm, field_hbm, momentum_hbm, out_ref, labels_ref, field_ref, moment_ref, sem
):
    rows = field_hbm.shape[0]
    loads = fetch(
        [(labels_hbm, labels_ref, sem.at[0])]
        + [
            (field_hbm.at[pl.ds(start, 2 * SUB), :], field_ref.at[side], sem.at[1 + side])
            for side, start in enumerate((0, rows - 2 * SUB))
        ]
        + [
            (momentum_hbm.at[pl.ds(start, SUB), :], moment_ref.at[side], sem.at[3 + side])
            for side, start in enumerate((0, rows - SUB))
        ]
    )
    for load in loads:
        load.wait()
    scales = Scales(betas_ref[labels_ref[0]])
    lane = lane_index()
    row = row_index()
    tiles = field_ref.shape[2] // LANES
    for side in range(2):
        ref = field_ref.at[side]
        m_ref = moment_ref.at[side]
        base = 0 if side == 0 else SUB
        inner = SUB - base
        values = [scales.root * ref[base : base + SUB, pl.ds(i * LANES, LANES)] for i in range(tiles)]
        sums, _ = beside(values, lane)
        for i in range(tiles):
            cols = pl.ds(i * LANES, LANES)
            other = scales.root * ref[inner : inner + SUB, cols]
            up = pltpu.roll(values[i], 1, 0)
            down = pltpu.roll(values[i], SUB - 1, 0)
            if side == 0:
                up = jnp.where(row == 0, 0.0, up)
                down = jnp.where(row == SUB - 1, pltpu.roll(other, SUB - 1, 0), down)
            else:
                up = jnp.where(row == 0, pltpu.roll(other, 1, 0), up)
                down = jnp.where(row == SUB - 1, 0.0, down)
            push = scales.speed * m_ref[:, cols] + scales.half((up + down) + sums[i], values[i])
            out_ref[side, 0, i] = values[i]
            out_ref[side, 1, i] = values[i] + push


def slots(row_block, tiles, per_member):
    shares = tiles // per_member
    return [(row_block * shares + s, s * per_member * LANES) for s in range(shares)]


def inner_kernel(
    per_member,
    betas_ref,
    labels_hbm,
    accept_hbm,
    field_hbm,
    momentum_hbm,
    send_hbm,
    state_hbm,
    energy_hbm,
    sums_ref,
    labels_ref,
    accept_ref,
    field_ref,
    momentum_ref,
    chosen_ref,
    first,
    second,
    energy,
    in_sem,
    send_sem,
    state_sem,
    scalar_sem,
):
    rows, width = field_ref.shape
    tiles = width // LANES
    blocks = rows // SUB
    chunk = rows // 8
    scalars = fetch(
        [(labels_hbm, labels_ref, scalar_sem.at[0]), (accept_hbm, accept_ref, scalar_sem.at[1])]
    )

    def load(a, k):
        source, target = ((field_hbm, field_ref), (momentum_hbm, momentum_ref))[a]
        part = pl.ds(pl.multiple_of(k * chunk, chunk), chunk)
        return pltpu.make_async_copy(source.at[part, :], target.at[part, :], in_sem.at[a, k])

    for k in range(8):
        load(0, k).start()
        load(1, k).start()
    for copy in scalars:
        copy.wait()
    scales = Scales(betas_ref[labels_ref[0]])
    accepted = accept_ref[0] == 1
    lane = lane_index()
    sub = row_index()
    zero = jnp.zeros((SUB, LANES), jnp.float32)
    for ref in (first, second):
        for t in range(tiles):
            ref[t, 0:SUB, :] = zero
            ref[t, SUB + rows : 2 * SUB + rows, :] = zero

    def bring(k):
        load(0, k).wait()
        for b in range(chunk // SUB):
            row = pl.multiple_of(k * chunk + b * SUB, SUB)
            for t in range(tiles):
                first[t, pl.ds(pl.multiple_of(SUB + row, SUB), SUB), :] = (
                    scales.root * field_ref[pl.ds(row, SUB), pl.ds(t * LANES, LANES)]
                )

    def begin(block, total):
        source = pl.multiple_of(block * SUB, SUB)
        row = pl.multiple_of(SUB + block * SUB, SUB)
        for t, value, near, below, right in around(first, row, tiles, lane):
            push = scales.speed * momentum_ref[pl.ds(source, SUB), pl.ds(t * LANES, LANES)]
            action = scales.site(value, below + right)
            energy[t, pl.ds(source, SUB), :] = scales.kinetic * (push * push) + action
            total = total + action
            second[t, pl.ds(row, SUB), :] = value + (push + scales.half(near, value))
        return total

    per_turn = 2

    def open_chunk(k, total):
        load(1, k).wait()
        for b in range(chunk // SUB):
            total = begin(k * (chunk // SUB) + b, total)
        return total

    def open_turn(k, total):
        bring(k + 1)
        return open_chunk(k, total)

    bring(0)
    old_action = open_chunk(7, lax.fori_loop(0, 7, open_turn, zero))

    group = GROUP if (blocks - 2) % GROUP == 0 else 1
    for time in range(1, STEPS):
        before, after = (second, first) if time % 2 == 1 else (first, second)
        advance(before, after, SUB, tiles, lane, scales, keep=sub <= time)
        advance(before, after, rows, tiles, lane, scales, keep=sub >= SUB - 1 - time)

        def turn(i, carry, before=before, after=after):
            for b in range(group):
                row = pl.multiple_of(2 * SUB + (i * group + b) * SUB, SUB)
                advance(before, after, row, tiles, lane, scales)
            return carry

        if group == blocks - 2:
            turn(0, 0)
        else:
            lax.fori_loop(0, (blocks - 2) // group, turn, 0)
    last, previous = (first, second) if STEPS % 2 == 0 else (second, first)
    stores = []
    for n, buffer in enumerate((last, previous)):
        for side, row in ((0, SUB), (1, SUB + rows - EDGE * SUB)):
            copy = pltpu.make_async_copy(
                buffer.at[:, pl.ds(row, EDGE * SUB), :], state_hbm.at[side, n], state_sem.at[side, n]
            )
            copy.start()
            stores.append(copy)
    for side, row in ((0, 0), (1, rows - 2 * SUB)):
        copy = pltpu.make_async_copy(
            energy.at[:, pl.ds(row, 2 * SUB), :], energy_hbm.at[side], state_sem.at[side, 2]
        )
        copy.start()
        stores.append(copy)

    def emit(block):
        row = block * SUB
        copies = []
        for member, column in slots(block, tiles, per_member):
            width_here = per_member * LANES
            copies.append(
                pltpu.make_async_copy(
                    chosen_ref.at[pl.ds(row, SUB), pl.ds(column, width_here)],
                    send_hbm.at[member, :, pl.ds(0, width_here)],
                    send_sem.at[member],
                )
            )
        return copies

    def choose(block, value, t):
        row = pl.multiple_of(block * SUB, SUB)
        cols = pl.ds(t * LANES, LANES)
        kept = field_ref[pl.ds(row, SUB), cols]
        chosen_ref[pl.ds(row, SUB), cols] = jnp.where(accepted, scales.back * value, kept)

    for block in (1, blocks - 2):
        for t in range(tiles):
            choose(block, last[t, SUB + block * SUB : 2 * SUB + block * SUB, :], t)
        for copy in emit(block):
            copy.start()
            stores.append(copy)

    def finish(block, carry):
        change, total = carry
        row = pl.multiple_of(SUB + block * SUB, SUB)
        source = pl.multiple_of(block * SUB, SUB)
        for t, value, near, below, right in around(last, row, tiles, lane):
            gone = value - previous[t, pl.ds(row, SUB), :]
            moment = gone + scales.half(near, value)
            action = scales.site(value, below + right)
            total = total + action
            change = change + (
                (scales.kinetic * (moment * moment) + action) - energy[t, pl.ds(source, SUB), :]
            )
            choose(block, value, t)
        return change, total

    sums = (zero, zero)
    if (blocks - 4) % per_turn == 0:
        for i in range((blocks - 4) // per_turn):
            sums = lax.fori_loop(
                0,
                1,
                lambda _, carry, i=i: functools.reduce(
                    lambda c, b: finish(2 + i * per_turn + b, c), range(per_turn), carry
                ),
                sums,
            )
            for b in range(per_turn):
                for copy in emit(2 + i * per_turn + b):
                    copy.start()
                    stores.append(copy)
    else:
        for block in range(2, blocks - 2):
            sums = finish(block, sums)
            for copy in emit(block):
                copy.start()
                stores.append(copy)
    sums_ref[0] = sums[0]
    sums_ref[1] = sums[1]
    sums_ref[2] = old_action
    for copy in stores:
        copy.wait()


def outer_kernel(
    per_member,
    halos,
    betas_ref,
    swap_ref,
    labels_hbm,
    accept_hbm,
    *refs,
):
    halo_refs = refs[:halos]
    (
        state_hbm,
        energy_hbm,
        sums_ref,
        head_ref,
        tail_ref,
        _,
        send_hbm,
        labels_ref,
        accept_ref,
        first,
        second,
        energy_ref,
        halo_ref,
        chosen_ref,
        note_ref,
        in_sem,
        send_sem,
        note_sem,
        scalar_sem,
    ) = refs[halos:]
    scalars = fetch(
        [(labels_hbm, labels_ref, scalar_sem.at[0]), (accept_hbm, accept_ref, scalar_sem.at[1])]
    )
    last, previous = (first, second) if STEPS % 2 == 0 else (second, first)
    loads = []
    for side in range(2):
        own = 2 * SUB if side == 0 else 0
        parts = [
            (state_hbm.at[side, n], buffer.at[side, :, pl.ds(own, EDGE * SUB), :])
            for n, buffer in enumerate((last, previous))
        ]
        parts.append((halo_refs[side % halos].at[1 - side], halo_ref.at[side]))
        parts.append((energy_hbm.at[side], energy_ref.at[side]))
        loads.append(fetch([part + (in_sem.at[side, n],) for n, part in enumerate(parts)]))
    for copy in scalars:
        copy.wait()
    scales = Scales(betas_ref[labels_ref[0]])
    label = swap_ref[labels_ref[0]].astype(jnp.float32)
    accepted = accept_ref[0] == 1
    lane = lane_index()
    sub = row_index()
    tiles = first.shape[1]
    members = send_hbm.shape[0]
    blocks = members * per_member // tiles
    zero = jnp.zeros((SUB, LANES), jnp.float32)
    old_extra = zero
    energy_extra = []
    for side in range(2):
        for copy in loads[side][:3]:
            copy.wait()
        edge = SUB if side == 0 else EDGE * SUB
        pad = 0 if side == 0 else (EDGE + 1) * SUB
        mine = 2 * SUB if side == 0 else (EDGE - 1) * SUB
        for t in range(tiles):
            for buffer in (last, previous):
                buffer[side, t, pad : pad + SUB, :] = zero
            start_halo = halo_ref[side, 0, t]
            start_mine = first[side, t, mine : mine + SUB, :]
            if side == 0:
                own_part = jnp.where(sub == SUB - 1, pltpu.roll(start_mine, SUB - 1, 0), 0.0)
                halo_part = jnp.where(sub == 0, pltpu.roll(start_halo, 1, 0), 0.0)
            else:
                own_part = jnp.where(sub == 0, pltpu.roll(start_mine, 1, 0), 0.0)
                halo_part = jnp.where(sub == SUB - 1, pltpu.roll(start_halo, SUB - 1, 0), 0.0)
                missing = -scales.bond * (start_mine * halo_part)
                old_extra = old_extra + missing
                energy_extra.append(missing)
            first[side, t, edge : edge + SUB, :] = start_halo
            second[side, t, edge : edge + SUB, :] = halo_ref[side, 1, t] + (
                0.5 * scales.pull
            ) * own_part
            second[side, t, mine : mine + SUB, :] = (
                second[side, t, mine : mine + SUB, :] + (0.5 * scales.pull) * halo_part
            )
    for time in range(1, STEPS):
        before, after = (second, first) if time % 2 == 1 else (first, second)
        for side in range(2):
            mine = 2 * SUB if side == 0 else (EDGE - 1) * SUB
            edge = SUB if side == 0 else EDGE * SUB
            keep = sub > time if side == 0 else sub < SUB - 1 - time
            advance(before.at[side], after.at[side], edge, tiles, lane, scales)
            advance(before.at[side], after.at[side], mine, tiles, lane, scales, keep=keep)
    change = sums_ref[0]
    total = sums_ref[1]
    copies = []
    for side in range(2):
        loads[side][3].wait()
        own = 2 * SUB if side == 0 else 0
        for b in range(2):
            place = b if side == 0 else EDGE - 2 + b
            row = own + place * SUB
            outermost = (side == 0 and b == 0) or (side == 1 and b == 1)
            for t, value, near, below, right in around(last.at[side], row, tiles, lane):
                gone = value - previous[side, t, pl.ds(row, SUB), :]
                moment = gone + scales.half(near, value)
                action = scales.site(value, below + right)
                total = total + action
                old = energy_ref[side, t, b * SUB : (b + 1) * SUB, :]
                if side == 1 and outermost:
                    old = old + energy_extra[t]
                change = change + ((scales.kinetic * (moment * moment) + action) - old)
                if outermost:
                    cols = pl.ds(t * LANES, LANES)
                    kept = head_ref[:, cols] if side == 0 else tail_ref[:, cols]
                    chosen_ref[side, :, cols] = jnp.where(accepted, scales.back * value, kept)
        block = 0 if side == 0 else blocks - 1
        for n, (member, column) in enumerate(slots(block, tiles, per_member)):
            size = per_member * LANES
            copies.append(
                pltpu.make_async_copy(
                    chosen_ref.at[side, :, pl.ds(column, size)],
                    send_hbm.at[member, :, pl.ds(0, size)],
                    send_sem.at[side, n],
                )
            )
    for copy in copies:
        copy.start()
    old_action = sums_ref[2] + old_extra
    sites = blocks * SUB * tiles * LANES
    action = scales.action(jnp.where(accepted, total, old_action), sites)
    change = jnp.sum(change)
    note_ref[...] = jnp.where(
        lane == 0, label, jnp.where(lane == 1, action, jnp.where(lane == 2, change, 0.0))
    )
    for member in range(members):
        copy = pltpu.make_async_copy(
            note_ref,
            send_hbm.at[member, :, pl.ds(per_member * LANES, LANES)],
            note_sem.at[member],
        )
        copy.start()
        copies.append(copy)
    for copy in copies:
        copy.wait()


def place_kernel(got_ref, _, out_hbm, notes_hbm, labels_ref, sem, note_sem):
    members, _, width = out_hbm.shape
    notes = got_ref.at[:, 0, pl.ds(width, LANES)]
    fetch = pltpu.make_async_copy(notes, labels_ref, note_sem.at[0])
    fetch.start()
    keep = pltpu.make_async_copy(notes, notes_hbm, note_sem.at[1])
    keep.start()
    fetch.wait()
    copies = []
    for r in range(members):
        slot = labels_ref[r, 0].astype(jnp.int32)
        copy = pltpu.make_async_copy(got_ref.at[r, :, pl.ds(0, width)], out_hbm.at[slot], sem.at[r])
        copy.start()
        copies.append(copy)
    keep.wait()
    for copy in copies:
        copy.wait()


def ladder_kernel(sites, notes_ref, sums_ref, label_ref, change_ref, ladder_ref):
    me = lax.axis_index("rep")
    notes = notes_ref[...]
    sums = sums_ref[...]
    lane = lax.broadcasted_iota(jnp.int32, notes.shape, 1)
    replica = lax.broadcasted_iota(jnp.int32, notes.shape, 0)
    held = (lane == 0) & (notes.astype(jnp.int32) == me)
    actions = pltpu.roll(sums, LANES - 1, 1)
    ladder_ref[0] = jnp.sum(jnp.where(held, actions, 0.0)) / sites
    own = replica == me
    label_ref[0] = jnp.sum(jnp.where(own & (lane == 0), notes, 0.0)).astype(jnp.int32)
    change_ref[0] = jnp.sum(jnp.where(own & (lane == 2), sums, 0.0))


def body(field, momentum, labels, betas, accept, swap_pairs):
    rows = field.shape[1]
    width = field.shape[2]
    members = lax.axis_size("rep")
    strips = lax.axis_size("dom")
    tiles = width // LANES
    per_member = (rows // SUB) * tiles // members
    shares = tiles // per_member
    piece = per_member * LANES
    f32 = jnp.float32
    start = field[0]
    moment = momentum[0]
    smem = pl.BlockSpec(memory_space=pltpu.SMEM)
    vmem = pl.BlockSpec(memory_space=pltpu.VMEM)
    anywhere = pl.BlockSpec(memory_space=pl.ANY)
    inhbm = pl.BlockSpec(memory_space=pltpu.HBM)
    dma = pltpu.SemaphoreType.DMA
    last8 = rows // SUB - 1
    scalar = pltpu.SMEM((1,), jnp.int32)
    edges = pl.pallas_call(
        pack_kernel,
        out_shape=jax.ShapeDtypeStruct((2, 2, tiles, SUB, LANES), f32),
        in_specs=[smem, inhbm, inhbm, inhbm],
        out_specs=vmem,
        scratch_shapes=[
            scalar,
            pltpu.VMEM((2, 2 * SUB, width), f32),
            pltpu.VMEM((2, SUB, width), f32),
            dma((5,)),
        ],
        name="pack",
    )(betas, labels, start, moment)
    forward = [(i, (i + 1) % strips) for i in range(strips)]
    backward = [((i + 1) % strips, i) for i in range(strips)]
    halos = (lax.ppermute(edges, "dom", forward),)
    if strips > 2:
        halos = halos + (lax.ppermute(edges, "dom", backward),)

    def strip_of(pieces):
        grouped = pieces.reshape(rows // SUB, shares, SUB, piece).transpose(0, 2, 1, 3)
        return grouped.reshape(1, rows, width)

    column = pltpu.VMEM((tiles, rows + 2 * SUB, LANES), f32)
    strip = pltpu.VMEM((rows, width), f32)
    outgoing, state, energy, sums = pl.pallas_call(
        functools.partial(inner_kernel, per_member),
        out_shape=(
            jax.ShapeDtypeStruct((members, SUB, piece + LANES), f32),
            jax.ShapeDtypeStruct((2, 2, tiles, EDGE * SUB, LANES), f32),
            jax.ShapeDtypeStruct((2, tiles, 2 * SUB, LANES), f32),
            jax.ShapeDtypeStruct((3, SUB, LANES), f32),
        ),
        in_specs=[smem, inhbm, inhbm, inhbm, inhbm],
        out_specs=(inhbm, inhbm, inhbm, vmem),
        scratch_shapes=[
            scalar,
            scalar,
            strip,
            strip,
            strip,
            column,
            column,
            pltpu.VMEM((tiles, rows, LANES), f32),
            dma((2, 8)),
            dma((members,)),
            dma((2, 3)),
            dma((2,)),
        ],
        cost_estimate=pl.CostEstimate(
            flops=100 * rows * width, bytes_accessed=16 * rows * width, transcendentals=0
        ),
        compiler_params=pltpu.CompilerParams(vmem_limit_bytes=WHOLE_VMEM),
        name="inner",
    )(betas, labels, accept, start, moment)
    window = pltpu.VMEM((2, tiles, (EDGE + 2) * SUB, LANES), f32)
    count = 4 + len(halos)
    outgoing = pl.pallas_call(
        functools.partial(outer_kernel, per_member, len(halos)),
        grid=(1,),
        out_shape=jax.ShapeDtypeStruct((members, SUB, piece + LANES), f32),
        in_specs=[smem, smem, inhbm, inhbm]
        + [anywhere] * len(halos)
        + [inhbm, inhbm, vmem]
        + [
            pl.BlockSpec((SUB, width), lambda i: (0, 0)),
            pl.BlockSpec((SUB, width), lambda i: (last8, 0)),
            inhbm,
        ],
        out_specs=inhbm,
        scratch_shapes=[
            scalar,
            scalar,
            window,
            window,
            pltpu.VMEM((2, tiles, 2 * SUB, LANES), f32),
            pltpu.VMEM((2, 2, tiles, SUB, LANES), f32),
            pltpu.VMEM((2, SUB, width), f32),
            pltpu.VMEM((SUB, LANES), f32),
            dma((2, 4)),
            dma((2, shares)),
            dma((members,)),
            dma((2,)),
        ],
        input_output_aliases={count + 5: 0},
        name="outer",
    )(betas, swap_pairs, labels, accept, *halos, state, energy, sums, start, start, outgoing)
    received = lax.all_to_all(outgoing, "rep", split_axis=0, concat_axis=0, tiled=True)
    out = strip_of(outgoing[:, :, :piece])
    ordered, notes = pl.pallas_call(
        place_kernel,
        out_shape=(
            jax.ShapeDtypeStruct((members, SUB, piece), f32),
            jax.ShapeDtypeStruct((members, LANES), f32),
        ),
        in_specs=[anywhere, anywhere],
        out_specs=(inhbm, inhbm),
        scratch_shapes=[
            pltpu.SMEM((members, LANES), f32),
            dma((members,)),
            dma((2,)),
        ],
        compiler_params=pltpu.CompilerParams(vmem_limit_bytes=4 << 20),
        name="place",
    )(received, out)
    returned = lax.all_to_all(ordered, "rep", split_axis=0, concat_axis=0, tiled=True)
    passing = notes
    both = notes
    for _ in range(strips - 1):
        passing = lax.ppermute(passing, "dom", forward)
        both = both + passing
    new_label, change, ladder = pl.pallas_call(
        functools.partial(ladder_kernel, strips * rows * width),
        out_shape=(
            jax.ShapeDtypeStruct((1,), jnp.int32),
            jax.ShapeDtypeStruct((1,), f32),
            jax.ShapeDtypeStruct((1,), f32),
        ),
        in_specs=[vmem, vmem],
        out_specs=(smem, smem, smem),
        compiler_params=pltpu.CompilerParams(vmem_limit_bytes=4 << 20),
        name="ladder",
    )(notes, both)
    return (out, strip_of(returned), new_label, change, ladder)


def solution(mesh):
    placed = (P("rep", "dom", None), P("rep", "dom", None), P("rep"), P(), P("rep"), P())
    return jax.shard_map(
        body,
        mesh=mesh,
        in_specs=placed,
        out_specs=(P("rep", "dom", None), P("rep", "dom", None), P("rep"), P("rep"), P("rep")),
        check_vma=False,
    )
```

```python
import functools

import jax
import jax.numpy as jnp
from jax import lax
from jax.experimental import pallas as pl
from jax.experimental.pallas import tpu as pltpu
from jax.sharding import PartitionSpec as P

STEPS = 8
hopping = 0.18
quartic = 0.3
step_size = 0.05

SUB = 8
LANES = 128
EDGE = 3
GROUP = 14
WHOLE_VMEM = 67043328


def lane_index():
    return lax.broadcasted_iota(jnp.int32, (SUB, LANES), 1)


def row_index():
    return lax.broadcasted_iota(jnp.int32, (SUB, LANES), 0)


class Scales:
    def __init__(self, cold):
        self.cold = cold
        squared = jnp.full((SUB, LANES), (4.0 * quartic * step_size * step_size) * cold)
        self.root = jnp.sqrt(squared)
        self.back = 1.0 / self.root
        self.back2 = self.back * self.back
        self.pull = (2.0 * hopping * step_size * step_size) * cold
        self.slope = -((2.0 - 4.0 * quartic) * step_size * step_size) * cold
        self.speed = step_size * self.root
        self.linear = ((1.0 - 2.0 * quartic) * cold) * self.back2
        self.square = (quartic * cold) * (self.back2 * self.back2)
        self.bond = ((2.0 * hopping) * cold) * self.back2
        unspeed = 1.0 / self.speed
        self.kinetic = 0.5 * (unspeed * unspeed)

    def half(self, near, value):
        return 0.5 * (self.pull * near + value * (self.slope - value * value))

    def step(self, near, value, before):
        return value + ((value - before) + (self.pull * near + value * (self.slope - value * value)))

    def site(self, value, ahead):
        squared = value * value
        return squared * (self.linear + self.square * squared) - self.bond * (value * ahead)

    def action(self, total, sites):
        return jnp.sum(total) / self.cold + quartic * sites


def chosen_scalars(labels_ref, betas_ref):
    return betas_ref[labels_ref[0]]


def paired(values, lane):
    half = len(values) // 2
    even = (lane & 1) == 0
    evens = [
        jnp.where(even, values[u], pltpu.roll(values[u + half], 1, 1)) for u in range(half)
    ]
    odds = [
        jnp.where(even, pltpu.roll(values[u], LANES - 1, 1), values[u + half]) for u in range(half)
    ]
    return evens + odds


def unpaired(evens, odds, lane):
    even = (lane & 1) == 0
    return (
        jnp.where(even, evens, pltpu.roll(odds, 1, 1)),
        jnp.where(even, pltpu.roll(evens, LANES - 1, 1), odds),
    )


def beside(load, tiles, lane):
    half = tiles // 2
    final = load(tiles - 1)
    behind = jnp.where(lane == 0, pltpu.roll(final, 1, 1), pltpu.roll(final, 3, 1))
    evens = load(0)
    begin = evens
    ahead = pltpu.roll(evens, LANES - 2, 1)
    for u in range(half):
        odds = load(u + half)
        forward = pltpu.roll(odds, 2, 1)
        left = jnp.where(lane < 2, behind, forward)
        if u + 1 < half:
            following = load(u + 1)
            ahead_next = pltpu.roll(following, LANES - 2, 1)
        else:
            following = begin
            ahead_next = jnp.where(
                lane == LANES - 1, pltpu.roll(begin, LANES - 1, 1), pltpu.roll(begin, LANES - 3, 1)
            )
        right = jnp.where(lane >= LANES - 2, ahead_next, ahead)
        yield u, evens, odds, left, right
        behind, evens, ahead = forward, following, ahead_next


def around(ref, row, tiles, lane):
    half = tiles // 2
    load = lambda t: ref[t, pl.ds(row, SUB), :]
    for u, evens, odds, left, right in beside(load, tiles, lane):
        for t, value, before, after in ((u, evens, left, odds), (u + half, odds, evens, right)):
            below = ref[t, pl.ds(row + 1, SUB), :]
            near = (ref[t, pl.ds(row - 1, SUB), :] + below) + (before + after)
            yield t, value, near, below, after


def advance(before, after, row, tiles, lane, scales, keep=None):
    for t, value, near, _, _ in around(before, row, tiles, lane):
        old = after[t, pl.ds(row, SUB), :]
        new = scales.step(near, value, old)
        if keep is not None:
            new = jnp.where(keep, old, new)
        after[t, pl.ds(row, SUB), :] = new


def pack_kernel(labels_ref, betas_ref, head_ref, tail_ref, head_m_ref, tail_m_ref, out_ref):
    scales = Scales(chosen_scalars(labels_ref, betas_ref))
    lane = lane_index()
    row = row_index()
    tiles = head_ref.shape[1] // LANES
    for side, ref, m_ref in ((0, head_ref, head_m_ref), (1, tail_ref, tail_m_ref)):
        base = 0 if side == 0 else SUB
        inner = SUB - base
        parts = []
        for start in (base, inner):
            parts.append(
                paired(
                    [
                        scales.root * ref[start : start + SUB, pl.ds(t * LANES, LANES)]
                        for t in range(tiles)
                    ],
                    lane,
                )
            )
        values, others = parts
        pushes = paired(
            [scales.speed * m_ref[:, pl.ds(t * LANES, LANES)] for t in range(tiles)], lane
        )
        for u, evens, odds, left, right in beside(lambda t: values[t], tiles, lane):
            half = tiles // 2
            for t, value, near in ((u, evens, left + odds), (u + half, odds, evens + right)):
                up = pltpu.roll(value, 1, 0)
                down = pltpu.roll(value, SUB - 1, 0)
                if side == 0:
                    up = jnp.where(row == 0, 0.0, up)
                    down = jnp.where(row == SUB - 1, pltpu.roll(others[t], SUB - 1, 0), down)
                else:
                    up = jnp.where(row == 0, pltpu.roll(others[t], 1, 0), up)
                    down = jnp.where(row == SUB - 1, 0.0, down)
                push = pushes[t] + scales.half((up + down) + near, value)
                out_ref[side, 0, t] = value
                out_ref[side, 1, t] = value + push


def slots(row_block, tiles, per_member):
    shares = tiles // per_member
    return [(row_block * shares + s, s * per_member * LANES) for s in range(shares)]


def inner_kernel(
    per_member,
    labels_ref,
    betas_ref,
    accept_ref,
    field_hbm,
    momentum_hbm,
    send_hbm,
    state_hbm,
    energy_hbm,
    sums_ref,
    field_ref,
    momentum_ref,
    chosen_ref,
    first,
    second,
    energy,
    in_sem,
    send_sem,
    state_sem,
):
    rows, width = field_ref.shape
    tiles = width // LANES
    blocks = rows // SUB
    chunk = rows // 8

    def load(a, k):
        source, target = ((field_hbm, field_ref), (momentum_hbm, momentum_ref))[a]
        part = pl.ds(pl.multiple_of(k * chunk, chunk), chunk)
        return pltpu.make_async_copy(source.at[part, :], target.at[part, :], in_sem.at[a, k])

    for k in range(8):
        load(0, k).start()
        load(1, k).start()
    scales = Scales(chosen_scalars(labels_ref, betas_ref))
    accepted = accept_ref[0] == 1
    lane = lane_index()
    sub = row_index()
    zero = jnp.zeros((SUB, LANES), jnp.float32)
    for ref in (first, second):
        for t in range(tiles):
            ref[t, 0:SUB, :] = zero
            ref[t, SUB + rows : 2 * SUB + rows, :] = zero

    def bring(k):
        load(0, k).wait()
        for b in range(chunk // SUB):
            row = pl.multiple_of(k * chunk + b * SUB, SUB)
            values = [
                scales.root * field_ref[pl.ds(row, SUB), pl.ds(t * LANES, LANES)] for t in range(tiles)
            ]
            for t, value in enumerate(paired(values, lane)):
                first[t, pl.ds(pl.multiple_of(SUB + row, SUB), SUB), :] = value

    def begin(block, total):
        source = pl.multiple_of(block * SUB, SUB)
        row = pl.multiple_of(SUB + block * SUB, SUB)
        pushes = paired(
            [
                scales.speed * momentum_ref[pl.ds(source, SUB), pl.ds(t * LANES, LANES)]
                for t in range(tiles)
            ],
            lane,
        )
        for t, value, near, below, right in around(first, row, tiles, lane):
            push = pushes[t]
            action = scales.site(value, below + right)
            energy[t, pl.ds(source, SUB), :] = scales.kinetic * (push * push) + action
            total = total + action
            second[t, pl.ds(row, SUB), :] = value + (push + scales.half(near, value))
        return total

    per_turn = 2

    def open_chunk(k, total):
        load(1, k).wait()
        for b in range(chunk // SUB):
            total = begin(k * (chunk // SUB) + b, total)
        return total

    def open_turn(k, total):
        bring(k + 1)
        return open_chunk(k, total)

    bring(0)
    old_action = open_chunk(7, lax.fori_loop(0, 7, open_turn, zero))

    group = GROUP if (blocks - 2) % GROUP == 0 else 1
    for time in range(1, STEPS):
        before, after = (second, first) if time % 2 == 1 else (first, second)
        advance(before, after, SUB, tiles, lane, scales, keep=sub <= time)
        advance(before, after, rows, tiles, lane, scales, keep=sub >= SUB - 1 - time)

        def turn(i, carry, before=before, after=after):
            for b in range(group):
                row = pl.multiple_of(2 * SUB + (i * group + b) * SUB, SUB)
                advance(before, after, row, tiles, lane, scales)
            return carry

        if group == blocks - 2:
            turn(0, 0)
        else:
            lax.fori_loop(0, (blocks - 2) // group, turn, 0)
    last, previous = (first, second) if STEPS % 2 == 0 else (second, first)
    stores = []
    for n, buffer in enumerate((last, previous)):
        for side, row in ((0, SUB), (1, SUB + rows - EDGE * SUB)):
            copy = pltpu.make_async_copy(
                buffer.at[:, pl.ds(row, EDGE * SUB), :], state_hbm.at[side, n], state_sem.at[side, n]
            )
            copy.start()
            stores.append(copy)
    for side, row in ((0, 0), (1, rows - 2 * SUB)):
        copy = pltpu.make_async_copy(
            energy.at[:, pl.ds(row, 2 * SUB), :], energy_hbm.at[side], state_sem.at[side, 2]
        )
        copy.start()
        stores.append(copy)

    def emit(block):
        row = block * SUB
        copies = []
        for member, column in slots(block, tiles, per_member):
            width_here = per_member * LANES
            copies.append(
                pltpu.make_async_copy(
                    chosen_ref.at[pl.ds(row, SUB), pl.ds(column, width_here)],
                    send_hbm.at[member, :, pl.ds(0, width_here)],
                    send_sem.at[member],
                )
            )
        return copies

    def choose(block, evens, odds, u):
        row = pl.multiple_of(block * SUB, SUB)
        for t, value in zip((u, u + tiles // 2), unpaired(evens, odds, lane)):
            cols = pl.ds(t * LANES, LANES)
            kept = field_ref[pl.ds(row, SUB), cols]
            chosen_ref[pl.ds(row, SUB), cols] = jnp.where(accepted, scales.back * value, kept)

    for block in (1, blocks - 2):
        part = pl.ds(SUB + block * SUB, SUB)
        for u in range(tiles // 2):
            choose(block, last[u, part, :], last[u + tiles // 2, part, :], u)
        for copy in emit(block):
            copy.start()
            stores.append(copy)

    def finish(block, carry):
        change, total = carry
        row = pl.multiple_of(SUB + block * SUB, SUB)
        source = pl.multiple_of(block * SUB, SUB)
        for t, value, near, below, right in around(last, row, tiles, lane):
            gone = value - previous[t, pl.ds(row, SUB), :]
            moment = gone + scales.half(near, value)
            action = scales.site(value, below + right)
            total = total + action
            change = change + (
                (scales.kinetic * (moment * moment) + action) - energy[t, pl.ds(source, SUB), :]
            )
            if t < tiles // 2:
                evens = value
            else:
                choose(block, evens, value, t - tiles // 2)
        return change, total

    sums = (zero, zero)
    if (blocks - 4) % per_turn == 0:
        for i in range((blocks - 4) // per_turn):
            sums = lax.fori_loop(
                0,
                1,
                lambda _, carry, i=i: functools.reduce(
                    lambda c, b: finish(2 + i * per_turn + b, c), range(per_turn), carry
                ),
                sums,
            )
            for b in range(per_turn):
                for copy in emit(2 + i * per_turn + b):
                    copy.start()
                    stores.append(copy)
    else:
        for block in range(2, blocks - 2):
            sums = finish(block, sums)
            for copy in emit(block):
                copy.start()
                stores.append(copy)
    sums_ref[0] = sums[0]
    sums_ref[1] = sums[1]
    sums_ref[2] = old_action
    for copy in stores:
        copy.wait()


def outer_kernel(
    per_member,
    halos,
    labels_ref,
    betas_ref,
    accept_ref,
    swap_ref,
    *refs,
):
    halo_refs = refs[:halos]
    (
        state_hbm,
        energy_hbm,
        sums_ref,
        head_ref,
        tail_ref,
        _,
        send_hbm,
        first,
        second,
        energy_ref,
        halo_ref,
        chosen_ref,
        note_ref,
        in_sem,
        send_sem,
        note_sem,
    ) = refs[halos:]
    last, previous = (first, second) if STEPS % 2 == 0 else (second, first)
    loads = []
    for side in range(2):
        own = 2 * SUB if side == 0 else 0
        parts = [
            (state_hbm.at[side, n], buffer.at[side, :, pl.ds(own, EDGE * SUB), :])
            for n, buffer in enumerate((last, previous))
        ]
        parts.append((halo_refs[side % halos].at[1 - side], halo_ref.at[side]))
        parts.append((energy_hbm.at[side], energy_ref.at[side]))
        for n, (source, target) in enumerate(parts):
            copy = pltpu.make_async_copy(source, target, in_sem.at[side, n])
            copy.start()
            loads.append(copy)
    scales = Scales(chosen_scalars(labels_ref, betas_ref))
    label = swap_ref[labels_ref[0]].astype(jnp.float32)
    accepted = accept_ref[0] == 1
    lane = lane_index()
    sub = row_index()
    tiles = first.shape[1]
    members = send_hbm.shape[0]
    blocks = members * per_member // tiles
    zero = jnp.zeros((SUB, LANES), jnp.float32)
    old_extra = zero
    energy_extra = []
    for copy in loads:
        copy.wait()
    for side in range(2):
        edge = SUB if side == 0 else EDGE * SUB
        pad = 0 if side == 0 else (EDGE + 1) * SUB
        mine = 2 * SUB if side == 0 else (EDGE - 1) * SUB
        for t in range(tiles):
            for buffer in (last, previous):
                buffer[side, t, pad : pad + SUB, :] = zero
            start_halo = halo_ref[side, 0, t]
            start_mine = first[side, t, mine : mine + SUB, :]
            if side == 0:
                own_part = jnp.where(sub == SUB - 1, pltpu.roll(start_mine, SUB - 1, 0), 0.0)
                halo_part = jnp.where(sub == 0, pltpu.roll(start_halo, 1, 0), 0.0)
            else:
                own_part = jnp.where(sub == 0, pltpu.roll(start_mine, 1, 0), 0.0)
                halo_part = jnp.where(sub == SUB - 1, pltpu.roll(start_halo, SUB - 1, 0), 0.0)
                missing = -scales.bond * (start_mine * halo_part)
                old_extra = old_extra + missing
                energy_extra.append(missing)
            first[side, t, edge : edge + SUB, :] = start_halo
            second[side, t, edge : edge + SUB, :] = halo_ref[side, 1, t] + (
                0.5 * scales.pull
            ) * own_part
            second[side, t, mine : mine + SUB, :] = (
                second[side, t, mine : mine + SUB, :] + (0.5 * scales.pull) * halo_part
            )
    for time in range(1, STEPS):
        before, after = (second, first) if time % 2 == 1 else (first, second)
        for side in range(2):
            mine = 2 * SUB if side == 0 else (EDGE - 1) * SUB
            edge = SUB if side == 0 else EDGE * SUB
            keep = sub > time if side == 0 else sub < SUB - 1 - time
            advance(before.at[side], after.at[side], edge, tiles, lane, scales)
            advance(before.at[side], after.at[side], mine, tiles, lane, scales, keep=keep)
    change = sums_ref[0]
    total = sums_ref[1]
    copies = []
    for side in range(2):
        own = 2 * SUB if side == 0 else 0
        for b in range(2):
            place = b if side == 0 else EDGE - 2 + b
            row = own + place * SUB
            outermost = (side == 0 and b == 0) or (side == 1 and b == 1)
            for t, value, near, below, right in around(last.at[side], row, tiles, lane):
                gone = value - previous[side, t, pl.ds(row, SUB), :]
                moment = gone + scales.half(near, value)
                action = scales.site(value, below + right)
                total = total + action
                old = energy_ref[side, t, b * SUB : (b + 1) * SUB, :]
                if side == 1 and outermost:
                    old = old + energy_extra[t]
                change = change + ((scales.kinetic * (moment * moment) + action) - old)
                if outermost and t < tiles // 2:
                    evens = value
                elif outermost:
                    u = t - tiles // 2
                    for c, part in zip((u, t), unpaired(evens, value, lane)):
                        cols = pl.ds(c * LANES, LANES)
                        kept = head_ref[:, cols] if side == 0 else tail_ref[:, cols]
                        chosen_ref[side, :, cols] = jnp.where(accepted, scales.back * part, kept)
        block = 0 if side == 0 else blocks - 1
        for n, (member, column) in enumerate(slots(block, tiles, per_member)):
            size = per_member * LANES
            copies.append(
                pltpu.make_async_copy(
                    chosen_ref.at[side, :, pl.ds(column, size)],
                    send_hbm.at[member, :, pl.ds(0, size)],
                    send_sem.at[side, n],
                )
            )
    for copy in copies:
        copy.start()
    old_action = sums_ref[2] + old_extra
    sites = blocks * SUB * tiles * LANES
    action = scales.action(jnp.where(accepted, total, old_action), sites)
    change = jnp.sum(change)
    note_ref[...] = jnp.where(
        lane == 0, label, jnp.where(lane == 1, action, jnp.where(lane == 2, change, 0.0))
    )
    for member in range(members):
        copy = pltpu.make_async_copy(
            note_ref,
            send_hbm.at[member, :, pl.ds(per_member * LANES, LANES)],
            note_sem.at[member],
        )
        copy.start()
        copies.append(copy)
    for copy in copies:
        copy.wait()


def place_kernel(got_ref, _, out_hbm, notes_hbm, labels_ref, sem, note_sem):
    members, _, width = out_hbm.shape
    notes = got_ref.at[:, 0, pl.ds(width, LANES)]
    fetch = pltpu.make_async_copy(notes, labels_ref, note_sem.at[0])
    fetch.start()
    keep = pltpu.make_async_copy(notes, notes_hbm, note_sem.at[1])
    keep.start()
    fetch.wait()
    copies = []
    for r in range(members):
        slot = labels_ref[r, 0].astype(jnp.int32)
        copy = pltpu.make_async_copy(got_ref.at[r, :, pl.ds(0, width)], out_hbm.at[slot], sem.at[r])
        copy.start()
        copies.append(copy)
    keep.wait()
    for copy in copies:
        copy.wait()


def ladder_kernel(sites, notes_ref, sums_ref, label_ref, change_ref, ladder_ref):
    me = lax.axis_index("rep")
    notes = notes_ref[...]
    sums = sums_ref[...]
    lane = lax.broadcasted_iota(jnp.int32, notes.shape, 1)
    replica = lax.broadcasted_iota(jnp.int32, notes.shape, 0)
    held = (lane == 0) & (notes.astype(jnp.int32) == me)
    actions = pltpu.roll(sums, LANES - 1, 1)
    ladder_ref[0] = jnp.sum(jnp.where(held, actions, 0.0)) / sites
    own = replica == me
    label_ref[0] = jnp.sum(jnp.where(own & (lane == 0), notes, 0.0)).astype(jnp.int32)
    change_ref[0] = jnp.sum(jnp.where(own & (lane == 2), sums, 0.0))


def body(field, momentum, labels, betas, accept, swap_pairs):
    rows = field.shape[1]
    width = field.shape[2]
    members = lax.axis_size("rep")
    strips = lax.axis_size("dom")
    tiles = width // LANES
    per_member = (rows // SUB) * tiles // members
    shares = tiles // per_member
    piece = per_member * LANES
    f32 = jnp.float32
    start = field[0]
    moment = momentum[0]
    smem = pl.BlockSpec(memory_space=pltpu.SMEM)
    vmem = pl.BlockSpec(memory_space=pltpu.VMEM)
    anywhere = pl.BlockSpec(memory_space=pl.ANY)
    inhbm = pl.BlockSpec(memory_space=pltpu.HBM)
    dma = pltpu.SemaphoreType.DMA
    last16 = rows // (2 * SUB) - 1
    last8 = rows // SUB - 1
    edges = pl.pallas_call(
        pack_kernel,
        grid=(1,),
        out_shape=jax.ShapeDtypeStruct((2, 2, tiles, SUB, LANES), f32),
        in_specs=[
            smem,
            smem,
            pl.BlockSpec((2 * SUB, width), lambda i: (0, 0)),
            pl.BlockSpec((2 * SUB, width), lambda i: (last16, 0)),
            pl.BlockSpec((SUB, width), lambda i: (0, 0)),
            pl.BlockSpec((SUB, width), lambda i: (last8, 0)),
        ],
        out_specs=pl.BlockSpec((2, 2, tiles, SUB, LANES), lambda i: (0, 0, 0, 0, 0)),
        name="pack",
    )(labels, betas, start, start, moment, moment)
    forward = [(i, (i + 1) % strips) for i in range(strips)]
    backward = [((i + 1) % strips, i) for i in range(strips)]
    halos = (lax.ppermute(edges, "dom", forward),)
    if strips > 2:
        halos = halos + (lax.ppermute(edges, "dom", backward),)

    def strip_of(pieces):
        grouped = pieces.reshape(rows // SUB, shares, SUB, piece).transpose(0, 2, 1, 3)
        return grouped.reshape(1, rows, width)

    column = pltpu.VMEM((tiles, rows + 2 * SUB, LANES), f32)
    strip = pltpu.VMEM((rows, width), f32)
    outgoing, state, energy, sums = pl.pallas_call(
        functools.partial(inner_kernel, per_member),
        out_shape=(
            jax.ShapeDtypeStruct((members, SUB, piece + LANES), f32),
            jax.ShapeDtypeStruct((2, 2, tiles, EDGE * SUB, LANES), f32),
            jax.ShapeDtypeStruct((2, tiles, 2 * SUB, LANES), f32),
            jax.ShapeDtypeStruct((3, SUB, LANES), f32),
        ),
        in_specs=[smem, smem, smem, inhbm, inhbm],
        out_specs=(inhbm, inhbm, inhbm, vmem),
        scratch_shapes=[
            strip,
            strip,
            strip,
            column,
            column,
            pltpu.VMEM((tiles, rows, LANES), f32),
            dma((2, 8)),
            dma((members,)),
            dma((2, 3)),
        ],
        cost_estimate=pl.CostEstimate(
            flops=100 * rows * width, bytes_accessed=16 * rows * width, transcendentals=0
        ),
        compiler_params=pltpu.CompilerParams(vmem_limit_bytes=WHOLE_VMEM),
        name="inner",
    )(labels, betas, accept, start, moment)
    window = pltpu.VMEM((2, tiles, (EDGE + 2) * SUB, LANES), f32)
    count = 4 + len(halos)
    outgoing = pl.pallas_call(
        functools.partial(outer_kernel, per_member, len(halos)),
        grid=(1,),
        out_shape=jax.ShapeDtypeStruct((members, SUB, piece + LANES), f32),
        in_specs=[smem] * 4
        + [anywhere] * len(halos)
        + [inhbm, inhbm, vmem]
        + [
            pl.BlockSpec((SUB, width), lambda i: (0, 0)),
            pl.BlockSpec((SUB, width), lambda i: (last8, 0)),
            inhbm,
        ],
        out_specs=inhbm,
        scratch_shapes=[
            window,
            window,
            pltpu.VMEM((2, tiles, 2 * SUB, LANES), f32),
            pltpu.VMEM((2, 2, tiles, SUB, LANES), f32),
            pltpu.VMEM((2, SUB, width), f32),
            pltpu.VMEM((SUB, LANES), f32),
            dma((2, 4)),
            dma((2, shares)),
            dma((members,)),
        ],
        input_output_aliases={count + 5: 0},
        name="outer",
    )(labels, betas, accept, swap_pairs, *halos, state, energy, sums, start, start, outgoing)
    received = lax.all_to_all(outgoing, "rep", split_axis=0, concat_axis=0, tiled=True)
    out = strip_of(outgoing[:, :, :piece])
    ordered, notes = pl.pallas_call(
        place_kernel,
        out_shape=(
            jax.ShapeDtypeStruct((members, SUB, piece), f32),
            jax.ShapeDtypeStruct((members, LANES), f32),
        ),
        in_specs=[anywhere, anywhere],
        out_specs=(inhbm, inhbm),
        scratch_shapes=[
            pltpu.SMEM((members, LANES), f32),
            dma((members,)),
            dma((2,)),
        ],
        compiler_params=pltpu.CompilerParams(vmem_limit_bytes=4 << 20),
        name="place",
    )(received, out)
    returned = lax.all_to_all(ordered, "rep", split_axis=0, concat_axis=0, tiled=True)
    passing = notes
    both = notes
    for _ in range(strips - 1):
        passing = lax.ppermute(passing, "dom", forward)
        both = both + passing
    new_label, change, ladder = pl.pallas_call(
        functools.partial(ladder_kernel, strips * rows * width),
        out_shape=(
            jax.ShapeDtypeStruct((1,), jnp.int32),
            jax.ShapeDtypeStruct((1,), f32),
            jax.ShapeDtypeStruct((1,), f32),
        ),
        in_specs=[vmem, vmem],
        out_specs=(smem, smem, smem),
        compiler_params=pltpu.CompilerParams(vmem_limit_bytes=4 << 20),
        name="ladder",
    )(notes, both)
    return (out, strip_of(returned), new_label, change, ladder)


def solution(mesh):
    placed = (P("rep", "dom", None), P("rep", "dom", None), P("rep"), P(), P("rep"), P())
    return jax.shard_map(
        body,
        mesh=mesh,
        in_specs=placed,
        out_specs=(P("rep", "dom", None), P("rep", "dom", None), P("rep"), P("rep"), P("rep")),
        check_vma=False,
    )
```

```python
import functools

import jax
import jax.numpy as jnp
from jax import lax
from jax.experimental import pallas as pl
from jax.experimental.pallas import tpu as pltpu
from jax.sharding import PartitionSpec as P

STEPS = 8
hopping = 0.18
quartic = 0.3
step_size = 0.05

SUB = 8
LANES = 128
EDGE = 3
GROUP = 14
WHOLE_VMEM = 67043328


def lane_index():
    return lax.broadcasted_iota(jnp.int32, (SUB, LANES), 1)


def row_index():
    return lax.broadcasted_iota(jnp.int32, (SUB, LANES), 0)


class Scales:
    def __init__(self, cold):
        self.cold = cold
        squared = jnp.full((SUB, LANES), (4.0 * quartic * step_size * step_size) * cold)
        self.root = jnp.sqrt(squared)
        self.back = 1.0 / self.root
        self.back2 = self.back * self.back
        self.pull = (2.0 * hopping * step_size * step_size) * cold
        self.slope = -((2.0 - 4.0 * quartic) * step_size * step_size) * cold
        self.speed = step_size * self.root
        self.linear = ((1.0 - 2.0 * quartic) * cold) * self.back2
        self.square = (quartic * cold) * (self.back2 * self.back2)
        self.bond = ((2.0 * hopping) * cold) * self.back2
        unspeed = 1.0 / self.speed
        self.kinetic = 0.5 * (unspeed * unspeed)

    def half(self, near, value):
        return 0.5 * (self.pull * near + value * (self.slope - value * value))

    def step(self, near, value, before):
        return value + ((value - before) + (self.pull * near + value * (self.slope - value * value)))

    def site(self, value, ahead):
        squared = value * value
        return squared * (self.linear + self.square * squared) - self.bond * (value * ahead)

    def action(self, total, sites):
        return jnp.sum(total) / self.cold + quartic * sites


def chosen_scalars(labels_ref, betas_ref):
    return betas_ref[labels_ref[0]]


def paired(values, lane):
    half = len(values) // 2
    even = (lane & 1) == 0
    evens = [
        jnp.where(even, values[u], pltpu.roll(values[u + half], 1, 1)) for u in range(half)
    ]
    odds = [
        jnp.where(even, pltpu.roll(values[u], LANES - 1, 1), values[u + half]) for u in range(half)
    ]
    return evens + odds


def unpaired(evens, odds, lane):
    even = (lane & 1) == 0
    return (
        jnp.where(even, evens, pltpu.roll(odds, 1, 1)),
        jnp.where(even, pltpu.roll(evens, LANES - 1, 1), odds),
    )


def beside(load, tiles, lane):
    half = tiles // 2
    final = load(tiles - 1)
    behind = jnp.where(lane == 0, pltpu.roll(final, 1, 1), pltpu.roll(final, 3, 1))
    evens = load(0)
    begin = evens
    ahead = pltpu.roll(evens, LANES - 2, 1)
    for u in range(half):
        odds = load(u + half)
        forward = pltpu.roll(odds, 2, 1)
        left = jnp.where(lane < 2, behind, forward)
        if u + 1 < half:
            following = load(u + 1)
            ahead_next = pltpu.roll(following, LANES - 2, 1)
        else:
            following = begin
            ahead_next = jnp.where(
                lane == LANES - 1, pltpu.roll(begin, LANES - 1, 1), pltpu.roll(begin, LANES - 3, 1)
            )
        right = jnp.where(lane >= LANES - 2, ahead_next, ahead)
        yield u, evens, odds, left, right
        behind, evens, ahead = forward, following, ahead_next


def around(ref, row, tiles, lane):
    half = tiles // 2
    load = lambda t: ref[t, pl.ds(row, SUB), :]
    for u, evens, odds, left, right in beside(load, tiles, lane):
        for t, value, before, after in ((u, evens, left, odds), (u + half, odds, evens, right)):
            below = ref[t, pl.ds(row + 1, SUB), :]
            near = (ref[t, pl.ds(row - 1, SUB), :] + below) + (before + after)
            yield t, value, near, below, after


def advance(before, after, row, tiles, lane, scales, keep=None):
    for t, value, near, _, _ in around(before, row, tiles, lane):
        old = after[t, pl.ds(row, SUB), :]
        new = scales.step(near, value, old)
        if keep is not None:
            new = jnp.where(keep, old, new)
        after[t, pl.ds(row, SUB), :] = new


def pack_kernel(labels_ref, betas_ref, head_ref, tail_ref, head_m_ref, tail_m_ref, out_ref):
    scales = Scales(chosen_scalars(labels_ref, betas_ref))
    lane = lane_index()
    row = row_index()
    tiles = head_ref.shape[1] // LANES
    for side, ref, m_ref in ((0, head_ref, head_m_ref), (1, tail_ref, tail_m_ref)):
        base = 0 if side == 0 else SUB
        inner = SUB - base
        parts = []
        for start in (base, inner):
            parts.append(
                paired(
                    [
                        scales.root * ref[start : start + SUB, pl.ds(t * LANES, LANES)]
                        for t in range(tiles)
                    ],
                    lane,
                )
            )
        values, others = parts
        pushes = paired(
            [scales.speed * m_ref[:, pl.ds(t * LANES, LANES)] for t in range(tiles)], lane
        )
        for u, evens, odds, left, right in beside(lambda t: values[t], tiles, lane):
            half = tiles // 2
            for t, value, near in ((u, evens, left + odds), (u + half, odds, evens + right)):
                up = pltpu.roll(value, 1, 0)
                down = pltpu.roll(value, SUB - 1, 0)
                if side == 0:
                    up = jnp.where(row == 0, 0.0, up)
                    down = jnp.where(row == SUB - 1, pltpu.roll(others[t], SUB - 1, 0), down)
                else:
                    up = jnp.where(row == 0, pltpu.roll(others[t], 1, 0), up)
                    down = jnp.where(row == SUB - 1, 0.0, down)
                push = pushes[t] + scales.half((up + down) + near, value)
                out_ref[side, 0, t] = value
                out_ref[side, 1, t] = value + push


def slots(row_block, tiles, per_member):
    shares = tiles // per_member
    return [(row_block * shares + s, s * per_member * LANES) for s in range(shares)]


def inner_kernel(
    per_member,
    labels_ref,
    betas_ref,
    accept_ref,
    field_hbm,
    momentum_hbm,
    send_hbm,
    state_hbm,
    energy_hbm,
    sums_ref,
    field_ref,
    momentum_ref,
    chosen_ref,
    first,
    second,
    energy,
    in_sem,
    send_sem,
    state_sem,
):
    rows, width = field_ref.shape
    tiles = width // LANES
    blocks = rows // SUB
    chunks = 4
    chunk = rows // chunks

    def load(a, k):
        source, target = ((field_hbm, field_ref), (momentum_hbm, momentum_ref))[a]
        part = pl.ds(pl.multiple_of(k * chunk, chunk), chunk)
        return pltpu.make_async_copy(source.at[part, :], target.at[part, :], in_sem.at[a, k])

    for k in range(chunks):
        load(0, k).start()
        load(1, k).start()
    scales = Scales(chosen_scalars(labels_ref, betas_ref))
    accepted = accept_ref[0] == 1
    lane = lane_index()
    sub = row_index()
    zero = jnp.zeros((SUB, LANES), jnp.float32)
    for ref in (first, second):
        for t in range(tiles):
            ref[t, 0:SUB, :] = zero
            ref[t, SUB + rows : 2 * SUB + rows, :] = zero

    def bring(k):
        load(0, k).wait()
        for b in range(chunk // SUB):
            row = pl.multiple_of(k * chunk + b * SUB, SUB)
            values = [
                scales.root * field_ref[pl.ds(row, SUB), pl.ds(t * LANES, LANES)] for t in range(tiles)
            ]
            for t, value in enumerate(paired(values, lane)):
                first[t, pl.ds(pl.multiple_of(SUB + row, SUB), SUB), :] = value

    def begin(block, total):
        source = pl.multiple_of(block * SUB, SUB)
        row = pl.multiple_of(SUB + block * SUB, SUB)
        pushes = paired(
            [
                scales.speed * momentum_ref[pl.ds(source, SUB), pl.ds(t * LANES, LANES)]
                for t in range(tiles)
            ],
            lane,
        )
        for t, value, near, below, right in around(first, row, tiles, lane):
            push = pushes[t]
            action = scales.site(value, below + right)
            energy[t, pl.ds(source, SUB), :] = scales.kinetic * (push * push) + action
            total = total + action
            second[t, pl.ds(row, SUB), :] = value + (push + scales.half(near, value))
        return total

    per_turn = 2

    def open_chunk(k, total):
        load(1, k).wait()
        for b in range(chunk // SUB):
            total = begin(k * (chunk // SUB) + b, total)
        return total

    def open_turn(k, total):
        bring(k + 1)
        return open_chunk(k, total)

    bring(0)
    old_action = open_chunk(chunks - 1, lax.fori_loop(0, chunks - 1, open_turn, zero))

    group = GROUP if (blocks - 2) % GROUP == 0 else 1
    for time in range(1, STEPS):
        before, after = (second, first) if time % 2 == 1 else (first, second)
        advance(before, after, SUB, tiles, lane, scales, keep=sub <= time)
        advance(before, after, rows, tiles, lane, scales, keep=sub >= SUB - 1 - time)

        def turn(i, carry, before=before, after=after):
            for b in range(group):
                row = pl.multiple_of(2 * SUB + (i * group + b) * SUB, SUB)
                advance(before, after, row, tiles, lane, scales)
            return carry

        if group == blocks - 2:
            turn(0, 0)
        else:
            lax.fori_loop(0, (blocks - 2) // group, turn, 0)
    last, previous = (first, second) if STEPS % 2 == 0 else (second, first)
    stores = []
    for n, buffer in enumerate((last, previous)):
        for side, row in ((0, SUB), (1, SUB + rows - EDGE * SUB)):
            copy = pltpu.make_async_copy(
                buffer.at[:, pl.ds(row, EDGE * SUB), :], state_hbm.at[side, n], state_sem.at[side, n]
            )
            copy.start()
            stores.append(copy)
    for side, row in ((0, 0), (1, rows - 2 * SUB)):
        copy = pltpu.make_async_copy(
            energy.at[:, pl.ds(row, 2 * SUB), :], energy_hbm.at[side], state_sem.at[side, 2]
        )
        copy.start()
        stores.append(copy)

    def emit(block):
        row = block * SUB
        copies = []
        for member, column in slots(block, tiles, per_member):
            width_here = per_member * LANES
            copies.append(
                pltpu.make_async_copy(
                    chosen_ref.at[pl.ds(row, SUB), pl.ds(column, width_here)],
                    send_hbm.at[member, :, pl.ds(0, width_here)],
                    send_sem.at[member],
                )
            )
        return copies

    def choose(block, evens, odds, u):
        row = pl.multiple_of(block * SUB, SUB)
        for t, value in zip((u, u + tiles // 2), unpaired(evens, odds, lane)):
            cols = pl.ds(t * LANES, LANES)
            kept = field_ref[pl.ds(row, SUB), cols]
            chosen_ref[pl.ds(row, SUB), cols] = jnp.where(accepted, scales.back * value, kept)

    for block in range(1, blocks - 1):
        part = pl.ds(SUB + block * SUB, SUB)
        for u in range(tiles // 2):
            choose(block, last[u, part, :], last[u + tiles // 2, part, :], u)
        for copy in emit(block):
            copy.start()
            stores.append(copy)

    def finish(block, carry):
        change, total = carry
        row = pl.multiple_of(SUB + block * SUB, SUB)
        source = pl.multiple_of(block * SUB, SUB)
        for t, value, near, below, right in around(last, row, tiles, lane):
            gone = value - previous[t, pl.ds(row, SUB), :]
            moment = gone + scales.half(near, value)
            action = scales.site(value, below + right)
            total = total + action
            change = change + (
                (scales.kinetic * (moment * moment) + action) - energy[t, pl.ds(source, SUB), :]
            )
        return change, total

    turns = 4 if (blocks - 4) % 4 == 0 else 1

    def finish_turn(i, carry):
        for b in range(turns):
            carry = finish(2 + i * turns + b, carry)
        return carry

    sums = lax.fori_loop(0, (blocks - 4) // turns, finish_turn, (zero, zero))
    sums_ref[0] = sums[0]
    sums_ref[1] = sums[1]
    sums_ref[2] = old_action
    for copy in stores:
        copy.wait()


def outer_kernel(
    per_member,
    halos,
    labels_ref,
    betas_ref,
    accept_ref,
    swap_ref,
    *refs,
):
    halo_refs = refs[:halos]
    (
        state_hbm,
        energy_hbm,
        sums_ref,
        head_ref,
        tail_ref,
        _,
        send_hbm,
        first,
        second,
        energy_ref,
        halo_ref,
        chosen_ref,
        note_ref,
        in_sem,
        send_sem,
        note_sem,
    ) = refs[halos:]
    last, previous = (first, second) if STEPS % 2 == 0 else (second, first)
    loads = []
    for side in range(2):
        own = 2 * SUB if side == 0 else 0
        parts = [
            (state_hbm.at[side, n], buffer.at[side, :, pl.ds(own, EDGE * SUB), :])
            for n, buffer in enumerate((last, previous))
        ]
        parts.append((halo_refs[side % halos].at[1 - side], halo_ref.at[side]))
        parts.append((energy_hbm.at[side], energy_ref.at[side]))
        for n, (source, target) in enumerate(parts):
            copy = pltpu.make_async_copy(source, target, in_sem.at[side, n])
            copy.start()
            loads.append(copy)
    scales = Scales(chosen_scalars(labels_ref, betas_ref))
    label = swap_ref[labels_ref[0]].astype(jnp.float32)
    accepted = accept_ref[0] == 1
    lane = lane_index()
    sub = row_index()
    tiles = first.shape[1]
    members = send_hbm.shape[0]
    blocks = members * per_member // tiles
    zero = jnp.zeros((SUB, LANES), jnp.float32)
    old_extra = zero
    energy_extra = []
    for side in range(2):
        for copy in loads[4 * side : 4 * side + 3]:
            copy.wait()
        edge = SUB if side == 0 else EDGE * SUB
        pad = 0 if side == 0 else (EDGE + 1) * SUB
        mine = 2 * SUB if side == 0 else (EDGE - 1) * SUB
        for t in range(tiles):
            for buffer in (last, previous):
                buffer[side, t, pad : pad + SUB, :] = zero
            start_halo = halo_ref[side, 0, t]
            start_mine = first[side, t, mine : mine + SUB, :]
            if side == 0:
                own_part = jnp.where(sub == SUB - 1, pltpu.roll(start_mine, SUB - 1, 0), 0.0)
                halo_part = jnp.where(sub == 0, pltpu.roll(start_halo, 1, 0), 0.0)
            else:
                own_part = jnp.where(sub == 0, pltpu.roll(start_mine, 1, 0), 0.0)
                halo_part = jnp.where(sub == SUB - 1, pltpu.roll(start_halo, SUB - 1, 0), 0.0)
                missing = -scales.bond * (start_mine * halo_part)
                old_extra = old_extra + missing
                energy_extra.append(missing)
            first[side, t, edge : edge + SUB, :] = start_halo
            second[side, t, edge : edge + SUB, :] = halo_ref[side, 1, t] + (
                0.5 * scales.pull
            ) * own_part
            second[side, t, mine : mine + SUB, :] = (
                second[side, t, mine : mine + SUB, :] + (0.5 * scales.pull) * halo_part
            )
    for time in range(1, STEPS):
        before, after = (second, first) if time % 2 == 1 else (first, second)
        for side in range(2):
            mine = 2 * SUB if side == 0 else (EDGE - 1) * SUB
            edge = SUB if side == 0 else EDGE * SUB
            keep = sub > time if side == 0 else sub < SUB - 1 - time
            advance(before.at[side], after.at[side], edge, tiles, lane, scales)
            advance(before.at[side], after.at[side], mine, tiles, lane, scales, keep=keep)
    copies = []
    for side in range(2):
        mine = 2 * SUB if side == 0 else (EDGE - 1) * SUB
        block = 0 if side == 0 else blocks - 1
        kept_ref = head_ref if side == 0 else tail_ref
        for u in range(tiles // 2):
            pair = (last[side, t, mine : mine + SUB, :] for t in (u, u + tiles // 2))
            for c, part in zip((u, u + tiles // 2), unpaired(*pair, lane)):
                cols = pl.ds(c * LANES, LANES)
                chosen_ref[side, :, cols] = jnp.where(
                    accepted, scales.back * part, kept_ref[:, cols]
                )
        for n, (member, column) in enumerate(slots(block, tiles, per_member)):
            size = per_member * LANES
            copy = pltpu.make_async_copy(
                chosen_ref.at[side, :, pl.ds(column, size)],
                send_hbm.at[member, :, pl.ds(0, size)],
                send_sem.at[side, n],
            )
            copy.start()
            copies.append(copy)
    change = sums_ref[0]
    total = sums_ref[1]
    for side in range(2):
        own = 2 * SUB if side == 0 else 0
        loads[4 * side + 3].wait()
        for b in range(2):
            place = b if side == 0 else EDGE - 2 + b
            row = own + place * SUB
            for t, value, near, below, right in around(last.at[side], row, tiles, lane):
                gone = value - previous[side, t, pl.ds(row, SUB), :]
                moment = gone + scales.half(near, value)
                action = scales.site(value, below + right)
                total = total + action
                old = energy_ref[side, t, b * SUB : (b + 1) * SUB, :]
                if side == 1 and b == 1:
                    old = old + energy_extra[t]
                change = change + ((scales.kinetic * (moment * moment) + action) - old)
    old_action = sums_ref[2] + old_extra
    sites = blocks * SUB * tiles * LANES
    action = scales.action(jnp.where(accepted, total, old_action), sites)
    change = jnp.sum(change)
    note_ref[...] = jnp.where(
        lane == 0, label, jnp.where(lane == 1, action, jnp.where(lane == 2, change, 0.0))
    )
    for member in range(members):
        copy = pltpu.make_async_copy(
            note_ref,
            send_hbm.at[member, :, pl.ds(per_member * LANES, LANES)],
            note_sem.at[member],
        )
        copy.start()
        copies.append(copy)
    for copy in copies:
        copy.wait()


def place_kernel(got_ref, _, out_hbm, notes_hbm, labels_ref, sem, note_sem):
    members, _, width = out_hbm.shape
    notes = got_ref.at[:, 0, pl.ds(width, LANES)]
    fetch = pltpu.make_async_copy(notes, labels_ref, note_sem.at[0])
    fetch.start()
    keep = pltpu.make_async_copy(notes, notes_hbm, note_sem.at[1])
    keep.start()
    fetch.wait()
    copies = []
    for r in range(members):
        slot = labels_ref[r, 0].astype(jnp.int32)
        copy = pltpu.make_async_copy(got_ref.at[r, :, pl.ds(0, width)], out_hbm.at[slot], sem.at[r])
        copy.start()
        copies.append(copy)
    keep.wait()
    for copy in copies:
        copy.wait()


def ladder_kernel(sites, notes_ref, sums_ref, label_ref, change_ref, ladder_ref):
    me = lax.axis_index("rep")
    notes = notes_ref[...]
    sums = sums_ref[...]
    lane = lax.broadcasted_iota(jnp.int32, notes.shape, 1)
    replica = lax.broadcasted_iota(jnp.int32, notes.shape, 0)
    held = (lane == 0) & (notes.astype(jnp.int32) == me)
    actions = pltpu.roll(sums, LANES - 1, 1)
    ladder_ref[0] = jnp.sum(jnp.where(held, actions, 0.0)) / sites
    own = replica == me
    label_ref[0] = jnp.sum(jnp.where(own & (lane == 0), notes, 0.0)).astype(jnp.int32)
    change_ref[0] = jnp.sum(jnp.where(own & (lane == 2), sums, 0.0))


def body(field, momentum, labels, betas, accept, swap_pairs):
    rows = field.shape[1]
    width = field.shape[2]
    members = lax.axis_size("rep")
    strips = lax.axis_size("dom")
    tiles = width // LANES
    per_member = (rows // SUB) * tiles // members
    shares = tiles // per_member
    piece = per_member * LANES
    f32 = jnp.float32
    start = field[0]
    moment = momentum[0]
    smem = pl.BlockSpec(memory_space=pltpu.SMEM)
    vmem = pl.BlockSpec(memory_space=pltpu.VMEM)
    anywhere = pl.BlockSpec(memory_space=pl.ANY)
    inhbm = pl.BlockSpec(memory_space=pltpu.HBM)
    dma = pltpu.SemaphoreType.DMA
    last16 = rows // (2 * SUB) - 1
    last8 = rows // SUB - 1
    edges = pl.pallas_call(
        pack_kernel,
        grid=(1,),
        out_shape=jax.ShapeDtypeStruct((2, 2, tiles, SUB, LANES), f32),
        in_specs=[
            smem,
            smem,
            pl.BlockSpec((2 * SUB, width), lambda i: (0, 0)),
            pl.BlockSpec((2 * SUB, width), lambda i: (last16, 0)),
            pl.BlockSpec((SUB, width), lambda i: (0, 0)),
            pl.BlockSpec((SUB, width), lambda i: (last8, 0)),
        ],
        out_specs=pl.BlockSpec((2, 2, tiles, SUB, LANES), lambda i: (0, 0, 0, 0, 0)),
        name="pack",
    )(labels, betas, start, start, moment, moment)
    forward = [(i, (i + 1) % strips) for i in range(strips)]
    backward = [((i + 1) % strips, i) for i in range(strips)]
    halos = (lax.ppermute(edges, "dom", forward),)
    if strips > 2:
        halos = halos + (lax.ppermute(edges, "dom", backward),)

    def strip_of(pieces):
        grouped = pieces.reshape(rows // SUB, shares, SUB, piece).transpose(0, 2, 1, 3)
        return grouped.reshape(1, rows, width)

    column = pltpu.VMEM((tiles, rows + 2 * SUB, LANES), f32)
    strip = pltpu.VMEM((rows, width), f32)
    outgoing, state, energy, sums = pl.pallas_call(
        functools.partial(inner_kernel, per_member),
        out_shape=(
            jax.ShapeDtypeStruct((members, SUB, piece + LANES), f32),
            jax.ShapeDtypeStruct((2, 2, tiles, EDGE * SUB, LANES), f32),
            jax.ShapeDtypeStruct((2, tiles, 2 * SUB, LANES), f32),
            jax.ShapeDtypeStruct((3, SUB, LANES), f32),
        ),
        in_specs=[smem, smem, smem, inhbm, inhbm],
        out_specs=(inhbm, inhbm, inhbm, vmem),
        scratch_shapes=[
            strip,
            strip,
            strip,
            column,
            column,
            pltpu.VMEM((tiles, rows, LANES), f32),
            dma((2, 4)),
            dma((members,)),
            dma((2, 3)),
        ],
        cost_estimate=pl.CostEstimate(
            flops=100 * rows * width, bytes_accessed=16 * rows * width, transcendentals=0
        ),
        compiler_params=pltpu.CompilerParams(vmem_limit_bytes=WHOLE_VMEM),
        name="inner",
    )(labels, betas, accept, start, moment)
    window = pltpu.VMEM((2, tiles, (EDGE + 2) * SUB, LANES), f32)
    count = 4 + len(halos)
    outgoing = pl.pallas_call(
        functools.partial(outer_kernel, per_member, len(halos)),
        grid=(1,),
        out_shape=jax.ShapeDtypeStruct((members, SUB, piece + LANES), f32),
        in_specs=[smem] * 4
        + [anywhere] * len(halos)
        + [inhbm, inhbm, vmem]
        + [
            pl.BlockSpec((SUB, width), lambda i: (0, 0)),
            pl.BlockSpec((SUB, width), lambda i: (last8, 0)),
            inhbm,
        ],
        out_specs=inhbm,
        scratch_shapes=[
            window,
            window,
            pltpu.VMEM((2, tiles, 2 * SUB, LANES), f32),
            pltpu.VMEM((2, 2, tiles, SUB, LANES), f32),
            pltpu.VMEM((2, SUB, width), f32),
            pltpu.VMEM((SUB, LANES), f32),
            dma((2, 4)),
            dma((2, shares)),
            dma((members,)),
        ],
        input_output_aliases={count + 5: 0},
        name="outer",
    )(labels, betas, accept, swap_pairs, *halos, state, energy, sums, start, start, outgoing)
    received = lax.all_to_all(outgoing, "rep", split_axis=0, concat_axis=0, tiled=True)
    out = strip_of(outgoing[:, :, :piece])
    ordered, notes = pl.pallas_call(
        place_kernel,
        out_shape=(
            jax.ShapeDtypeStruct((members, SUB, piece), f32),
            jax.ShapeDtypeStruct((members, LANES), f32),
        ),
        in_specs=[anywhere, anywhere],
        out_specs=(inhbm, inhbm),
        scratch_shapes=[
            pltpu.SMEM((members, LANES), f32),
            dma((members,)),
            dma((2,)),
        ],
        compiler_params=pltpu.CompilerParams(vmem_limit_bytes=4 << 20),
        name="place",
    )(received, out)
    returned = lax.all_to_all(ordered, "rep", split_axis=0, concat_axis=0, tiled=True)
    passing = notes
    both = notes
    for _ in range(strips - 1):
        passing = lax.ppermute(passing, "dom", forward)
        both = both + passing
    new_label, change, ladder = pl.pallas_call(
        functools.partial(ladder_kernel, strips * rows * width),
        out_shape=(
            jax.ShapeDtypeStruct((1,), jnp.int32),
            jax.ShapeDtypeStruct((1,), f32),
            jax.ShapeDtypeStruct((1,), f32),
        ),
        in_specs=[vmem, vmem],
        out_specs=(smem, smem, smem),
        compiler_params=pltpu.CompilerParams(vmem_limit_bytes=4 << 20),
        name="ladder",
    )(notes, both)
    return (out, strip_of(returned), new_label, change, ladder)


def solution(mesh):
    placed = (P("rep", "dom", None), P("rep", "dom", None), P("rep"), P(), P("rep"), P())
    return jax.shard_map(
        body,
        mesh=mesh,
        in_specs=placed,
        out_specs=(P("rep", "dom", None), P("rep", "dom", None), P("rep"), P("rep"), P("rep")),
        check_vma=False,
    )
```

```python
import functools

import jax
import jax.numpy as jnp
from jax import lax
from jax.experimental import pallas as pl
from jax.experimental.pallas import tpu as pltpu
from jax.sharding import PartitionSpec as P

STEPS = 8
hopping = 0.18
quartic = 0.3
step_size = 0.05

SUB = 8
LANES = 128
EDGE = 3
GROUP = 14
WHOLE_VMEM = 67043328


def lane_index():
    return lax.broadcasted_iota(jnp.int32, (SUB, LANES), 1)


def row_index():
    return lax.broadcasted_iota(jnp.int32, (SUB, LANES), 0)


class Scales:
    def __init__(self, cold):
        self.cold = cold
        squared = jnp.full((SUB, LANES), (4.0 * quartic * step_size * step_size) * cold)
        self.root = jnp.sqrt(squared)
        self.back = 1.0 / self.root
        self.back2 = self.back * self.back
        self.pull = (2.0 * hopping * step_size * step_size) * cold
        self.slope = -((2.0 - 4.0 * quartic) * step_size * step_size) * cold
        self.speed = step_size * self.root
        self.linear = ((1.0 - 2.0 * quartic) * cold) * self.back2
        self.square = (quartic * cold) * (self.back2 * self.back2)
        self.bond = ((2.0 * hopping) * cold) * self.back2
        unspeed = 1.0 / self.speed
        self.kinetic = 0.5 * (unspeed * unspeed)

    def half(self, near, value):
        return 0.5 * (self.pull * near + value * (self.slope - value * value))

    def step(self, near, value, before):
        return value + ((value - before) + (self.pull * near + value * (self.slope - value * value)))

    def site(self, value, ahead):
        squared = value * value
        return squared * (self.linear + self.square * squared) - self.bond * (value * ahead)

    def action(self, total, sites):
        return jnp.sum(total) / self.cold + quartic * sites


def paired(values, lane):
    half = len(values) // 2
    even = (lane & 1) == 0
    evens = [
        jnp.where(even, values[u], pltpu.roll(values[u + half], 1, 1)) for u in range(half)
    ]
    odds = [
        jnp.where(even, pltpu.roll(values[u], LANES - 1, 1), values[u + half]) for u in range(half)
    ]
    return evens + odds


def unpaired(evens, odds, lane):
    even = (lane & 1) == 0
    return (
        jnp.where(even, evens, pltpu.roll(odds, 1, 1)),
        jnp.where(even, pltpu.roll(evens, LANES - 1, 1), odds),
    )


def beside(load, tiles, lane):
    half = tiles // 2
    final = load(tiles - 1)
    behind = jnp.where(lane == 0, pltpu.roll(final, 1, 1), pltpu.roll(final, 3, 1))
    evens = load(0)
    begin = evens
    ahead = pltpu.roll(evens, LANES - 2, 1)
    for u in range(half):
        odds = load(u + half)
        forward = pltpu.roll(odds, 2, 1)
        left = jnp.where(lane < 2, behind, forward)
        if u + 1 < half:
            following = load(u + 1)
            ahead_next = pltpu.roll(following, LANES - 2, 1)
        else:
            following = begin
            ahead_next = jnp.where(
                lane == LANES - 1, pltpu.roll(begin, LANES - 1, 1), pltpu.roll(begin, LANES - 3, 1)
            )
        right = jnp.where(lane >= LANES - 2, ahead_next, ahead)
        yield u, evens, odds, left, right
        behind, evens, ahead = forward, following, ahead_next


def around(ref, row, tiles, lane):
    half = tiles // 2
    load = lambda t: ref[t, pl.ds(row, SUB), :]
    for u, evens, odds, left, right in beside(load, tiles, lane):
        for t, value, before, after in ((u, evens, left, odds), (u + half, odds, evens, right)):
            below = ref[t, pl.ds(row + 1, SUB), :]
            near = (ref[t, pl.ds(row - 1, SUB), :] + below) + (before + after)
            yield t, value, near, below, after


def advance(before, after, row, tiles, lane, scales, keep=None):
    for t, value, near, _, _ in around(before, row, tiles, lane):
        old = after[t, pl.ds(row, SUB), :]
        new = scales.step(near, value, old)
        if keep is not None:
            new = jnp.where(keep, old, new)
        after[t, pl.ds(row, SUB), :] = new


def pack_kernel(
    labels_ref,
    betas_ref,
    swap_ref,
    head_ref,
    tail_ref,
    head_m_ref,
    tail_m_ref,
    edges_hbm,
    cold_ref,
    label_ref,
    out_ref,
    out_sem,
):
    cold = betas_ref[labels_ref[0]]
    cold_ref[0] = cold
    label_ref[0] = swap_ref[labels_ref[0]]
    copies = []
    scales = Scales(cold)
    lane = lane_index()
    row = row_index()
    tiles = head_ref.shape[1] // LANES
    for side, ref, m_ref in ((0, head_ref, head_m_ref), (1, tail_ref, tail_m_ref)):
        base = 0 if side == 0 else SUB
        inner = SUB - base
        parts = []
        for start in (base, inner):
            parts.append(
                paired(
                    [
                        scales.root * ref[start : start + SUB, pl.ds(t * LANES, LANES)]
                        for t in range(tiles)
                    ],
                    lane,
                )
            )
        values, others = parts
        pushes = paired(
            [scales.speed * m_ref[:, pl.ds(t * LANES, LANES)] for t in range(tiles)], lane
        )
        for u, evens, odds, left, right in beside(lambda t: values[t], tiles, lane):
            half = tiles // 2
            for t, value, near in ((u, evens, left + odds), (u + half, odds, evens + right)):
                up = pltpu.roll(value, 1, 0)
                down = pltpu.roll(value, SUB - 1, 0)
                if side == 0:
                    up = jnp.where(row == 0, 0.0, up)
                    down = jnp.where(row == SUB - 1, pltpu.roll(others[t], SUB - 1, 0), down)
                else:
                    up = jnp.where(row == 0, pltpu.roll(others[t], 1, 0), up)
                    down = jnp.where(row == SUB - 1, 0.0, down)
                push = pushes[t] + scales.half((up + down) + near, value)
                out_ref[side, 0, t] = value
                out_ref[side, 1, t] = value + push
        copy = pltpu.make_async_copy(out_ref.at[side], edges_hbm.at[side], out_sem.at[side])
        copy.start()
        copies.append(copy)
    for copy in copies:
        copy.wait()


def slots(row_block, tiles, per_member):
    shares = tiles // per_member
    return [(row_block * shares + s, s * per_member * LANES) for s in range(shares)]


def inner_kernel(
    per_member,
    cold_ref,
    accept_ref,
    field_hbm,
    momentum_hbm,
    send_hbm,
    state_hbm,
    energy_hbm,
    sums_hbm,
    sums_ref,
    field_ref,
    momentum_ref,
    chosen_ref,
    first,
    second,
    energy,
    in_sem,
    send_sem,
    state_sem,
):
    rows, width = field_ref.shape
    tiles = width // LANES
    blocks = rows // SUB
    chunks = 4
    chunk = rows // chunks

    def load(a, k):
        source, target = ((field_hbm, field_ref), (momentum_hbm, momentum_ref))[a]
        part = pl.ds(pl.multiple_of(k * chunk, chunk), chunk)
        return pltpu.make_async_copy(source.at[part, :], target.at[part, :], in_sem.at[a, k])

    for k in range(chunks):
        load(0, k).start()
        load(1, k).start()
    scales = Scales(cold_ref[0])
    accepted = accept_ref[0] == 1
    lane = lane_index()
    sub = row_index()
    zero = jnp.zeros((SUB, LANES), jnp.float32)
    for ref in (first, second):
        for t in range(tiles):
            ref[t, 0:SUB, :] = zero
            ref[t, SUB + rows : 2 * SUB + rows, :] = zero

    def bring(k):
        load(0, k).wait()
        for b in range(chunk // SUB):
            row = pl.multiple_of(k * chunk + b * SUB, SUB)
            values = [
                scales.root * field_ref[pl.ds(row, SUB), pl.ds(t * LANES, LANES)] for t in range(tiles)
            ]
            for t, value in enumerate(paired(values, lane)):
                first[t, pl.ds(pl.multiple_of(SUB + row, SUB), SUB), :] = value

    def begin(block, total):
        source = pl.multiple_of(block * SUB, SUB)
        row = pl.multiple_of(SUB + block * SUB, SUB)
        pushes = paired(
            [
                scales.speed * momentum_ref[pl.ds(source, SUB), pl.ds(t * LANES, LANES)]
                for t in range(tiles)
            ],
            lane,
        )
        for t, value, near, below, right in around(first, row, tiles, lane):
            push = pushes[t]
            action = scales.site(value, below + right)
            energy[t, pl.ds(source, SUB), :] = scales.kinetic * (push * push) + action
            total = total + action
            second[t, pl.ds(row, SUB), :] = value + (push + scales.half(near, value))
        return total

    per_turn = 2

    def open_chunk(k, total):
        load(1, k).wait()
        for b in range(chunk // SUB):
            total = begin(k * (chunk // SUB) + b, total)
        return total

    def open_turn(k, total):
        bring(k + 1)
        return open_chunk(k, total)

    bring(0)
    old_action = open_chunk(chunks - 1, lax.fori_loop(0, chunks - 1, open_turn, zero))

    group = GROUP if (blocks - 2) % GROUP == 0 else 1
    for time in range(1, STEPS):
        before, after = (second, first) if time % 2 == 1 else (first, second)
        advance(before, after, SUB, tiles, lane, scales, keep=sub <= time)
        advance(before, after, rows, tiles, lane, scales, keep=sub >= SUB - 1 - time)

        def turn(i, carry, before=before, after=after):
            for b in range(group):
                row = pl.multiple_of(2 * SUB + (i * group + b) * SUB, SUB)
                advance(before, after, row, tiles, lane, scales)
            return carry

        if group == blocks - 2:
            turn(0, 0)
        else:
            lax.fori_loop(0, (blocks - 2) // group, turn, 0)
    last, previous = (first, second) if STEPS % 2 == 0 else (second, first)
    stores = []
    for n, buffer in enumerate((last, previous)):
        for side, row in ((0, SUB), (1, SUB + rows - EDGE * SUB)):
            copy = pltpu.make_async_copy(
                buffer.at[:, pl.ds(row, EDGE * SUB), :], state_hbm.at[side, n], state_sem.at[side, n]
            )
            copy.start()
            stores.append(copy)
    for side, row in ((0, 0), (1, rows - 2 * SUB)):
        copy = pltpu.make_async_copy(
            energy.at[:, pl.ds(row, 2 * SUB), :], energy_hbm.at[side], state_sem.at[side, 2]
        )
        copy.start()
        stores.append(copy)

    def emit(block):
        row = block * SUB
        copies = []
        for member, column in slots(block, tiles, per_member):
            width_here = per_member * LANES
            copies.append(
                pltpu.make_async_copy(
                    chosen_ref.at[pl.ds(row, SUB), pl.ds(column, width_here)],
                    send_hbm.at[member, :, pl.ds(0, width_here)],
                    send_sem.at[member],
                )
            )
        return copies

    def choose(block, evens, odds, u):
        row = pl.multiple_of(block * SUB, SUB)
        for t, value in zip((u, u + tiles // 2), unpaired(evens, odds, lane)):
            cols = pl.ds(t * LANES, LANES)
            kept = field_ref[pl.ds(row, SUB), cols]
            chosen_ref[pl.ds(row, SUB), cols] = jnp.where(accepted, scales.back * value, kept)

    for block in range(1, blocks - 1):
        part = pl.ds(SUB + block * SUB, SUB)
        for u in range(tiles // 2):
            choose(block, last[u, part, :], last[u + tiles // 2, part, :], u)
        for copy in emit(block):
            copy.start()
            stores.append(copy)

    def finish(block, carry):
        change, total = carry
        row = pl.multiple_of(SUB + block * SUB, SUB)
        source = pl.multiple_of(block * SUB, SUB)
        for t, value, near, below, right in around(last, row, tiles, lane):
            gone = value - previous[t, pl.ds(row, SUB), :]
            moment = gone + scales.half(near, value)
            action = scales.site(value, below + right)
            total = total + action
            change = change + (
                (scales.kinetic * (moment * moment) + action) - energy[t, pl.ds(source, SUB), :]
            )
        return change, total

    turns = 4 if (blocks - 4) % 4 == 0 else 1

    def finish_turn(i, carry):
        for b in range(turns):
            carry = finish(2 + i * turns + b, carry)
        return carry

    sums = lax.fori_loop(0, (blocks - 4) // turns, finish_turn, (zero, zero))
    sums_ref[0] = sums[0]
    sums_ref[1] = sums[1]
    sums_ref[2] = old_action
    copy = pltpu.make_async_copy(sums_ref, sums_hbm, state_sem.at[0, 3])
    copy.start()
    stores.append(copy)
    for copy in stores:
        copy.wait()


def outer_kernel(
    per_member,
    halos,
    cold_ref,
    accept_ref,
    label_ref,
    *refs,
):
    halo_refs = refs[:halos]
    (
        state_hbm,
        energy_hbm,
        sums_hbm,
        field_hbm,
        _,
        send_hbm,
        first,
        second,
        energy_ref,
        halo_ref,
        chosen_ref,
        field_ref,
        sums_ref,
        note_ref,
        in_sem,
        send_sem,
        note_sem,
    ) = refs[halos:]
    last, previous = (first, second) if STEPS % 2 == 0 else (second, first)
    loads = []
    for side in range(2):
        own = 2 * SUB if side == 0 else 0
        parts = [
            (state_hbm.at[side, n], buffer.at[side, :, pl.ds(own, EDGE * SUB), :])
            for n, buffer in enumerate((last, previous))
        ]
        parts.append((halo_refs[side % halos].at[1 - side], halo_ref.at[side]))
        edge_rows = pl.ds(0 if side == 0 else field_hbm.shape[0] - SUB, SUB)
        parts.append((energy_hbm.at[side], energy_ref.at[side]))
        parts.append((field_hbm.at[edge_rows, :], field_ref.at[side]))
        if side == 1:
            parts.append((sums_hbm, sums_ref))
        for n, (source, target) in enumerate(parts):
            copy = pltpu.make_async_copy(source, target, in_sem.at[side, n])
            copy.start()
            loads.append(copy)
    scales = Scales(cold_ref[0])
    label = label_ref[0].astype(jnp.float32)
    accepted = accept_ref[0] == 1
    lane = lane_index()
    sub = row_index()
    tiles = first.shape[1]
    members = send_hbm.shape[0]
    blocks = members * per_member // tiles
    zero = jnp.zeros((SUB, LANES), jnp.float32)
    old_extra = zero
    energy_extra = []
    for side in range(2):
        for copy in loads[5 * side : 5 * side + 3]:
            copy.wait()
        edge = SUB if side == 0 else EDGE * SUB
        pad = 0 if side == 0 else (EDGE + 1) * SUB
        mine = 2 * SUB if side == 0 else (EDGE - 1) * SUB
        for t in range(tiles):
            for buffer in (last, previous):
                buffer[side, t, pad : pad + SUB, :] = zero
            start_halo = halo_ref[side, 0, t]
            start_mine = first[side, t, mine : mine + SUB, :]
            if side == 0:
                own_part = jnp.where(sub == SUB - 1, pltpu.roll(start_mine, SUB - 1, 0), 0.0)
                halo_part = jnp.where(sub == 0, pltpu.roll(start_halo, 1, 0), 0.0)
            else:
                own_part = jnp.where(sub == 0, pltpu.roll(start_mine, 1, 0), 0.0)
                halo_part = jnp.where(sub == SUB - 1, pltpu.roll(start_halo, SUB - 1, 0), 0.0)
                missing = -scales.bond * (start_mine * halo_part)
                old_extra = old_extra + missing
                energy_extra.append(missing)
            first[side, t, edge : edge + SUB, :] = start_halo
            second[side, t, edge : edge + SUB, :] = halo_ref[side, 1, t] + (
                0.5 * scales.pull
            ) * own_part
            second[side, t, mine : mine + SUB, :] = (
                second[side, t, mine : mine + SUB, :] + (0.5 * scales.pull) * halo_part
            )
    for time in range(1, STEPS):
        before, after = (second, first) if time % 2 == 1 else (first, second)
        for side in range(2):
            mine = 2 * SUB if side == 0 else (EDGE - 1) * SUB
            edge = SUB if side == 0 else EDGE * SUB
            keep = sub > time if side == 0 else sub < SUB - 1 - time
            advance(before.at[side], after.at[side], edge, tiles, lane, scales)
            advance(before.at[side], after.at[side], mine, tiles, lane, scales, keep=keep)
    copies = []
    for side in range(2):
        mine = 2 * SUB if side == 0 else (EDGE - 1) * SUB
        block = 0 if side == 0 else blocks - 1
        loads[5 * side + 4].wait()
        kept_ref = field_ref.at[side]
        for u in range(tiles // 2):
            pair = (last[side, t, mine : mine + SUB, :] for t in (u, u + tiles // 2))
            for c, part in zip((u, u + tiles // 2), unpaired(*pair, lane)):
                cols = pl.ds(c * LANES, LANES)
                chosen_ref[side, :, cols] = jnp.where(
                    accepted, scales.back * part, kept_ref[:, cols]
                )
        for n, (member, column) in enumerate(slots(block, tiles, per_member)):
            size = per_member * LANES
            copy = pltpu.make_async_copy(
                chosen_ref.at[side, :, pl.ds(column, size)],
                send_hbm.at[member, :, pl.ds(0, size)],
                send_sem.at[side, n],
            )
            copy.start()
            copies.append(copy)
    loads[10].wait()
    change = sums_ref[0]
    total = sums_ref[1]
    for side in range(2):
        own = 2 * SUB if side == 0 else 0
        loads[5 * side + 3].wait()
        for b in range(2):
            place = b if side == 0 else EDGE - 2 + b
            row = own + place * SUB
            for t, value, near, below, right in around(last.at[side], row, tiles, lane):
                gone = value - previous[side, t, pl.ds(row, SUB), :]
                moment = gone + scales.half(near, value)
                action = scales.site(value, below + right)
                total = total + action
                old = energy_ref[side, t, b * SUB : (b + 1) * SUB, :]
                if side == 1 and b == 1:
                    old = old + energy_extra[t]
                change = change + ((scales.kinetic * (moment * moment) + action) - old)
    old_action = sums_ref[2] + old_extra
    sites = blocks * SUB * tiles * LANES
    action = scales.action(jnp.where(accepted, total, old_action), sites)
    change = jnp.sum(change)
    note = jnp.where(
        lane == 0, label, jnp.where(lane == 1, action, jnp.where(lane == 2, change, 0.0))
    )
    for member in range(members):
        note_ref[member] = note
    copy = pltpu.make_async_copy(
        note_ref, send_hbm.at[:, :, pl.ds(per_member * LANES, LANES)], note_sem
    )
    copy.start()
    copies.append(copy)
    for copy in copies:
        copy.wait()


def place_kernel(got_ref, _, out_hbm, notes_hbm, labels_ref, sem, note_sem):
    members, _, width = out_hbm.shape
    notes = got_ref.at[:, 0, pl.ds(width, LANES)]
    fetch = pltpu.make_async_copy(notes, labels_ref, note_sem.at[0])
    fetch.start()
    keep = pltpu.make_async_copy(notes, notes_hbm, note_sem.at[1])
    keep.start()
    fetch.wait()
    copies = []
    for r in range(members):
        slot = labels_ref[r, 0].astype(jnp.int32)
        copy = pltpu.make_async_copy(got_ref.at[r, :, pl.ds(0, width)], out_hbm.at[slot], sem.at[r])
        copy.start()
        copies.append(copy)
    keep.wait()
    for copy in copies:
        copy.wait()


def ladder_kernel(sites, notes_ref, sums_ref, change_ref, ladder_ref):
    me = lax.axis_index("rep")
    notes = notes_ref[...]
    sums = sums_ref[...]
    lane = lax.broadcasted_iota(jnp.int32, notes.shape, 1)
    replica = lax.broadcasted_iota(jnp.int32, notes.shape, 0)
    held = (lane == 0) & (notes.astype(jnp.int32) == me)
    actions = pltpu.roll(sums, LANES - 1, 1)
    ladder_ref[0] = jnp.sum(jnp.where(held, actions, 0.0)) / sites
    own = replica == me
    change_ref[0] = jnp.sum(jnp.where(own & (lane == 2), sums, 0.0))


def body(field, momentum, labels, betas, accept, swap_pairs):
    rows = field.shape[1]
    width = field.shape[2]
    members = lax.axis_size("rep")
    strips = lax.axis_size("dom")
    tiles = width // LANES
    per_member = (rows // SUB) * tiles // members
    shares = tiles // per_member
    piece = per_member * LANES
    f32 = jnp.float32
    start = field[0]
    moment = momentum[0]
    smem = pl.BlockSpec(memory_space=pltpu.SMEM)
    vmem = pl.BlockSpec(memory_space=pltpu.VMEM)
    anywhere = pl.BlockSpec(memory_space=pl.ANY)
    inhbm = pl.BlockSpec(memory_space=pltpu.HBM)
    dma = pltpu.SemaphoreType.DMA
    last16 = rows // (2 * SUB) - 1
    last8 = rows // SUB - 1
    edges, cold, new_label = pl.pallas_call(
        pack_kernel,
        grid=(1,),
        out_shape=(
            jax.ShapeDtypeStruct((2, 2, tiles, SUB, LANES), f32),
            jax.ShapeDtypeStruct((1,), f32),
            jax.ShapeDtypeStruct((1,), jnp.int32),
        ),
        in_specs=[
            smem,
            smem,
            smem,
            pl.BlockSpec((2 * SUB, width), lambda i: (0, 0)),
            pl.BlockSpec((2 * SUB, width), lambda i: (last16, 0)),
            pl.BlockSpec((SUB, width), lambda i: (0, 0)),
            pl.BlockSpec((SUB, width), lambda i: (last8, 0)),
        ],
        out_specs=(inhbm, smem, smem),
        scratch_shapes=[pltpu.VMEM((2, 2, tiles, SUB, LANES), f32), dma((2,))],
        name="pack",
    )(labels, betas, swap_pairs, start, start, moment, moment)
    forward = [(i, (i + 1) % strips) for i in range(strips)]
    backward = [((i + 1) % strips, i) for i in range(strips)]
    halos = (lax.ppermute(edges, "dom", forward),)
    if strips > 2:
        halos = halos + (lax.ppermute(edges, "dom", backward),)

    def strip_of(pieces):
        grouped = pieces.reshape(rows // SUB, shares, SUB, piece).transpose(0, 2, 1, 3)
        return grouped.reshape(1, rows, width)

    column = pltpu.VMEM((tiles, rows + 2 * SUB, LANES), f32)
    strip = pltpu.VMEM((rows, width), f32)
    outgoing, state, energy, sums = pl.pallas_call(
        functools.partial(inner_kernel, per_member),
        out_shape=(
            jax.ShapeDtypeStruct((members, SUB, piece + LANES), f32),
            jax.ShapeDtypeStruct((2, 2, tiles, EDGE * SUB, LANES), f32),
            jax.ShapeDtypeStruct((2, tiles, 2 * SUB, LANES), f32),
            jax.ShapeDtypeStruct((3, SUB, LANES), f32),
        ),
        in_specs=[smem, smem, inhbm, inhbm],
        out_specs=(inhbm, inhbm, inhbm, inhbm),
        scratch_shapes=[
            pltpu.VMEM((3, SUB, LANES), f32),
            strip,
            strip,
            strip,
            column,
            column,
            pltpu.VMEM((tiles, rows, LANES), f32),
            dma((2, 4)),
            dma((members,)),
            dma((2, 4)),
        ],
        cost_estimate=pl.CostEstimate(
            flops=100 * rows * width, bytes_accessed=16 * rows * width, transcendentals=0
        ),
        compiler_params=pltpu.CompilerParams(vmem_limit_bytes=WHOLE_VMEM),
        name="inner",
    )(cold, accept, start, moment)
    window = pltpu.VMEM((2, tiles, (EDGE + 2) * SUB, LANES), f32)
    outgoing = pl.pallas_call(
        functools.partial(outer_kernel, per_member, len(halos)),
        out_shape=jax.ShapeDtypeStruct((members, SUB, piece + LANES), f32),
        in_specs=[smem] * 3 + [anywhere] * len(halos) + [inhbm] * 5,
        out_specs=inhbm,
        scratch_shapes=[
            window,
            window,
            pltpu.VMEM((2, tiles, 2 * SUB, LANES), f32),
            pltpu.VMEM((2, 2, tiles, SUB, LANES), f32),
            pltpu.VMEM((2, SUB, width), f32),
            pltpu.VMEM((2, SUB, width), f32),
            pltpu.VMEM((3, SUB, LANES), f32),
            pltpu.VMEM((members, SUB, LANES), f32),
            dma((2, 6)),
            dma((2, shares)),
            dma,
        ],
        input_output_aliases={7 + len(halos): 0},
        name="outer",
    )(cold, accept, new_label, *halos, state, energy, sums, start, outgoing)
    received = lax.all_to_all(outgoing, "rep", split_axis=0, concat_axis=0, tiled=True)
    out = strip_of(outgoing[:, :, :piece])
    ordered, notes = pl.pallas_call(
        place_kernel,
        out_shape=(
            jax.ShapeDtypeStruct((members, SUB, piece), f32),
            jax.ShapeDtypeStruct((members, LANES), f32),
        ),
        in_specs=[anywhere, anywhere],
        out_specs=(inhbm, inhbm),
        scratch_shapes=[
            pltpu.SMEM((members, LANES), f32),
            dma((members,)),
            dma((2,)),
        ],
        compiler_params=pltpu.CompilerParams(vmem_limit_bytes=4 << 20),
        name="place",
    )(received, out)
    returned = lax.all_to_all(ordered, "rep", split_axis=0, concat_axis=0, tiled=True)
    passing = notes
    both = notes
    for _ in range(strips - 1):
        passing = lax.ppermute(passing, "dom", forward)
        both = both + passing
    change, ladder = pl.pallas_call(
        functools.partial(ladder_kernel, strips * rows * width),
        out_shape=(
            jax.ShapeDtypeStruct((1,), f32),
            jax.ShapeDtypeStruct((1,), f32),
        ),
        in_specs=[vmem, vmem],
        out_specs=(smem, smem),
        compiler_params=pltpu.CompilerParams(vmem_limit_bytes=4 << 20),
        name="ladder",
    )(notes, both)
    return (out, strip_of(returned), new_label, change, ladder)


def solution(mesh):
    placed = (P("rep", "dom", None), P("rep", "dom", None), P("rep"), P(), P("rep"), P())
    return jax.shard_map(
        body,
        mesh=mesh,
        in_specs=placed,
        out_specs=(P("rep", "dom", None), P("rep", "dom", None), P("rep"), P("rep"), P("rep")),
        check_vma=False,
    )
```

```python
import functools

import jax
import jax.numpy as jnp
from jax import lax
from jax.experimental import pallas as pl
from jax.experimental.pallas import tpu as pltpu
from jax.sharding import PartitionSpec as P

STEPS = 8
hopping = 0.18
quartic = 0.3
step_size = 0.05

SUB = 8
LANES = 128
EDGE = 3
GROUP = 14
WHOLE_VMEM = 67043328


def lane_index():
    return lax.broadcasted_iota(jnp.int32, (SUB, LANES), 1)


def row_index():
    return lax.broadcasted_iota(jnp.int32, (SUB, LANES), 0)


class Scales:
    def __init__(self, cold):
        self.cold = cold
        squared = jnp.full((SUB, LANES), (4.0 * quartic * step_size * step_size) * cold)
        self.root = jnp.sqrt(squared)
        self.back = 1.0 / self.root
        self.back2 = self.back * self.back
        self.pull = (2.0 * hopping * step_size * step_size) * cold
        self.slope = -((2.0 - 4.0 * quartic) * step_size * step_size) * cold
        self.speed = step_size * self.root
        self.linear = ((1.0 - 2.0 * quartic) * cold) * self.back2
        self.square = (quartic * cold) * (self.back2 * self.back2)
        self.bond = ((2.0 * hopping) * cold) * self.back2
        unspeed = 1.0 / self.speed
        self.kinetic = 0.5 * (unspeed * unspeed)

    def half(self, near, value):
        return 0.5 * (self.pull * near + value * (self.slope - value * value))

    def step(self, near, value, before):
        return value + ((value - before) + (self.pull * near + value * (self.slope - value * value)))

    def site(self, value, ahead):
        squared = value * value
        return squared * (self.linear + self.square * squared) - self.bond * (value * ahead)

    def action(self, total, sites):
        return jnp.sum(total) / self.cold + quartic * sites


def paired(values, lane):
    half = len(values) // 2
    even = (lane & 1) == 0
    evens = [
        jnp.where(even, values[u], pltpu.roll(values[u + half], 1, 1)) for u in range(half)
    ]
    odds = [
        jnp.where(even, pltpu.roll(values[u], LANES - 1, 1), values[u + half]) for u in range(half)
    ]
    return evens + odds


def unpaired(evens, odds, lane):
    even = (lane & 1) == 0
    return (
        jnp.where(even, evens, pltpu.roll(odds, 1, 1)),
        jnp.where(even, pltpu.roll(evens, LANES - 1, 1), odds),
    )


def beside(load, tiles, lane):
    half = tiles // 2
    final = load(tiles - 1)
    behind = jnp.where(lane == 0, pltpu.roll(final, 1, 1), pltpu.roll(final, 3, 1))
    evens = load(0)
    begin = evens
    ahead = pltpu.roll(evens, LANES - 2, 1)
    for u in range(half):
        odds = load(u + half)
        forward = pltpu.roll(odds, 2, 1)
        left = jnp.where(lane < 2, behind, forward)
        if u + 1 < half:
            following = load(u + 1)
            ahead_next = pltpu.roll(following, LANES - 2, 1)
        else:
            following = begin
            ahead_next = jnp.where(
                lane == LANES - 1, pltpu.roll(begin, LANES - 1, 1), pltpu.roll(begin, LANES - 3, 1)
            )
        right = jnp.where(lane >= LANES - 2, ahead_next, ahead)
        yield u, evens, odds, left, right
        behind, evens, ahead = forward, following, ahead_next


def around(ref, row, tiles, lane):
    half = tiles // 2
    load = lambda t: ref[t, pl.ds(row, SUB), :]
    for u, evens, odds, left, right in beside(load, tiles, lane):
        for t, value, before, after in ((u, evens, left, odds), (u + half, odds, evens, right)):
            below = ref[t, pl.ds(row + 1, SUB), :]
            near = (ref[t, pl.ds(row - 1, SUB), :] + below) + (before + after)
            yield t, value, near, below, after


def advance(before, after, row, tiles, lane, scales, keep=None):
    for t, value, near, _, _ in around(before, row, tiles, lane):
        old = after[t, pl.ds(row, SUB), :]
        new = scales.step(near, value, old)
        if keep is not None:
            new = jnp.where(keep, old, new)
        after[t, pl.ds(row, SUB), :] = new


def pack_kernel(labels_ref, betas_ref, head_ref, tail_ref, head_m_ref, tail_m_ref, out_ref):
    scales = Scales(betas_ref[labels_ref[0]])
    lane = lane_index()
    row = row_index()
    tiles = head_ref.shape[1] // LANES
    for side, ref, m_ref in ((0, head_ref, head_m_ref), (1, tail_ref, tail_m_ref)):
        base = 0 if side == 0 else SUB
        inner = SUB - base
        parts = []
        for start in (base, inner):
            parts.append(
                paired(
                    [
                        scales.root * ref[start : start + SUB, pl.ds(t * LANES, LANES)]
                        for t in range(tiles)
                    ],
                    lane,
                )
            )
        values, others = parts
        pushes = paired(
            [scales.speed * m_ref[:, pl.ds(t * LANES, LANES)] for t in range(tiles)], lane
        )
        for u, evens, odds, left, right in beside(lambda t: values[t], tiles, lane):
            half = tiles // 2
            for t, value, near in ((u, evens, left + odds), (u + half, odds, evens + right)):
                up = pltpu.roll(value, 1, 0)
                down = pltpu.roll(value, SUB - 1, 0)
                if side == 0:
                    up = jnp.where(row == 0, 0.0, up)
                    down = jnp.where(row == SUB - 1, pltpu.roll(others[t], SUB - 1, 0), down)
                else:
                    up = jnp.where(row == 0, pltpu.roll(others[t], 1, 0), up)
                    down = jnp.where(row == SUB - 1, 0.0, down)
                push = pushes[t] + scales.half((up + down) + near, value)
                out_ref[side, 0, t] = value
                out_ref[side, 1, t] = value + push


def slots(row_block, tiles, per_member):
    shares = tiles // per_member
    return [(row_block * shares + s, s * per_member * LANES) for s in range(shares)]


def inner_kernel(
    per_member,
    labels_ref,
    betas_ref,
    accept_ref,
    field_hbm,
    momentum_hbm,
    send_hbm,
    state_hbm,
    energy_hbm,
    sums_hbm,
    sums_ref,
    field_ref,
    momentum_ref,
    chosen_ref,
    first,
    second,
    energy,
    in_sem,
    send_sem,
    state_sem,
):
    rows, width = field_ref.shape
    tiles = width // LANES
    blocks = rows // SUB
    chunks = 4
    chunk = rows // chunks

    def load(a, k):
        source, target = ((field_hbm, field_ref), (momentum_hbm, momentum_ref))[a]
        part = pl.ds(pl.multiple_of(k * chunk, chunk), chunk)
        return pltpu.make_async_copy(source.at[part, :], target.at[part, :], in_sem.at[a, k])

    for k in range(chunks):
        load(0, k).start()
        load(1, k).start()
    scales = Scales(betas_ref[labels_ref[0]])
    accepted = accept_ref[0] == 1
    lane = lane_index()
    sub = row_index()
    zero = jnp.zeros((SUB, LANES), jnp.float32)
    for ref in (first, second):
        for t in range(tiles):
            ref[t, 0:SUB, :] = zero
            ref[t, SUB + rows : 2 * SUB + rows, :] = zero

    def bring(k):
        load(0, k).wait()
        for b in range(chunk // SUB):
            row = pl.multiple_of(k * chunk + b * SUB, SUB)
            values = [
                scales.root * field_ref[pl.ds(row, SUB), pl.ds(t * LANES, LANES)] for t in range(tiles)
            ]
            for t, value in enumerate(paired(values, lane)):
                first[t, pl.ds(pl.multiple_of(SUB + row, SUB), SUB), :] = value

    def begin(block, total):
        source = pl.multiple_of(block * SUB, SUB)
        row = pl.multiple_of(SUB + block * SUB, SUB)
        pushes = paired(
            [
                scales.speed * momentum_ref[pl.ds(source, SUB), pl.ds(t * LANES, LANES)]
                for t in range(tiles)
            ],
            lane,
        )
        for t, value, near, below, right in around(first, row, tiles, lane):
            push = pushes[t]
            action = scales.site(value, below + right)
            energy[t, pl.ds(source, SUB), :] = scales.kinetic * (push * push) + action
            total = total + action
            second[t, pl.ds(row, SUB), :] = value + (push + scales.half(near, value))
        return total

    per_turn = 2

    def open_chunk(k, total):
        load(1, k).wait()
        for b in range(chunk // SUB):
            total = begin(k * (chunk // SUB) + b, total)
        return total

    def open_turn(k, total):
        bring(k + 1)
        return open_chunk(k, total)

    bring(0)
    old_action = open_chunk(chunks - 1, lax.fori_loop(0, chunks - 1, open_turn, zero))

    group = GROUP if (blocks - 2) % GROUP == 0 else 1
    for time in range(1, STEPS):
        before, after = (second, first) if time % 2 == 1 else (first, second)
        advance(before, after, SUB, tiles, lane, scales, keep=sub <= time)
        advance(before, after, rows, tiles, lane, scales, keep=sub >= SUB - 1 - time)

        def turn(i, carry, before=before, after=after):
            for b in range(group):
                row = pl.multiple_of(2 * SUB + (i * group + b) * SUB, SUB)
                advance(before, after, row, tiles, lane, scales)
            return carry

        if group == blocks - 2:
            turn(0, 0)
        else:
            lax.fori_loop(0, (blocks - 2) // group, turn, 0)
    last, previous = (first, second) if STEPS % 2 == 0 else (second, first)
    stores = []
    for n, buffer in enumerate((last, previous)):
        for side, row in ((0, SUB), (1, SUB + rows - EDGE * SUB)):
            copy = pltpu.make_async_copy(
                buffer.at[:, pl.ds(row, EDGE * SUB), :], state_hbm.at[side, n], state_sem.at[side, n]
            )
            copy.start()
            stores.append(copy)
    for side, row in ((0, 0), (1, rows - 2 * SUB)):
        copy = pltpu.make_async_copy(
            energy.at[:, pl.ds(row, 2 * SUB), :], energy_hbm.at[side], state_sem.at[side, 2]
        )
        copy.start()
        stores.append(copy)

    def emit(block):
        row = block * SUB
        copies = []
        for member, column in slots(block, tiles, per_member):
            width_here = per_member * LANES
            copies.append(
                pltpu.make_async_copy(
                    chosen_ref.at[pl.ds(row, SUB), pl.ds(column, width_here)],
                    send_hbm.at[member, :, pl.ds(0, width_here)],
                    send_sem.at[member],
                )
            )
        return copies

    def choose(block, evens, odds, u):
        row = pl.multiple_of(block * SUB, SUB)
        for t, value in zip((u, u + tiles // 2), unpaired(evens, odds, lane)):
            cols = pl.ds(t * LANES, LANES)
            kept = field_ref[pl.ds(row, SUB), cols]
            chosen_ref[pl.ds(row, SUB), cols] = jnp.where(accepted, scales.back * value, kept)

    for block in range(1, blocks - 1):
        part = pl.ds(SUB + block * SUB, SUB)
        for u in range(tiles // 2):
            choose(block, last[u, part, :], last[u + tiles // 2, part, :], u)
        for copy in emit(block):
            copy.start()
            stores.append(copy)

    def finish(block, carry):
        change, total = carry
        row = pl.multiple_of(SUB + block * SUB, SUB)
        source = pl.multiple_of(block * SUB, SUB)
        for t, value, near, below, right in around(last, row, tiles, lane):
            gone = value - previous[t, pl.ds(row, SUB), :]
            moment = gone + scales.half(near, value)
            action = scales.site(value, below + right)
            total = total + action
            change = change + (
                (scales.kinetic * (moment * moment) + action) - energy[t, pl.ds(source, SUB), :]
            )
        return change, total

    turns = 4 if (blocks - 4) % 4 == 0 else 1

    def finish_turn(i, carry):
        for b in range(turns):
            carry = finish(2 + i * turns + b, carry)
        return carry

    sums = lax.fori_loop(0, (blocks - 4) // turns, finish_turn, (zero, zero))
    sums_ref[0] = sums[0]
    sums_ref[1] = sums[1]
    sums_ref[2] = old_action
    copy = pltpu.make_async_copy(sums_ref, sums_hbm, state_sem.at[0, 3])
    copy.start()
    stores.append(copy)
    for copy in stores:
        copy.wait()


def outer_kernel(
    per_member,
    halos,
    labels_ref,
    betas_ref,
    accept_ref,
    swap_ref,
    *refs,
):
    halo_refs = refs[:halos]
    (
        state_hbm,
        energy_hbm,
        sums_hbm,
        field_hbm,
        _,
        send_hbm,
        first,
        second,
        energy_ref,
        halo_ref,
        chosen_ref,
        field_ref,
        sums_ref,
        note_ref,
        in_sem,
        send_sem,
        note_sem,
    ) = refs[halos:]
    last, previous = (first, second) if STEPS % 2 == 0 else (second, first)
    loads = []
    for side in range(2):
        own = 2 * SUB if side == 0 else 0
        parts = [
            (state_hbm.at[side, n], buffer.at[side, :, pl.ds(own, EDGE * SUB), :])
            for n, buffer in enumerate((last, previous))
        ]
        parts.append((halo_refs[side % halos].at[1 - side], halo_ref.at[side]))
        edge_rows = pl.ds(0 if side == 0 else field_hbm.shape[0] - SUB, SUB)
        parts.append((energy_hbm.at[side], energy_ref.at[side]))
        parts.append((field_hbm.at[edge_rows, :], field_ref.at[side]))
        if side == 1:
            parts.append((sums_hbm, sums_ref))
        for n, (source, target) in enumerate(parts):
            copy = pltpu.make_async_copy(source, target, in_sem.at[side, n])
            copy.start()
            loads.append(copy)
    scales = Scales(betas_ref[labels_ref[0]])
    label = swap_ref[labels_ref[0]].astype(jnp.float32)
    accepted = accept_ref[0] == 1
    lane = lane_index()
    sub = row_index()
    tiles = first.shape[1]
    members = send_hbm.shape[0]
    blocks = members * per_member // tiles
    zero = jnp.zeros((SUB, LANES), jnp.float32)
    old_extra = zero
    energy_extra = []
    for side in range(2):
        for copy in loads[5 * side : 5 * side + 3]:
            copy.wait()
        edge = SUB if side == 0 else EDGE * SUB
        pad = 0 if side == 0 else (EDGE + 1) * SUB
        mine = 2 * SUB if side == 0 else (EDGE - 1) * SUB
        for t in range(tiles):
            for buffer in (last, previous):
                buffer[side, t, pad : pad + SUB, :] = zero
            start_halo = halo_ref[side, 0, t]
            start_mine = first[side, t, mine : mine + SUB, :]
            if side == 0:
                own_part = jnp.where(sub == SUB - 1, pltpu.roll(start_mine, SUB - 1, 0), 0.0)
                halo_part = jnp.where(sub == 0, pltpu.roll(start_halo, 1, 0), 0.0)
            else:
                own_part = jnp.where(sub == 0, pltpu.roll(start_mine, 1, 0), 0.0)
                halo_part = jnp.where(sub == SUB - 1, pltpu.roll(start_halo, SUB - 1, 0), 0.0)
                missing = -scales.bond * (start_mine * halo_part)
                old_extra = old_extra + missing
                energy_extra.append(missing)
            first[side, t, edge : edge + SUB, :] = start_halo
            second[side, t, edge : edge + SUB, :] = halo_ref[side, 1, t] + (
                0.5 * scales.pull
            ) * own_part
            second[side, t, mine : mine + SUB, :] = (
                second[side, t, mine : mine + SUB, :] + (0.5 * scales.pull) * halo_part
            )
    for time in range(1, STEPS):
        before, after = (second, first) if time % 2 == 1 else (first, second)
        for side in range(2):
            mine = 2 * SUB if side == 0 else (EDGE - 1) * SUB
            edge = SUB if side == 0 else EDGE * SUB
            keep = sub > time if side == 0 else sub < SUB - 1 - time
            advance(before.at[side], after.at[side], edge, tiles, lane, scales)
            advance(before.at[side], after.at[side], mine, tiles, lane, scales, keep=keep)
    copies = []
    for side in range(2):
        mine = 2 * SUB if side == 0 else (EDGE - 1) * SUB
        block = 0 if side == 0 else blocks - 1
        loads[5 * side + 4].wait()
        kept_ref = field_ref.at[side]
        for u in range(tiles // 2):
            pair = (last[side, t, mine : mine + SUB, :] for t in (u, u + tiles // 2))
            for c, part in zip((u, u + tiles // 2), unpaired(*pair, lane)):
                cols = pl.ds(c * LANES, LANES)
                chosen_ref[side, :, cols] = jnp.where(
                    accepted, scales.back * part, kept_ref[:, cols]
                )
        for n, (member, column) in enumerate(slots(block, tiles, per_member)):
            size = per_member * LANES
            copy = pltpu.make_async_copy(
                chosen_ref.at[side, :, pl.ds(column, size)],
                send_hbm.at[member, :, pl.ds(0, size)],
                send_sem.at[side, n],
            )
            copy.start()
            copies.append(copy)
    loads[10].wait()
    change = sums_ref[0]
    total = sums_ref[1]
    for side in range(2):
        own = 2 * SUB if side == 0 else 0
        loads[5 * side + 3].wait()
        for b in range(2):
            place = b if side == 0 else EDGE - 2 + b
            row = own + place * SUB
            for t, value, near, below, right in around(last.at[side], row, tiles, lane):
                gone = value - previous[side, t, pl.ds(row, SUB), :]
                moment = gone + scales.half(near, value)
                action = scales.site(value, below + right)
                total = total + action
                old = energy_ref[side, t, b * SUB : (b + 1) * SUB, :]
                if side == 1 and b == 1:
                    old = old + energy_extra[t]
                change = change + ((scales.kinetic * (moment * moment) + action) - old)
    old_action = sums_ref[2] + old_extra
    sites = blocks * SUB * tiles * LANES
    action = scales.action(jnp.where(accepted, total, old_action), sites)
    change = jnp.sum(change)
    note = jnp.where(
        lane == 0, label, jnp.where(lane == 1, action, jnp.where(lane == 2, change, 0.0))
    )
    for member in range(members):
        note_ref[member] = note
    copy = pltpu.make_async_copy(
        note_ref, send_hbm.at[:, :, pl.ds(per_member * LANES, LANES)], note_sem
    )
    copy.start()
    copies.append(copy)
    for copy in copies:
        copy.wait()


def place_kernel(got_ref, _, out_hbm, notes_hbm, labels_ref, sem, note_sem):
    members, _, width = out_hbm.shape
    notes = got_ref.at[:, 0, pl.ds(width, LANES)]
    fetch = pltpu.make_async_copy(notes, labels_ref, note_sem.at[0])
    fetch.start()
    keep = pltpu.make_async_copy(notes, notes_hbm, note_sem.at[1])
    keep.start()
    fetch.wait()
    copies = []
    for r in range(members):
        slot = labels_ref[r, 0].astype(jnp.int32)
        copy = pltpu.make_async_copy(got_ref.at[r, :, pl.ds(0, width)], out_hbm.at[slot], sem.at[r])
        copy.start()
        copies.append(copy)
    keep.wait()
    for copy in copies:
        copy.wait()


def ladder_kernel(sites, notes_ref, sums_ref, label_ref, change_ref, ladder_ref):
    me = lax.axis_index("rep")
    notes = notes_ref[...]
    sums = sums_ref[...]
    lane = lax.broadcasted_iota(jnp.int32, notes.shape, 1)
    replica = lax.broadcasted_iota(jnp.int32, notes.shape, 0)
    held = (lane == 0) & (notes.astype(jnp.int32) == me)
    actions = pltpu.roll(sums, LANES - 1, 1)
    ladder_ref[0] = jnp.sum(jnp.where(held, actions, 0.0)) / sites
    own = replica == me
    label_ref[0] = jnp.sum(jnp.where(own & (lane == 0), notes, 0.0)).astype(jnp.int32)
    change_ref[0] = jnp.sum(jnp.where(own & (lane == 2), sums, 0.0))


def body(field, momentum, labels, betas, accept, swap_pairs):
    rows = field.shape[1]
    width = field.shape[2]
    members = lax.axis_size("rep")
    strips = lax.axis_size("dom")
    tiles = width // LANES
    per_member = (rows // SUB) * tiles // members
    shares = tiles // per_member
    piece = per_member * LANES
    f32 = jnp.float32
    start = field[0]
    moment = momentum[0]
    smem = pl.BlockSpec(memory_space=pltpu.SMEM)
    vmem = pl.BlockSpec(memory_space=pltpu.VMEM)
    anywhere = pl.BlockSpec(memory_space=pl.ANY)
    inhbm = pl.BlockSpec(memory_space=pltpu.HBM)
    dma = pltpu.SemaphoreType.DMA
    last16 = rows // (2 * SUB) - 1
    last8 = rows // SUB - 1
    edges = pl.pallas_call(
        pack_kernel,
        grid=(1,),
        out_shape=jax.ShapeDtypeStruct((2, 2, tiles, SUB, LANES), f32),
        in_specs=[
            smem,
            smem,
            pl.BlockSpec((2 * SUB, width), lambda i: (0, 0)),
            pl.BlockSpec((2 * SUB, width), lambda i: (last16, 0)),
            pl.BlockSpec((SUB, width), lambda i: (0, 0)),
            pl.BlockSpec((SUB, width), lambda i: (last8, 0)),
        ],
        out_specs=pl.BlockSpec((2, 2, tiles, SUB, LANES), lambda i: (0, 0, 0, 0, 0)),
        name="pack",
    )(labels, betas, start, start, moment, moment)
    forward = [(i, (i + 1) % strips) for i in range(strips)]
    backward = [((i + 1) % strips, i) for i in range(strips)]
    halos = (lax.ppermute(edges, "dom", forward),)
    if strips > 2:
        halos = halos + (lax.ppermute(edges, "dom", backward),)

    def strip_of(pieces):
        grouped = pieces.reshape(rows // SUB, shares, SUB, piece).transpose(0, 2, 1, 3)
        return grouped.reshape(1, rows, width)

    column = pltpu.VMEM((tiles, rows + 2 * SUB, LANES), f32)
    strip = pltpu.VMEM((rows, width), f32)
    outgoing, state, energy, sums = pl.pallas_call(
        functools.partial(inner_kernel, per_member),
        out_shape=(
            jax.ShapeDtypeStruct((members, SUB, piece + LANES), f32),
            jax.ShapeDtypeStruct((2, 2, tiles, EDGE * SUB, LANES), f32),
            jax.ShapeDtypeStruct((2, tiles, 2 * SUB, LANES), f32),
            jax.ShapeDtypeStruct((3, SUB, LANES), f32),
        ),
        grid=(1,),
        in_specs=[smem, smem, smem, inhbm, inhbm],
        out_specs=(inhbm, inhbm, inhbm, inhbm),
        scratch_shapes=[
            pltpu.VMEM((3, SUB, LANES), f32),
            strip,
            strip,
            strip,
            column,
            column,
            pltpu.VMEM((tiles, rows, LANES), f32),
            dma((2, 4)),
            dma((members,)),
            dma((2, 4)),
        ],
        cost_estimate=pl.CostEstimate(
            flops=100 * rows * width, bytes_accessed=16 * rows * width, transcendentals=0
        ),
        compiler_params=pltpu.CompilerParams(vmem_limit_bytes=WHOLE_VMEM),
        name="inner",
    )(labels, betas, accept, start, moment)
    window = pltpu.VMEM((2, tiles, (EDGE + 2) * SUB, LANES), f32)
    outgoing = pl.pallas_call(
        functools.partial(outer_kernel, per_member, len(halos)),
        out_shape=jax.ShapeDtypeStruct((members, SUB, piece + LANES), f32),
        grid=(1,),
        in_specs=[smem] * 4 + [anywhere] * len(halos) + [inhbm] * 5,
        out_specs=inhbm,
        scratch_shapes=[
            window,
            window,
            pltpu.VMEM((2, tiles, 2 * SUB, LANES), f32),
            pltpu.VMEM((2, 2, tiles, SUB, LANES), f32),
            pltpu.VMEM((2, SUB, width), f32),
            pltpu.VMEM((2, SUB, width), f32),
            pltpu.VMEM((3, SUB, LANES), f32),
            pltpu.VMEM((members, SUB, LANES), f32),
            dma((2, 6)),
            dma((2, shares)),
            dma,
        ],
        input_output_aliases={8 + len(halos): 0},
        name="outer",
    )(labels, betas, accept, swap_pairs, *halos, state, energy, sums, start, outgoing)
    received = lax.all_to_all(outgoing, "rep", split_axis=0, concat_axis=0, tiled=True)
    out = strip_of(outgoing[:, :, :piece])
    ordered, notes = pl.pallas_call(
        place_kernel,
        out_shape=(
            jax.ShapeDtypeStruct((members, SUB, piece), f32),
            jax.ShapeDtypeStruct((members, LANES), f32),
        ),
        in_specs=[anywhere, anywhere],
        out_specs=(inhbm, inhbm),
        scratch_shapes=[
            pltpu.SMEM((members, LANES), f32),
            dma((members,)),
            dma((2,)),
        ],
        compiler_params=pltpu.CompilerParams(vmem_limit_bytes=4 << 20),
        name="place",
    )(received, out)
    returned = lax.all_to_all(ordered, "rep", split_axis=0, concat_axis=0, tiled=True)
    passing = notes
    both = notes
    for _ in range(strips - 1):
        passing = lax.ppermute(passing, "dom", forward)
        both = both + passing
    new_label, change, ladder = pl.pallas_call(
        functools.partial(ladder_kernel, strips * rows * width),
        out_shape=(
            jax.ShapeDtypeStruct((1,), jnp.int32),
            jax.ShapeDtypeStruct((1,), f32),
            jax.ShapeDtypeStruct((1,), f32),
        ),
        in_specs=[vmem, vmem],
        out_specs=(smem, smem, smem),
        compiler_params=pltpu.CompilerParams(vmem_limit_bytes=4 << 20),
        name="ladder",
    )(notes, both)
    return (out, strip_of(returned), new_label, change, ladder)


def solution(mesh):
    placed = (P("rep", "dom", None), P("rep", "dom", None), P("rep"), P(), P("rep"), P())
    return jax.shard_map(
        body,
        mesh=mesh,
        in_specs=placed,
        out_specs=(P("rep", "dom", None), P("rep", "dom", None), P("rep"), P("rep"), P("rep")),
        check_vma=False,
    )
```

```python
import functools

import jax
import jax.numpy as jnp
from jax import lax
from jax.experimental import pallas as pl
from jax.experimental.pallas import tpu as pltpu
from jax.sharding import PartitionSpec as P

STEPS = 8
hopping = 0.18
quartic = 0.3
step_size = 0.05

SUB = 8
LANES = 128
EDGE = 3
GROUP = 14
WHOLE_VMEM = 67043328


def lane_index():
    return lax.broadcasted_iota(jnp.int32, (SUB, LANES), 1)


def row_index():
    return lax.broadcasted_iota(jnp.int32, (SUB, LANES), 0)


class Scales:
    def __init__(self, cold):
        self.cold = cold
        squared = jnp.full((SUB, LANES), (4.0 * quartic * step_size * step_size) * cold)
        self.root = jnp.sqrt(squared)
        self.back = 1.0 / self.root
        self.back2 = self.back * self.back
        self.pull = (2.0 * hopping * step_size * step_size) * cold
        self.slope = -((2.0 - 4.0 * quartic) * step_size * step_size) * cold
        self.speed = step_size * self.root
        self.linear = ((1.0 - 2.0 * quartic) * cold) * self.back2
        self.square = (quartic * cold) * (self.back2 * self.back2)
        self.bond = ((2.0 * hopping) * cold) * self.back2
        unspeed = 1.0 / self.speed
        self.kinetic = 0.5 * (unspeed * unspeed)

    def half(self, near, value):
        return 0.5 * (self.pull * near + value * (self.slope - value * value))

    def step(self, near, value, before):
        return value + ((value - before) + (self.pull * near + value * (self.slope - value * value)))

    def gain(self, near, value):
        return self.pull * near + value * (self.slope - value * value)

    def site(self, value, ahead):
        squared = value * value
        return squared * (self.linear + self.square * squared) - self.bond * (value * ahead)

    def action(self, total, sites):
        return jnp.sum(total) / self.cold + quartic * sites


def paired(values, lane):
    half = len(values) // 2
    even = (lane & 1) == 0
    evens = [
        jnp.where(even, values[u], pltpu.roll(values[u + half], 1, 1)) for u in range(half)
    ]
    odds = [
        jnp.where(even, pltpu.roll(values[u], LANES - 1, 1), values[u + half]) for u in range(half)
    ]
    return evens + odds


def unpaired(evens, odds, lane):
    even = (lane & 1) == 0
    return (
        jnp.where(even, evens, pltpu.roll(odds, 1, 1)),
        jnp.where(even, pltpu.roll(evens, LANES - 1, 1), odds),
    )


def beside(load, tiles, lane):
    half = tiles // 2
    final = load(tiles - 1)
    behind = jnp.where(lane == 0, pltpu.roll(final, 1, 1), pltpu.roll(final, 3, 1))
    evens = load(0)
    begin = evens
    ahead = pltpu.roll(evens, LANES - 2, 1)
    for u in range(half):
        odds = load(u + half)
        forward = pltpu.roll(odds, 2, 1)
        left = jnp.where(lane < 2, behind, forward)
        if u + 1 < half:
            following = load(u + 1)
            ahead_next = pltpu.roll(following, LANES - 2, 1)
        else:
            following = begin
            ahead_next = jnp.where(
                lane == LANES - 1, pltpu.roll(begin, LANES - 1, 1), pltpu.roll(begin, LANES - 3, 1)
            )
        right = jnp.where(lane >= LANES - 2, ahead_next, ahead)
        yield u, evens, odds, left, right
        behind, evens, ahead = forward, following, ahead_next


def around(ref, row, tiles, lane):
    half = tiles // 2
    load = lambda t: ref[t, pl.ds(row, SUB), :]
    for u, evens, odds, left, right in beside(load, tiles, lane):
        for t, value, before, after in ((u, evens, left, odds), (u + half, odds, evens, right)):
            below = ref[t, pl.ds(row + 1, SUB), :]
            near = (ref[t, pl.ds(row - 1, SUB), :] + below) + (before + after)
            yield t, value, near, below, after


def advance(before, after, row, tiles, lane, scales, keep=None):
    for t, value, near, _, _ in around(before, row, tiles, lane):
        old = after[t, pl.ds(row, SUB), :]
        new = scales.step(near, value, old)
        if keep is not None:
            new = jnp.where(keep, old, new)
        after[t, pl.ds(row, SUB), :] = new


def glide(before, after, rise, row, tiles, lane, scales):
    part = pl.ds(row, SUB)
    for t, value, near, _, _ in around(before, row, tiles, lane):
        step = rise[t, part, :] + scales.gain(near, value)
        rise[t, part, :] = step
        after[t, part, :] = value + step


def pack_kernel(labels_ref, betas_ref, head_ref, tail_ref, head_m_ref, tail_m_ref, out_ref):
    scales = Scales(betas_ref[labels_ref[0]])
    lane = lane_index()
    row = row_index()
    tiles = head_ref.shape[1] // LANES
    for side, ref, m_ref in ((0, head_ref, head_m_ref), (1, tail_ref, tail_m_ref)):
        base = 0 if side == 0 else SUB
        inner = SUB - base
        parts = []
        for start in (base, inner):
            parts.append(
                paired(
                    [
                        scales.root * ref[start : start + SUB, pl.ds(t * LANES, LANES)]
                        for t in range(tiles)
                    ],
                    lane,
                )
            )
        values, others = parts
        pushes = paired(
            [scales.speed * m_ref[:, pl.ds(t * LANES, LANES)] for t in range(tiles)], lane
        )
        for u, evens, odds, left, right in beside(lambda t: values[t], tiles, lane):
            half = tiles // 2
            for t, value, near in ((u, evens, left + odds), (u + half, odds, evens + right)):
                up = pltpu.roll(value, 1, 0)
                down = pltpu.roll(value, SUB - 1, 0)
                if side == 0:
                    up = jnp.where(row == 0, 0.0, up)
                    down = jnp.where(row == SUB - 1, pltpu.roll(others[t], SUB - 1, 0), down)
                else:
                    up = jnp.where(row == 0, pltpu.roll(others[t], 1, 0), up)
                    down = jnp.where(row == SUB - 1, 0.0, down)
                push = pushes[t] + scales.half((up + down) + near, value)
                out_ref[side, 0, t] = value
                out_ref[side, 1, t] = value + push


def slots(row_block, tiles, per_member):
    shares = tiles // per_member
    return [(row_block * shares + s, s * per_member * LANES) for s in range(shares)]


def inner_kernel(
    per_member,
    labels_ref,
    betas_ref,
    accept_ref,
    field_hbm,
    momentum_hbm,
    send_hbm,
    state_hbm,
    energy_hbm,
    sums_hbm,
    sums_ref,
    field_ref,
    momentum_ref,
    chosen_ref,
    first,
    second,
    rise,
    energy,
    in_sem,
    send_sem,
    state_sem,
):
    rows, width = field_ref.shape
    tiles = width // LANES
    blocks = rows // SUB
    chunks = 4
    chunk = rows // chunks

    def load(a, k):
        source, target = ((field_hbm, field_ref), (momentum_hbm, momentum_ref))[a]
        part = pl.ds(pl.multiple_of(k * chunk, chunk), chunk)
        return pltpu.make_async_copy(source.at[part, :], target.at[part, :], in_sem.at[a, k])

    for k in range(chunks):
        load(0, k).start()
        load(1, k).start()
    scales = Scales(betas_ref[labels_ref[0]])
    accepted = accept_ref[0] == 1
    lane = lane_index()
    sub = row_index()
    zero = jnp.zeros((SUB, LANES), jnp.float32)
    for ref in (first, second):
        for t in range(tiles):
            ref[t, 0:SUB, :] = zero
            ref[t, SUB + rows : 2 * SUB + rows, :] = zero

    def bring(k):
        load(0, k).wait()
        for b in range(chunk // SUB):
            row = pl.multiple_of(k * chunk + b * SUB, SUB)
            values = [
                scales.root * field_ref[pl.ds(row, SUB), pl.ds(t * LANES, LANES)] for t in range(tiles)
            ]
            for t, value in enumerate(paired(values, lane)):
                first[t, pl.ds(pl.multiple_of(SUB + row, SUB), SUB), :] = value

    def begin(block, total):
        source = pl.multiple_of(block * SUB, SUB)
        row = pl.multiple_of(SUB + block * SUB, SUB)
        pushes = paired(
            [
                scales.speed * momentum_ref[pl.ds(source, SUB), pl.ds(t * LANES, LANES)]
                for t in range(tiles)
            ],
            lane,
        )
        for t, value, near, below, right in around(first, row, tiles, lane):
            push = pushes[t]
            action = scales.site(value, below + right)
            energy[t, pl.ds(source, SUB), :] = scales.kinetic * (push * push) + action
            total = total + action
            step = push + scales.half(near, value)
            rise[t, pl.ds(row, SUB), :] = step
            second[t, pl.ds(row, SUB), :] = value + step
        return total

    per_turn = 2

    def open_chunk(k, total):
        load(1, k).wait()
        for b in range(chunk // SUB):
            total = begin(k * (chunk // SUB) + b, total)
        return total

    def open_turn(k, total):
        bring(k + 1)
        return open_chunk(k, total)

    bring(0)
    old_action = open_chunk(chunks - 1, lax.fori_loop(0, chunks - 1, open_turn, zero))

    group = GROUP if (blocks - 2) % GROUP == 0 else 1
    for time in range(1, STEPS):
        before, after = (second, first) if time % 2 == 1 else (first, second)
        advance(before, after, SUB, tiles, lane, scales, keep=sub <= time)
        advance(before, after, rows, tiles, lane, scales, keep=sub >= SUB - 1 - time)

        def turn(i, carry, before=before, after=after):
            for b in range(group):
                row = pl.multiple_of(2 * SUB + (i * group + b) * SUB, SUB)
                glide(before, after, rise, row, tiles, lane, scales)
            return carry

        if group == blocks - 2:
            turn(0, 0)
        else:
            lax.fori_loop(0, (blocks - 2) // group, turn, 0)
    last, previous = (first, second) if STEPS % 2 == 0 else (second, first)
    stores = []
    for n, buffer in enumerate((last, previous)):
        for side, row in ((0, SUB), (1, SUB + rows - EDGE * SUB)):
            copy = pltpu.make_async_copy(
                buffer.at[:, pl.ds(row, EDGE * SUB), :], state_hbm.at[side, n], state_sem.at[side, n]
            )
            copy.start()
            stores.append(copy)
    for side, row in ((0, 0), (1, rows - 2 * SUB)):
        copy = pltpu.make_async_copy(
            energy.at[:, pl.ds(row, 2 * SUB), :], energy_hbm.at[side], state_sem.at[side, 2]
        )
        copy.start()
        stores.append(copy)

    def emit(block):
        row = block * SUB
        copies = []
        for member, column in slots(block, tiles, per_member):
            width_here = per_member * LANES
            copies.append(
                pltpu.make_async_copy(
                    chosen_ref.at[pl.ds(row, SUB), pl.ds(column, width_here)],
                    send_hbm.at[member, :, pl.ds(0, width_here)],
                    send_sem.at[member],
                )
            )
        return copies

    def choose(block, evens, odds, u):
        row = pl.multiple_of(block * SUB, SUB)
        for t, value in zip((u, u + tiles // 2), unpaired(evens, odds, lane)):
            cols = pl.ds(t * LANES, LANES)
            kept = field_ref[pl.ds(row, SUB), cols]
            chosen_ref[pl.ds(row, SUB), cols] = jnp.where(accepted, scales.back * value, kept)

    for block in range(1, blocks - 1):
        part = pl.ds(SUB + block * SUB, SUB)
        for u in range(tiles // 2):
            choose(block, last[u, part, :], last[u + tiles // 2, part, :], u)
        for copy in emit(block):
            copy.start()
            stores.append(copy)

    def finish(block, carry):
        change, total = carry
        row = pl.multiple_of(SUB + block * SUB, SUB)
        source = pl.multiple_of(block * SUB, SUB)
        for t, value, near, below, right in around(last, row, tiles, lane):
            gone = value - previous[t, pl.ds(row, SUB), :]
            moment = gone + scales.half(near, value)
            action = scales.site(value, below + right)
            total = total + action
            change = change + (
                (scales.kinetic * (moment * moment) + action) - energy[t, pl.ds(source, SUB), :]
            )
        return change, total

    turns = 4 if (blocks - 4) % 4 == 0 else 1

    def finish_turn(i, carry):
        for b in range(turns):
            carry = finish(2 + i * turns + b, carry)
        return carry

    sums = lax.fori_loop(0, (blocks - 4) // turns, finish_turn, (zero, zero))
    sums_ref[0] = sums[0]
    sums_ref[1] = sums[1]
    sums_ref[2] = old_action
    copy = pltpu.make_async_copy(sums_ref, sums_hbm, state_sem.at[0, 3])
    copy.start()
    stores.append(copy)
    for copy in stores:
        copy.wait()


def outer_kernel(
    per_member,
    halos,
    labels_ref,
    betas_ref,
    accept_ref,
    swap_ref,
    *refs,
):
    halo_refs = refs[:halos]
    (
        state_hbm,
        energy_hbm,
        sums_hbm,
        field_hbm,
        _,
        send_hbm,
        first,
        second,
        energy_ref,
        halo_ref,
        chosen_ref,
        field_ref,
        sums_ref,
        note_ref,
        in_sem,
        send_sem,
        note_sem,
    ) = refs[halos:]
    last, previous = (first, second) if STEPS % 2 == 0 else (second, first)
    loads = []
    for side in range(2):
        own = 2 * SUB if side == 0 else 0
        parts = [
            (state_hbm.at[side, n], buffer.at[side, :, pl.ds(own, EDGE * SUB), :])
            for n, buffer in enumerate((last, previous))
        ]
        parts.append((halo_refs[side % halos].at[1 - side], halo_ref.at[side]))
        edge_rows = pl.ds(0 if side == 0 else field_hbm.shape[0] - SUB, SUB)
        parts.append((energy_hbm.at[side], energy_ref.at[side]))
        parts.append((field_hbm.at[edge_rows, :], field_ref.at[side]))
        if side == 1:
            parts.append((sums_hbm, sums_ref))
        for n, (source, target) in enumerate(parts):
            copy = pltpu.make_async_copy(source, target, in_sem.at[side, n])
            copy.start()
            loads.append(copy)
    scales = Scales(betas_ref[labels_ref[0]])
    label = swap_ref[labels_ref[0]].astype(jnp.float32)
    accepted = accept_ref[0] == 1
    lane = lane_index()
    sub = row_index()
    tiles = first.shape[1]
    members = send_hbm.shape[0]
    blocks = members * per_member // tiles
    zero = jnp.zeros((SUB, LANES), jnp.float32)
    old_extra = zero
    energy_extra = []
    for side in range(2):
        for copy in loads[5 * side : 5 * side + 3]:
            copy.wait()
        edge = SUB if side == 0 else EDGE * SUB
        pad = 0 if side == 0 else (EDGE + 1) * SUB
        mine = 2 * SUB if side == 0 else (EDGE - 1) * SUB
        for t in range(tiles):
            for buffer in (last, previous):
                buffer[side, t, pad : pad + SUB, :] = zero
            start_halo = halo_ref[side, 0, t]
            start_mine = first[side, t, mine : mine + SUB, :]
            if side == 0:
                own_part = jnp.where(sub == SUB - 1, pltpu.roll(start_mine, SUB - 1, 0), 0.0)
                halo_part = jnp.where(sub == 0, pltpu.roll(start_halo, 1, 0), 0.0)
            else:
                own_part = jnp.where(sub == 0, pltpu.roll(start_mine, 1, 0), 0.0)
                halo_part = jnp.where(sub == SUB - 1, pltpu.roll(start_halo, SUB - 1, 0), 0.0)
                missing = -scales.bond * (start_mine * halo_part)
                old_extra = old_extra + missing
                energy_extra.append(missing)
            first[side, t, edge : edge + SUB, :] = start_halo
            second[side, t, edge : edge + SUB, :] = halo_ref[side, 1, t] + (
                0.5 * scales.pull
            ) * own_part
            second[side, t, mine : mine + SUB, :] = (
                second[side, t, mine : mine + SUB, :] + (0.5 * scales.pull) * halo_part
            )
    for time in range(1, STEPS):
        before, after = (second, first) if time % 2 == 1 else (first, second)
        for side in range(2):
            mine = 2 * SUB if side == 0 else (EDGE - 1) * SUB
            edge = SUB if side == 0 else EDGE * SUB
            keep = sub > time if side == 0 else sub < SUB - 1 - time
            advance(before.at[side], after.at[side], edge, tiles, lane, scales)
            advance(before.at[side], after.at[side], mine, tiles, lane, scales, keep=keep)
    copies = []
    for side in range(2):
        mine = 2 * SUB if side == 0 else (EDGE - 1) * SUB
        block = 0 if side == 0 else blocks - 1
        loads[5 * side + 4].wait()
        kept_ref = field_ref.at[side]
        for u in range(tiles // 2):
            pair = (last[side, t, mine : mine + SUB, :] for t in (u, u + tiles // 2))
            for c, part in zip((u, u + tiles // 2), unpaired(*pair, lane)):
                cols = pl.ds(c * LANES, LANES)
                chosen_ref[side, :, cols] = jnp.where(
                    accepted, scales.back * part, kept_ref[:, cols]
                )
        for n, (member, column) in enumerate(slots(block, tiles, per_member)):
            size = per_member * LANES
            copy = pltpu.make_async_copy(
                chosen_ref.at[side, :, pl.ds(column, size)],
                send_hbm.at[member, :, pl.ds(0, size)],
                send_sem.at[side, n],
            )
            copy.start()
            copies.append(copy)
    loads[10].wait()
    change = sums_ref[0]
    total = sums_ref[1]
    for side in range(2):
        own = 2 * SUB if side == 0 else 0
        loads[5 * side + 3].wait()
        for b in range(2):
            place = b if side == 0 else EDGE - 2 + b
            row = own + place * SUB
            for t, value, near, below, right in around(last.at[side], row, tiles, lane):
                gone = value - previous[side, t, pl.ds(row, SUB), :]
                moment = gone + scales.half(near, value)
                action = scales.site(value, below + right)
                total = total + action
                old = energy_ref[side, t, b * SUB : (b + 1) * SUB, :]
                if side == 1 and b == 1:
                    old = old + energy_extra[t]
                change = change + ((scales.kinetic * (moment * moment) + action) - old)
    old_action = sums_ref[2] + old_extra
    sites = blocks * SUB * tiles * LANES
    action = scales.action(jnp.where(accepted, total, old_action), sites)
    change = jnp.sum(change)
    note = jnp.where(
        lane == 0, label, jnp.where(lane == 1, action, jnp.where(lane == 2, change, 0.0))
    )
    for member in range(members):
        note_ref[member] = note
    copy = pltpu.make_async_copy(
        note_ref, send_hbm.at[:, :, pl.ds(per_member * LANES, LANES)], note_sem
    )
    copy.start()
    copies.append(copy)
    for copy in copies:
        copy.wait()


def place_kernel(got_ref, _, out_hbm, notes_hbm, labels_ref, sem, note_sem):
    members, _, width = out_hbm.shape
    notes = got_ref.at[:, 0, pl.ds(width, LANES)]
    fetch = pltpu.make_async_copy(notes, labels_ref, note_sem.at[0])
    fetch.start()
    keep = pltpu.make_async_copy(notes, notes_hbm, note_sem.at[1])
    keep.start()
    fetch.wait()
    copies = []
    for r in range(members):
        slot = labels_ref[r, 0].astype(jnp.int32)
        copy = pltpu.make_async_copy(got_ref.at[r, :, pl.ds(0, width)], out_hbm.at[slot], sem.at[r])
        copy.start()
        copies.append(copy)
    keep.wait()
    for copy in copies:
        copy.wait()


def ladder_kernel(sites, notes_ref, sums_ref, label_ref, change_ref, ladder_ref):
    me = lax.axis_index("rep")
    notes = notes_ref[...]
    sums = sums_ref[...]
    lane = lax.broadcasted_iota(jnp.int32, notes.shape, 1)
    replica = lax.broadcasted_iota(jnp.int32, notes.shape, 0)
    held = (lane == 0) & (notes.astype(jnp.int32) == me)
    actions = pltpu.roll(sums, LANES - 1, 1)
    ladder_ref[0] = jnp.sum(jnp.where(held, actions, 0.0)) / sites
    own = replica == me
    label_ref[0] = jnp.sum(jnp.where(own & (lane == 0), notes, 0.0)).astype(jnp.int32)
    change_ref[0] = jnp.sum(jnp.where(own & (lane == 2), sums, 0.0))


def body(field, momentum, labels, betas, accept, swap_pairs):
    rows = field.shape[1]
    width = field.shape[2]
    members = lax.axis_size("rep")
    strips = lax.axis_size("dom")
    tiles = width // LANES
    per_member = (rows // SUB) * tiles // members
    shares = tiles // per_member
    piece = per_member * LANES
    f32 = jnp.float32
    start = field[0]
    moment = momentum[0]
    smem = pl.BlockSpec(memory_space=pltpu.SMEM)
    vmem = pl.BlockSpec(memory_space=pltpu.VMEM)
    anywhere = pl.BlockSpec(memory_space=pl.ANY)
    inhbm = pl.BlockSpec(memory_space=pltpu.HBM)
    dma = pltpu.SemaphoreType.DMA
    last16 = rows // (2 * SUB) - 1
    last8 = rows // SUB - 1
    edges = pl.pallas_call(
        pack_kernel,
        grid=(1,),
        out_shape=jax.ShapeDtypeStruct((2, 2, tiles, SUB, LANES), f32),
        in_specs=[
            smem,
            smem,
            pl.BlockSpec((2 * SUB, width), lambda i: (0, 0)),
            pl.BlockSpec((2 * SUB, width), lambda i: (last16, 0)),
            pl.BlockSpec((SUB, width), lambda i: (0, 0)),
            pl.BlockSpec((SUB, width), lambda i: (last8, 0)),
        ],
        out_specs=pl.BlockSpec((2, 2, tiles, SUB, LANES), lambda i: (0, 0, 0, 0, 0)),
        name="pack",
    )(labels, betas, start, start, moment, moment)
    forward = [(i, (i + 1) % strips) for i in range(strips)]
    backward = [((i + 1) % strips, i) for i in range(strips)]
    halos = (lax.ppermute(edges, "dom", forward),)
    if strips > 2:
        halos = halos + (lax.ppermute(edges, "dom", backward),)

    def strip_of(pieces):
        grouped = pieces.reshape(rows // SUB, shares, SUB, piece).transpose(0, 2, 1, 3)
        return grouped.reshape(1, rows, width)

    column = pltpu.VMEM((tiles, rows + 2 * SUB, LANES), f32)
    strip = pltpu.VMEM((rows, width), f32)
    outgoing, state, energy, sums = pl.pallas_call(
        functools.partial(inner_kernel, per_member),
        out_shape=(
            jax.ShapeDtypeStruct((members, SUB, piece + LANES), f32),
            jax.ShapeDtypeStruct((2, 2, tiles, EDGE * SUB, LANES), f32),
            jax.ShapeDtypeStruct((2, tiles, 2 * SUB, LANES), f32),
            jax.ShapeDtypeStruct((3, SUB, LANES), f32),
        ),
        grid=(1,),
        in_specs=[smem, smem, smem, inhbm, inhbm],
        out_specs=(inhbm, inhbm, inhbm, inhbm),
        scratch_shapes=[
            pltpu.VMEM((3, SUB, LANES), f32),
            strip,
            strip,
            strip,
            column,
            column,
            column,
            pltpu.VMEM((tiles, rows, LANES), f32),
            dma((2, 4)),
            dma((members,)),
            dma((2, 4)),
        ],
        cost_estimate=pl.CostEstimate(
            flops=100 * rows * width, bytes_accessed=16 * rows * width, transcendentals=0
        ),
        compiler_params=pltpu.CompilerParams(vmem_limit_bytes=WHOLE_VMEM),
        name="inner",
    )(labels, betas, accept, start, moment)
    window = pltpu.VMEM((2, tiles, (EDGE + 2) * SUB, LANES), f32)
    outgoing = pl.pallas_call(
        functools.partial(outer_kernel, per_member, len(halos)),
        out_shape=jax.ShapeDtypeStruct((members, SUB, piece + LANES), f32),
        grid=(1,),
        in_specs=[smem] * 4 + [anywhere] * len(halos) + [inhbm] * 5,
        out_specs=inhbm,
        scratch_shapes=[
            window,
            window,
            pltpu.VMEM((2, tiles, 2 * SUB, LANES), f32),
            pltpu.VMEM((2, 2, tiles, SUB, LANES), f32),
            pltpu.VMEM((2, SUB, width), f32),
            pltpu.VMEM((2, SUB, width), f32),
            pltpu.VMEM((3, SUB, LANES), f32),
            pltpu.VMEM((members, SUB, LANES), f32),
            dma((2, 6)),
            dma((2, shares)),
            dma,
        ],
        input_output_aliases={8 + len(halos): 0},
        name="outer",
    )(labels, betas, accept, swap_pairs, *halos, state, energy, sums, start, outgoing)
    received = lax.all_to_all(outgoing, "rep", split_axis=0, concat_axis=0, tiled=True)
    out = strip_of(outgoing[:, :, :piece])
    ordered, notes = pl.pallas_call(
        place_kernel,
        out_shape=(
            jax.ShapeDtypeStruct((members, SUB, piece), f32),
            jax.ShapeDtypeStruct((members, LANES), f32),
        ),
        in_specs=[anywhere, anywhere],
        out_specs=(inhbm, inhbm),
        scratch_shapes=[
            pltpu.SMEM((members, LANES), f32),
            dma((members,)),
            dma((2,)),
        ],
        compiler_params=pltpu.CompilerParams(vmem_limit_bytes=4 << 20),
        name="place",
    )(received, out)
    returned = lax.all_to_all(ordered, "rep", split_axis=0, concat_axis=0, tiled=True)
    passing = notes
    both = notes
    for _ in range(strips - 1):
        passing = lax.ppermute(passing, "dom", forward)
        both = both + passing
    new_label, change, ladder = pl.pallas_call(
        functools.partial(ladder_kernel, strips * rows * width),
        out_shape=(
            jax.ShapeDtypeStruct((1,), jnp.int32),
            jax.ShapeDtypeStruct((1,), f32),
            jax.ShapeDtypeStruct((1,), f32),
        ),
        in_specs=[vmem, vmem],
        out_specs=(smem, smem, smem),
        compiler_params=pltpu.CompilerParams(vmem_limit_bytes=4 << 20),
        name="ladder",
    )(notes, both)
    return (out, strip_of(returned), new_label, change, ladder)


def solution(mesh):
    placed = (P("rep", "dom", None), P("rep", "dom", None), P("rep"), P(), P("rep"), P())
    return jax.shard_map(
        body,
        mesh=mesh,
        in_specs=placed,
        out_specs=(P("rep", "dom", None), P("rep", "dom", None), P("rep"), P("rep"), P("rep")),
        check_vma=False,
    )
```

```python
import functools

import jax
import jax.numpy as jnp
from jax import lax
from jax.experimental import pallas as pl
from jax.experimental.pallas import tpu as pltpu
from jax.sharding import PartitionSpec as P

STEPS = 8
hopping = 0.18
quartic = 0.3
step_size = 0.05

SUB = 8
LANES = 128
EDGE = 3
GROUP = 14
WHOLE_VMEM = 67043328


def lane_index():
    return lax.broadcasted_iota(jnp.int32, (SUB, LANES), 1)


def row_index():
    return lax.broadcasted_iota(jnp.int32, (SUB, LANES), 0)


class Scales:
    def __init__(self, cold):
        self.cold = cold
        squared = jnp.full((SUB, LANES), (4.0 * quartic * step_size * step_size) * cold)
        self.root = jnp.sqrt(squared)
        self.back = 1.0 / self.root
        self.back2 = self.back * self.back
        self.pull = (2.0 * hopping * step_size * step_size) * cold
        self.slope = -((2.0 - 4.0 * quartic) * step_size * step_size) * cold
        self.speed = step_size * self.root
        self.linear = ((1.0 - 2.0 * quartic) * cold) * self.back2
        self.square = (quartic * cold) * (self.back2 * self.back2)
        self.bond = ((2.0 * hopping) * cold) * self.back2
        unspeed = 1.0 / self.speed
        self.kinetic = 0.5 * (unspeed * unspeed)

    def half(self, near, value):
        return 0.5 * (self.pull * near + value * (self.slope - value * value))

    def step(self, near, value, before):
        return value + ((value - before) + (self.pull * near + value * (self.slope - value * value)))

    def gain(self, near, value):
        return self.pull * near + value * (self.slope - value * value)

    def site(self, value, ahead):
        squared = value * value
        return squared * (self.linear + self.square * squared) - self.bond * (value * ahead)

    def action(self, total, sites):
        return jnp.sum(total) / self.cold + quartic * sites


def paired(values, lane):
    half = len(values) // 2
    even = (lane & 1) == 0
    evens = [
        jnp.where(even, values[u], pltpu.roll(values[u + half], 1, 1)) for u in range(half)
    ]
    odds = [
        jnp.where(even, pltpu.roll(values[u], LANES - 1, 1), values[u + half]) for u in range(half)
    ]
    return evens + odds


def unpaired(evens, odds, lane):
    even = (lane & 1) == 0
    return (
        jnp.where(even, evens, pltpu.roll(odds, 1, 1)),
        jnp.where(even, pltpu.roll(evens, LANES - 1, 1), odds),
    )


def beside(load, tiles, lane):
    half = tiles // 2
    final = load(tiles - 1)
    behind = jnp.where(lane == 0, pltpu.roll(final, 1, 1), pltpu.roll(final, 3, 1))
    evens = load(0)
    begin = evens
    ahead = pltpu.roll(evens, LANES - 2, 1)
    for u in range(half):
        odds = load(u + half)
        forward = pltpu.roll(odds, 2, 1)
        left = jnp.where(lane < 2, behind, forward)
        if u + 1 < half:
            following = load(u + 1)
            ahead_next = pltpu.roll(following, LANES - 2, 1)
        else:
            following = begin
            ahead_next = jnp.where(
                lane == LANES - 1, pltpu.roll(begin, LANES - 1, 1), pltpu.roll(begin, LANES - 3, 1)
            )
        right = jnp.where(lane >= LANES - 2, ahead_next, ahead)
        yield u, evens, odds, left, right
        behind, evens, ahead = forward, following, ahead_next


def around(ref, row, tiles, lane):
    half = tiles // 2
    load = lambda t: ref[t, pl.ds(row, SUB), :]
    for u, evens, odds, left, right in beside(load, tiles, lane):
        for t, value, before, after in ((u, evens, left, odds), (u + half, odds, evens, right)):
            below = ref[t, pl.ds(row + 1, SUB), :]
            near = (ref[t, pl.ds(row - 1, SUB), :] + below) + (before + after)
            yield t, value, near, below, after


def advance(before, after, row, tiles, lane, scales, keep=None):
    for t, value, near, _, _ in around(before, row, tiles, lane):
        old = after[t, pl.ds(row, SUB), :]
        new = scales.step(near, value, old)
        if keep is not None:
            new = jnp.where(keep, old, new)
        after[t, pl.ds(row, SUB), :] = new


def glide(before, after, rise, row, tiles, lane, scales):
    part = pl.ds(row, SUB)
    for t, value, near, _, _ in around(before, row, tiles, lane):
        step = rise[t, part, :] + scales.gain(near, value)
        rise[t, part, :] = step
        after[t, part, :] = value + step


def pack_kernel(labels_ref, betas_ref, head_ref, tail_ref, head_m_ref, tail_m_ref, out_ref):
    scales = Scales(betas_ref[labels_ref[0]])
    lane = lane_index()
    row = row_index()
    tiles = head_ref.shape[1] // LANES
    for side, ref, m_ref in ((0, head_ref, head_m_ref), (1, tail_ref, tail_m_ref)):
        base = 0 if side == 0 else SUB
        inner = SUB - base
        parts = []
        for start in (base, inner):
            parts.append(
                paired(
                    [
                        scales.root * ref[start : start + SUB, pl.ds(t * LANES, LANES)]
                        for t in range(tiles)
                    ],
                    lane,
                )
            )
        values, others = parts
        pushes = paired(
            [scales.speed * m_ref[:, pl.ds(t * LANES, LANES)] for t in range(tiles)], lane
        )
        for u, evens, odds, left, right in beside(lambda t: values[t], tiles, lane):
            half = tiles // 2
            for t, value, near in ((u, evens, left + odds), (u + half, odds, evens + right)):
                up = pltpu.roll(value, 1, 0)
                down = pltpu.roll(value, SUB - 1, 0)
                if side == 0:
                    up = jnp.where(row == 0, 0.0, up)
                    down = jnp.where(row == SUB - 1, pltpu.roll(others[t], SUB - 1, 0), down)
                else:
                    up = jnp.where(row == 0, pltpu.roll(others[t], 1, 0), up)
                    down = jnp.where(row == SUB - 1, 0.0, down)
                push = pushes[t] + scales.half((up + down) + near, value)
                out_ref[side, 0, t] = value
                out_ref[side, 1, t] = value + push


def slots(row_block, tiles, per_member):
    shares = tiles // per_member
    return [(row_block * shares + s, s * per_member * LANES) for s in range(shares)]


def inner_kernel(
    per_member,
    labels_ref,
    betas_ref,
    accept_ref,
    field_hbm,
    momentum_hbm,
    send_hbm,
    state_hbm,
    energy_hbm,
    sums_hbm,
    sums_ref,
    field_ref,
    momentum_ref,
    chosen_ref,
    first,
    second,
    rise,
    energy,
    in_sem,
    send_sem,
    state_sem,
):
    rows, width = field_ref.shape
    tiles = width // LANES
    blocks = rows // SUB
    chunks = 4
    chunk = rows // chunks

    def load(a, k):
        source, target = ((field_hbm, field_ref), (momentum_hbm, momentum_ref))[a]
        part = pl.ds(pl.multiple_of(k * chunk, chunk), chunk)
        return pltpu.make_async_copy(source.at[part, :], target.at[part, :], in_sem.at[a, k])

    for k in range(chunks):
        load(0, k).start()
        load(1, k).start()
    scales = Scales(betas_ref[labels_ref[0]])
    accepted = accept_ref[0] == 1
    lane = lane_index()
    sub = row_index()
    zero = jnp.zeros((SUB, LANES), jnp.float32)
    for ref in (first, second):
        for t in range(tiles):
            ref[t, 0:SUB, :] = zero
            ref[t, SUB + rows : 2 * SUB + rows, :] = zero

    def bring(k):
        load(0, k).wait()
        for b in range(chunk // SUB):
            row = pl.multiple_of(k * chunk + b * SUB, SUB)
            values = [
                scales.root * field_ref[pl.ds(row, SUB), pl.ds(t * LANES, LANES)] for t in range(tiles)
            ]
            for t, value in enumerate(paired(values, lane)):
                first[t, pl.ds(pl.multiple_of(SUB + row, SUB), SUB), :] = value

    def begin(block, total):
        source = pl.multiple_of(block * SUB, SUB)
        row = pl.multiple_of(SUB + block * SUB, SUB)
        pushes = paired(
            [
                scales.speed * momentum_ref[pl.ds(source, SUB), pl.ds(t * LANES, LANES)]
                for t in range(tiles)
            ],
            lane,
        )
        for t, value, near, below, right in around(first, row, tiles, lane):
            push = pushes[t]
            action = scales.site(value, below + right)
            energy[t, pl.ds(source, SUB), :] = scales.kinetic * (push * push) + action
            total = total + action
            step = push + scales.half(near, value)
            rise[t, pl.ds(row, SUB), :] = step
            second[t, pl.ds(row, SUB), :] = value + step
        return total

    per_turn = 2

    def open_chunk(k, total):
        load(1, k).wait()
        for b in range(chunk // SUB):
            total = begin(k * (chunk // SUB) + b, total)
        return total

    def open_turn(k, total):
        bring(k + 1)
        return open_chunk(k, total)

    bring(0)
    old_action = open_chunk(chunks - 1, lax.fori_loop(0, chunks - 1, open_turn, zero))

    group = GROUP if (blocks - 2) % GROUP == 0 else 1
    for time in range(1, STEPS):
        before, after = (second, first) if time % 2 == 1 else (first, second)
        advance(before, after, SUB, tiles, lane, scales, keep=sub <= time)
        advance(before, after, rows, tiles, lane, scales, keep=sub >= SUB - 1 - time)

        def turn(i, carry, before=before, after=after):
            for b in range(group):
                row = pl.multiple_of(2 * SUB + (i * group + b) * SUB, SUB)
                glide(before, after, rise, row, tiles, lane, scales)
            return carry

        if group == blocks - 2:
            turn(0, 0)
        else:
            lax.fori_loop(0, (blocks - 2) // group, turn, 0)
    last, previous = (first, second) if STEPS % 2 == 0 else (second, first)
    stores = []
    for n, buffer in enumerate((last, previous)):
        for side, row in ((0, SUB), (1, SUB + rows - EDGE * SUB)):
            copy = pltpu.make_async_copy(
                buffer.at[:, pl.ds(row, EDGE * SUB), :], state_hbm.at[side, n], state_sem.at[side, n]
            )
            copy.start()
            stores.append(copy)
    for side, row in ((0, 0), (1, rows - 2 * SUB)):
        copy = pltpu.make_async_copy(
            energy.at[:, pl.ds(row, 2 * SUB), :], energy_hbm.at[side], state_sem.at[side, 2]
        )
        copy.start()
        stores.append(copy)

    def emit(block):
        row = block * SUB
        copies = []
        for member, column in slots(block, tiles, per_member):
            width_here = per_member * LANES
            copies.append(
                pltpu.make_async_copy(
                    chosen_ref.at[pl.ds(row, SUB), pl.ds(column, width_here)],
                    send_hbm.at[member, :, pl.ds(0, width_here)],
                    send_sem.at[member],
                )
            )
        return copies

    def choose(block, evens, odds, u):
        row = pl.multiple_of(block * SUB, SUB)
        for t, value in zip((u, u + tiles // 2), unpaired(evens, odds, lane)):
            cols = pl.ds(t * LANES, LANES)
            kept = field_ref[pl.ds(row, SUB), cols]
            chosen_ref[pl.ds(row, SUB), cols] = jnp.where(accepted, scales.back * value, kept)

    for block in range(1, blocks - 1):
        part = pl.ds(SUB + block * SUB, SUB)
        for u in range(tiles // 2):
            choose(block, last[u, part, :], last[u + tiles // 2, part, :], u)
        for copy in emit(block):
            copy.start()
            stores.append(copy)

    def finish(block, carry):
        change, total = carry
        row = pl.multiple_of(SUB + block * SUB, SUB)
        source = pl.multiple_of(block * SUB, SUB)
        for t, value, near, below, right in around(last, row, tiles, lane):
            gone = value - previous[t, pl.ds(row, SUB), :]
            moment = gone + scales.half(near, value)
            action = scales.site(value, below + right)
            total = total + action
            change = change + (
                (scales.kinetic * (moment * moment) + action) - energy[t, pl.ds(source, SUB), :]
            )
        return change, total

    turns = 6 if (blocks - 4) % 6 == 0 else 1

    def finish_turn(i, carry):
        for b in range(turns):
            carry = finish(2 + i * turns + b, carry)
        return carry

    sums = lax.fori_loop(0, (blocks - 4) // turns, finish_turn, (zero, zero))
    sums_ref[0] = sums[0]
    sums_ref[1] = sums[1]
    sums_ref[2] = old_action
    copy = pltpu.make_async_copy(sums_ref, sums_hbm, state_sem.at[0, 3])
    copy.start()
    stores.append(copy)
    for copy in stores:
        copy.wait()


def outer_kernel(
    per_member,
    halos,
    labels_ref,
    betas_ref,
    accept_ref,
    swap_ref,
    *refs,
):
    halo_refs = refs[:halos]
    (
        state_hbm,
        energy_hbm,
        sums_hbm,
        field_hbm,
        _,
        send_hbm,
        first,
        second,
        energy_ref,
        halo_ref,
        chosen_ref,
        field_ref,
        sums_ref,
        note_ref,
        in_sem,
        send_sem,
        note_sem,
    ) = refs[halos:]
    last, previous = (first, second) if STEPS % 2 == 0 else (second, first)
    loads = []
    for side in range(2):
        own = 2 * SUB if side == 0 else 0
        parts = [
            (state_hbm.at[side, n], buffer.at[side, :, pl.ds(own, EDGE * SUB), :])
            for n, buffer in enumerate((last, previous))
        ]
        parts.append((halo_refs[side % halos].at[1 - side], halo_ref.at[side]))
        edge_rows = pl.ds(0 if side == 0 else field_hbm.shape[0] - SUB, SUB)
        parts.append((energy_hbm.at[side], energy_ref.at[side]))
        parts.append((field_hbm.at[edge_rows, :], field_ref.at[side]))
        if side == 1:
            parts.append((sums_hbm, sums_ref))
        for n, (source, target) in enumerate(parts):
            copy = pltpu.make_async_copy(source, target, in_sem.at[side, n])
            copy.start()
            loads.append(copy)
    scales = Scales(betas_ref[labels_ref[0]])
    label = swap_ref[labels_ref[0]].astype(jnp.float32)
    accepted = accept_ref[0] == 1
    lane = lane_index()
    sub = row_index()
    tiles = first.shape[1]
    members = send_hbm.shape[0]
    blocks = members * per_member // tiles
    zero = jnp.zeros((SUB, LANES), jnp.float32)
    old_extra = zero
    energy_extra = []
    for side in range(2):
        for copy in loads[5 * side : 5 * side + 3]:
            copy.wait()
        edge = SUB if side == 0 else EDGE * SUB
        pad = 0 if side == 0 else (EDGE + 1) * SUB
        mine = 2 * SUB if side == 0 else (EDGE - 1) * SUB
        for t in range(tiles):
            for buffer in (last, previous):
                buffer[side, t, pad : pad + SUB, :] = zero
            start_halo = halo_ref[side, 0, t]
            start_mine = first[side, t, mine : mine + SUB, :]
            if side == 0:
                own_part = jnp.where(sub == SUB - 1, pltpu.roll(start_mine, SUB - 1, 0), 0.0)
                halo_part = jnp.where(sub == 0, pltpu.roll(start_halo, 1, 0), 0.0)
            else:
                own_part = jnp.where(sub == 0, pltpu.roll(start_mine, 1, 0), 0.0)
                halo_part = jnp.where(sub == SUB - 1, pltpu.roll(start_halo, SUB - 1, 0), 0.0)
                missing = -scales.bond * (start_mine * halo_part)
                old_extra = old_extra + missing
                energy_extra.append(missing)
            first[side, t, edge : edge + SUB, :] = start_halo
            second[side, t, edge : edge + SUB, :] = halo_ref[side, 1, t] + (
                0.5 * scales.pull
            ) * own_part
            second[side, t, mine : mine + SUB, :] = (
                second[side, t, mine : mine + SUB, :] + (0.5 * scales.pull) * halo_part
            )
    for time in range(1, STEPS):
        before, after = (second, first) if time % 2 == 1 else (first, second)
        for side in range(2):
            mine = 2 * SUB if side == 0 else (EDGE - 1) * SUB
            edge = SUB if side == 0 else EDGE * SUB
            keep = sub > time if side == 0 else sub < SUB - 1 - time
            advance(before.at[side], after.at[side], edge, tiles, lane, scales)
            advance(before.at[side], after.at[side], mine, tiles, lane, scales, keep=keep)
    copies = []
    for side in range(2):
        mine = 2 * SUB if side == 0 else (EDGE - 1) * SUB
        block = 0 if side == 0 else blocks - 1
        loads[5 * side + 4].wait()
        kept_ref = field_ref.at[side]
        for u in range(tiles // 2):
            pair = (last[side, t, mine : mine + SUB, :] for t in (u, u + tiles // 2))
            for c, part in zip((u, u + tiles // 2), unpaired(*pair, lane)):
                cols = pl.ds(c * LANES, LANES)
                chosen_ref[side, :, cols] = jnp.where(
                    accepted, scales.back * part, kept_ref[:, cols]
                )
        for n, (member, column) in enumerate(slots(block, tiles, per_member)):
            size = per_member * LANES
            copy = pltpu.make_async_copy(
                chosen_ref.at[side, :, pl.ds(column, size)],
                send_hbm.at[member, :, pl.ds(0, size)],
                send_sem.at[side, n],
            )
            copy.start()
            copies.append(copy)
    loads[10].wait()
    change = sums_ref[0]
    total = sums_ref[1]
    for side in range(2):
        own = 2 * SUB if side == 0 else 0
        loads[5 * side + 3].wait()
        for b in range(2):
            place = b if side == 0 else EDGE - 2 + b
            row = own + place * SUB
            for t, value, near, below, right in around(last.at[side], row, tiles, lane):
                gone = value - previous[side, t, pl.ds(row, SUB), :]
                moment = gone + scales.half(near, value)
                action = scales.site(value, below + right)
                total = total + action
                old = energy_ref[side, t, b * SUB : (b + 1) * SUB, :]
                if side == 1 and b == 1:
                    old = old + energy_extra[t]
                change = change + ((scales.kinetic * (moment * moment) + action) - old)
    old_action = sums_ref[2] + old_extra
    sites = blocks * SUB * tiles * LANES
    action = scales.action(jnp.where(accepted, total, old_action), sites)
    change = jnp.sum(change)
    note = jnp.where(
        lane == 0, label, jnp.where(lane == 1, action, jnp.where(lane == 2, change, 0.0))
    )
    for member in range(members):
        note_ref[member] = note
    copy = pltpu.make_async_copy(
        note_ref, send_hbm.at[:, :, pl.ds(per_member * LANES, LANES)], note_sem
    )
    copy.start()
    copies.append(copy)
    for copy in copies:
        copy.wait()


def place_kernel(got_ref, _, out_hbm, notes_hbm, labels_ref, sem, note_sem):
    members, _, width = out_hbm.shape
    notes = got_ref.at[:, 0, pl.ds(width, LANES)]
    fetch = pltpu.make_async_copy(notes, labels_ref, note_sem.at[0])
    fetch.start()
    keep = pltpu.make_async_copy(notes, notes_hbm, note_sem.at[1])
    keep.start()
    fetch.wait()
    copies = []
    for r in range(members):
        slot = labels_ref[r, 0].astype(jnp.int32)
        copy = pltpu.make_async_copy(got_ref.at[r, :, pl.ds(0, width)], out_hbm.at[slot], sem.at[r])
        copy.start()
        copies.append(copy)
    keep.wait()
    for copy in copies:
        copy.wait()


def ladder_kernel(sites, notes_ref, sums_ref, label_ref, change_ref, ladder_ref):
    me = lax.axis_index("rep")
    notes = notes_ref[...]
    sums = sums_ref[...]
    lane = lax.broadcasted_iota(jnp.int32, notes.shape, 1)
    replica = lax.broadcasted_iota(jnp.int32, notes.shape, 0)
    held = (lane == 0) & (notes.astype(jnp.int32) == me)
    actions = pltpu.roll(sums, LANES - 1, 1)
    ladder_ref[0] = jnp.sum(jnp.where(held, actions, 0.0)) / sites
    own = replica == me
    label_ref[0] = jnp.sum(jnp.where(own & (lane == 0), notes, 0.0)).astype(jnp.int32)
    change_ref[0] = jnp.sum(jnp.where(own & (lane == 2), sums, 0.0))


def body(field, momentum, labels, betas, accept, swap_pairs):
    rows = field.shape[1]
    width = field.shape[2]
    members = lax.axis_size("rep")
    strips = lax.axis_size("dom")
    tiles = width // LANES
    per_member = (rows // SUB) * tiles // members
    shares = tiles // per_member
    piece = per_member * LANES
    f32 = jnp.float32
    start = field[0]
    moment = momentum[0]
    smem = pl.BlockSpec(memory_space=pltpu.SMEM)
    vmem = pl.BlockSpec(memory_space=pltpu.VMEM)
    anywhere = pl.BlockSpec(memory_space=pl.ANY)
    inhbm = pl.BlockSpec(memory_space=pltpu.HBM)
    dma = pltpu.SemaphoreType.DMA
    last16 = rows // (2 * SUB) - 1
    last8 = rows // SUB - 1
    edges = pl.pallas_call(
        pack_kernel,
        grid=(1,),
        out_shape=jax.ShapeDtypeStruct((2, 2, tiles, SUB, LANES), f32),
        in_specs=[
            smem,
            smem,
            pl.BlockSpec((2 * SUB, width), lambda i: (0, 0)),
            pl.BlockSpec((2 * SUB, width), lambda i: (last16, 0)),
            pl.BlockSpec((SUB, width), lambda i: (0, 0)),
            pl.BlockSpec((SUB, width), lambda i: (last8, 0)),
        ],
        out_specs=pl.BlockSpec((2, 2, tiles, SUB, LANES), lambda i: (0, 0, 0, 0, 0)),
        name="pack",
    )(labels, betas, start, start, moment, moment)
    forward = [(i, (i + 1) % strips) for i in range(strips)]
    backward = [((i + 1) % strips, i) for i in range(strips)]
    halos = (lax.ppermute(edges, "dom", forward),)
    if strips > 2:
        halos = halos + (lax.ppermute(edges, "dom", backward),)

    def strip_of(pieces):
        grouped = pieces.reshape(rows // SUB, shares, SUB, piece).transpose(0, 2, 1, 3)
        return grouped.reshape(1, rows, width)

    column = pltpu.VMEM((tiles, rows + 2 * SUB, LANES), f32)
    strip = pltpu.VMEM((rows, width), f32)
    outgoing, state, energy, sums = pl.pallas_call(
        functools.partial(inner_kernel, per_member),
        out_shape=(
            jax.ShapeDtypeStruct((members, SUB, piece + LANES), f32),
            jax.ShapeDtypeStruct((2, 2, tiles, EDGE * SUB, LANES), f32),
            jax.ShapeDtypeStruct((2, tiles, 2 * SUB, LANES), f32),
            jax.ShapeDtypeStruct((3, SUB, LANES), f32),
        ),
        grid=(1,),
        in_specs=[smem, smem, smem, inhbm, inhbm],
        out_specs=(inhbm, inhbm, inhbm, inhbm),
        scratch_shapes=[
            pltpu.VMEM((3, SUB, LANES), f32),
            strip,
            strip,
            strip,
            column,
            column,
            column,
            pltpu.VMEM((tiles, rows, LANES), f32),
            dma((2, 4)),
            dma((members,)),
            dma((2, 4)),
        ],
        cost_estimate=pl.CostEstimate(
            flops=100 * rows * width, bytes_accessed=16 * rows * width, transcendentals=0
        ),
        compiler_params=pltpu.CompilerParams(vmem_limit_bytes=WHOLE_VMEM),
        name="inner",
    )(labels, betas, accept, start, moment)
    window = pltpu.VMEM((2, tiles, (EDGE + 2) * SUB, LANES), f32)
    outgoing = pl.pallas_call(
        functools.partial(outer_kernel, per_member, len(halos)),
        out_shape=jax.ShapeDtypeStruct((members, SUB, piece + LANES), f32),
        grid=(1,),
        in_specs=[smem] * 4 + [anywhere] * len(halos) + [inhbm] * 5,
        out_specs=inhbm,
        scratch_shapes=[
            window,
            window,
            pltpu.VMEM((2, tiles, 2 * SUB, LANES), f32),
            pltpu.VMEM((2, 2, tiles, SUB, LANES), f32),
            pltpu.VMEM((2, SUB, width), f32),
            pltpu.VMEM((2, SUB, width), f32),
            pltpu.VMEM((3, SUB, LANES), f32),
            pltpu.VMEM((members, SUB, LANES), f32),
            dma((2, 6)),
            dma((2, shares)),
            dma,
        ],
        input_output_aliases={8 + len(halos): 0},
        name="outer",
    )(labels, betas, accept, swap_pairs, *halos, state, energy, sums, start, outgoing)
    received = lax.all_to_all(outgoing, "rep", split_axis=0, concat_axis=0, tiled=True)
    out = strip_of(outgoing[:, :, :piece])
    ordered, notes = pl.pallas_call(
        place_kernel,
        out_shape=(
            jax.ShapeDtypeStruct((members, SUB, piece), f32),
            jax.ShapeDtypeStruct((members, LANES), f32),
        ),
        in_specs=[anywhere, anywhere],
        out_specs=(inhbm, inhbm),
        scratch_shapes=[
            pltpu.SMEM((members, LANES), f32),
            dma((members,)),
            dma((2,)),
        ],
        compiler_params=pltpu.CompilerParams(vmem_limit_bytes=4 << 20),
        name="place",
    )(received, out)
    returned = lax.all_to_all(ordered, "rep", split_axis=0, concat_axis=0, tiled=True)
    passing = notes
    both = notes
    for _ in range(strips - 1):
        passing = lax.ppermute(passing, "dom", forward)
        both = both + passing
    new_label, change, ladder = pl.pallas_call(
        functools.partial(ladder_kernel, strips * rows * width),
        out_shape=(
            jax.ShapeDtypeStruct((1,), jnp.int32),
            jax.ShapeDtypeStruct((1,), f32),
            jax.ShapeDtypeStruct((1,), f32),
        ),
        in_specs=[vmem, vmem],
        out_specs=(smem, smem, smem),
        compiler_params=pltpu.CompilerParams(vmem_limit_bytes=4 << 20),
        name="ladder",
    )(notes, both)
    return (out, strip_of(returned), new_label, change, ladder)


def solution(mesh):
    placed = (P("rep", "dom", None), P("rep", "dom", None), P("rep"), P(), P("rep"), P())
    return jax.shard_map(
        body,
        mesh=mesh,
        in_specs=placed,
        out_specs=(P("rep", "dom", None), P("rep", "dom", None), P("rep"), P("rep"), P("rep")),
        check_vma=False,
    )
```
